32 devices in a mesh: band: 8 (over z, y), plane: 4 (over x, core).
Axes of the slice: x: 2, y: 2, z: 4, core: 2. Of those that a mesh axis runs over, the one named last changes fastest.
Arguments:
- coeffs: float32 [8, 4, 65, 2048], P('band', None, None, 'plane'), may hold values from -6 to 6
- potential: float32 [128, 128, 128], P('plane', 'band'), may hold values from -6 to 6
- stick_map: int32 [3, 2048], replicated, may hold values from -32 to 32, as said below
Outputs:
- applied_coeffs: float32 [8, 4, 65, 2048], P('band', None, None, 'plane')
The draws below stay inside these ranges and needn't reach their ends.
Inputs may be any that keep to these rules, and one draw needn't show every extreme that they name: `stick_map`: column s describes stick slot s: rows 0 and 1 are its G_x and G_y, row 2 its half-height h, or -1 for an empty slot (then G_x = G_y = 0). The live slots hold every column (x, y) with x*x + y*y <= 32 squared and x > 0, or x = 0 and y > 0, exactly once, with h the largest integer for which x*x + y*y + h*h <= 32 squared. Which slot holds which column is drawn.
All inputs are finite; a program needn't handle non-finite values.
Results may differ from the reference program's by a relative error of at most 0.00007.
Values sent between devices are 32-bit elements; how exact they have to be, the bound alone decides.
No kernel may reach another device: no remote copies, remote signals or barrier semaphores. Data moves between devices by JAX's collectives and lax.ppermute only.
A program may use at most 64 MiB of HBM per device.

```python
import jax
import jax.numpy as jnp
from jax import lax

GRID = 128
RADIUS = 32
STICKS = 2048
ZSPAN = 65
PAIRS = 8


def draw_stick_map(key, part):
    side_len = 2 * RADIUS + 1
    lattice = jnp.arange(side_len * side_len, dtype=jnp.int32)
    candidate_x = lattice // side_len - RADIUS
    candidate_y = lattice % side_len - RADIUS
    distance = candidate_x * candidate_x + candidate_y * candidate_y
    inside = (distance <= RADIUS * RADIUS) & ((candidate_x > 0) | (candidate_x == 0) & (candidate_y > 0))
    levels = jnp.arange(1, RADIUS + 1, dtype=jnp.int32)
    heights = jnp.sum((levels[None, :] * levels[None, :] <= RADIUS * RADIUS - distance[:, None]).astype(jnp.int32), axis=1)
    ranking = jnp.argsort(jnp.where(inside, 0, 1).astype(jnp.int32), stable=True)
    chosen = ranking[:STICKS]
    is_live = inside[chosen]
    column_x = jnp.where(is_live, candidate_x[chosen], 0)
    column_y = jnp.where(is_live, candidate_y[chosen], 0)
    column_h = jnp.where(is_live, heights[chosen], -1)
    shuffle = jax.random.permutation(jax.random.fold_in(key, 7), STICKS)
    return jnp.stack([column_x[shuffle], column_y[shuffle], column_h[shuffle]]).astype(jnp.int32)


def block_scale(rng, dims, shards, least, high):
    level, own = 1.0, jax.random.fold_in(rng, 6)
    for axis_at, shards_of in shards:
        draws = jnp.exp(jax.random.uniform(jax.random.fold_in(own, axis_at), (shards_of,), jnp.float32, least / len(shards), high / len(shards)))
        level = level * jnp.repeat(draws, dims[axis_at] // shards_of).reshape([-1 if axis == axis_at else 1 for axis in range(len(dims))])
    return level


def gaussian(own_key, extent, spread, bound, pieces=(), held_as=jnp.bfloat16):
    result = jax.random.normal(own_key, extent, jnp.float32) * spread
    if len(pieces) > 0:
        result = block_scale(own_key, extent, pieces, -0.22, 0.18) * result
    return jnp.clip(result, min=-bound, max=bound).astype(held_as)


def setup_inputs(seed: int = 0) -> dict:
    arg_keys = jax.random.split(jax.random.key(seed), 4)
    coeffs = gaussian(arg_keys[0], (PAIRS, 4, ZSPAN, STICKS), 1.0, 6.0, ((0, 8), (3, 4)), jnp.float32)
    potential = gaussian(arg_keys[1], (GRID, GRID, GRID), 1.0, 6.0, ((0, 4), (1, 8)), jnp.float32)
    stick_map = draw_stick_map(jax.random.fold_in(arg_keys[3], 71), 0)
    return {"coeffs": coeffs, "potential": potential, "stick_map": stick_map}


def reference(coeffs, potential, stick_map):
    stick_x = stick_map[0]
    stick_y = stick_map[1]
    heights = stick_map[2]
    depth_ids = jnp.arange(ZSPAN, dtype=jnp.int32) - RADIUS
    live_mask = jnp.abs(depth_ids)[:, None] <= heights[None, :]
    shape_two = (ZSPAN, STICKS)
    plus_x = jnp.broadcast_to(jnp.mod(stick_x, GRID)[None, :], shape_two).astype(jnp.int32)
    plus_y = jnp.broadcast_to(jnp.mod(stick_y, GRID)[None, :], shape_two).astype(jnp.int32)
    plus_z = jnp.broadcast_to(jnp.mod(depth_ids, GRID)[:, None], shape_two).astype(jnp.int32)
    minus_x = jnp.broadcast_to(jnp.mod(-stick_x, GRID)[None, :], shape_two).astype(jnp.int32)
    minus_y = jnp.broadcast_to(jnp.mod(-stick_y, GRID)[None, :], shape_two).astype(jnp.int32)
    minus_z = jnp.broadcast_to(jnp.mod(-depth_ids, GRID)[:, None], shape_two).astype(jnp.int32)
    field = jnp.transpose(potential, (1, 2, 0))
    volume = float(GRID) ** 3

    def one_pair(coeff_block):
        masked = jnp.where(live_mask[None], coeff_block, jnp.zeros_like(coeff_block))
        first_orb = lax.complex(masked[0], masked[1])
        second_orb = lax.complex(masked[2], masked[3])
        packed = first_orb + 1j * second_orb
        mirrored = jnp.conj(first_orb) + 1j * jnp.conj(second_orb)
        spectrum = jnp.zeros((GRID, GRID, GRID), packed.dtype)
        spectrum = spectrum.at[plus_x, plus_y, plus_z].add(packed)
        spectrum = spectrum.at[minus_x, minus_y, minus_z].add(mirrored)
        orbitals = jnp.fft.ifftn(spectrum) * volume
        applied = jnp.fft.fftn(orbitals * field) / volume
        direct = applied[plus_x, plus_y, plus_z]
        opposite = jnp.conj(applied[minus_x, minus_y, minus_z])
        new_first = 0.5 * (direct + opposite)
        new_second = -0.5j * (direct - opposite)
        stacked = jnp.stack([jnp.real(new_first), jnp.imag(new_first), jnp.real(new_second), jnp.imag(new_second)])
        stacked = stacked.astype(coeff_block.dtype)
        return jnp.where(live_mask[None], stacked, jnp.zeros_like(stacked))

    return lax.map(one_pair, coeffs)
```

```python
import functools
import math

import jax
import jax.numpy as jnp
import ml_dtypes
import numpy as np
from jax import lax
from jax.experimental import pallas as pl
from jax.experimental.pallas import tpu as pltpu
from jax.sharding import PartitionSpec as P


bf16 = jnp.bfloat16
f32 = jnp.float32
VMEM = pl.BlockSpec(memory_space=pltpu.VMEM)
SMEM = pl.BlockSpec(memory_space=pltpu.SMEM)


def up8(n):
    return -(-n // 8) * 8


def halves(table):
    high = table.astype(ml_dtypes.bfloat16)
    return high, (table - high.astype(np.float64)).astype(ml_dtypes.bfloat16)


def split(value):
    high = value.astype(bf16)
    return high, (value - high.astype(f32)).astype(bf16)


class Sizes:
    def __init__(self, span, sticks, length, planes, devices):
        self.span, self.length, self.planes, self.devices = span, length, planes, devices
        self.sticks = sticks
        self.radius = (span - 1) // 2
        self.rows_y = 2 * self.radius
        self.span_pad = up8(span)
        self.tiles = self.radius // 2 + 1
        self.even = up8(self.tiles)
        self.odd = up8(self.radius // 2)
        self.kept = 2 * (self.even + self.odd)
        self.batch = 2 * planes


def tables(s):
    turn = 2.0 * math.pi / s.length
    grid = np.arange(s.length)
    depth = np.arange(s.span) - s.radius
    y = np.arange(s.rows_y) + 1 - s.radius

    def trig(left, right):
        angle = turn * np.mod(np.outer(left, right), s.length)
        return np.cos(angle), np.sin(angle)

    cos, sin = trig(depth, grid)
    ahead = np.zeros((s.devices, 2, s.planes, 2, s.span_pad))
    back = np.zeros((s.devices, 2, s.span_pad, 2, s.planes))
    scale = 1.0 / float(s.length) ** 3
    for d in range(s.devices):
        own = slice(d * s.planes, (d + 1) * s.planes)
        c, n = cos[:, own], sin[:, own]
        ahead[d, 0, :, 0, : s.span] = c.T
        ahead[d, 0, :, 1, : s.span] = -n.T
        ahead[d, 1, :, 0, : s.span] = n.T
        ahead[d, 1, :, 1, : s.span] = c.T
        back[d, 0, : s.span, 0] = c * scale
        back[d, 0, : s.span, 1] = n * scale
        back[d, 1, : s.span, 0] = -n * scale
        back[d, 1, : s.span, 1] = c * scale
    ahead = ahead.reshape(s.devices, 2 * s.planes, 2 * s.span_pad)
    back = back.reshape(s.devices, 2 * s.span_pad, 2 * s.planes)

    cos, sin = trig(y, grid)
    y_ahead = np.zeros((2, 2, s.rows_y, 2, 2, s.length))
    y_back = np.zeros((2, 2, s.length, 2, 2, s.rows_y))
    for parity in range(2):
        y_ahead[0, parity, :, parity, 0] = cos
        y_ahead[1, parity, :, parity, 0] = -sin
        y_ahead[0, parity, :, parity, 1] = sin
        y_ahead[1, parity, :, parity, 1] = cos
        y_back[parity, 0, :, 0, parity] = cos.T
        y_back[parity, 1, :, 0, parity] = sin.T
        y_back[parity, 0, :, 1, parity] = -sin.T
        y_back[parity, 1, :, 1, parity] = cos.T
    y_ahead = y_ahead.reshape(4 * s.rows_y, 4 * s.length)
    y_back = y_back.reshape(4 * s.length, 4 * s.rows_y)

    x_ahead = np.zeros((s.length, s.kept))
    x_back = np.zeros((s.kept, s.length))
    at = 0
    for component in range(2):
        for parity in range(2):
            count = s.tiles if parity == 0 else s.radius // 2
            cos, sin = trig(2 * np.arange(count) + parity, grid)
            x_ahead[:, at : at + count] = 2.0 * cos.T if component == 0 else -2.0 * sin.T
            x_back[at : at + count] = cos if component == 0 else -sin
            at += s.even if parity == 0 else s.odd

    def beside(table, axis, order):
        parts = halves(table)
        return np.concatenate([parts[i] for i in order], axis)

    zero = np.zeros(x_back.shape, ml_dtypes.bfloat16)
    high, low = halves(x_back)
    return dict(
        z_ahead=beside(ahead, 2, (0, 1, 0)),
        z_back=beside(back, 2, (0, 1, 0)),
        y_ahead=beside(y_ahead, 0, (0, 0, 1)),
        y_back=beside(y_back, 0, (0, 0, 1)),
        x_ahead=beside(x_ahead, 1, (0, 1, 0)),
        x_back=np.concatenate([np.concatenate([high, high], 1), np.concatenate([low, zero], 1)], 0),
    )


def dot(left, right):
    return jnp.dot(left, right, preferred_element_type=f32)


def partner(me, k):
    return jnp.bitwise_xor(me, k)


def live_of(s, sticks_ref, source):
    columns = pl.ds(pl.multiple_of(source * s.sticks, s.sticks), s.sticks)
    depth = lax.broadcasted_iota(jnp.int32, (s.span, s.sticks), 0) - s.radius
    return jnp.abs(depth) <= sticks_ref[2:3, columns]


def ahead_kernel(s, me_ref, coeffs_ref, sticks_ref, table_ref, *out_refs):
    me = me_ref[0]
    live = live_of(s, sticks_ref, me)
    table = jnp.concatenate([table_ref[partner(me, k)] for k in range(s.devices)], 0)
    gap = jnp.zeros((s.span_pad - s.span, s.sticks), f32)
    for orbital in range(2):
        parts = []
        for component in range(2):
            parts += [jnp.where(live, coeffs_ref[0, 2 * orbital + component], 0.0), gap]
        high, low = split(jnp.concatenate(parts, 0))
        moved = dot(table, jnp.concatenate([high, high, low], 0))
        for k in range(s.devices):
            for component in range(2):
                row = (2 * k + component) * s.planes
                out_refs[k][pl.ds(component * s.batch + orbital * s.planes, s.planes), :] = moved[row : row + s.planes]


def back_kernel(s, me_ref, *refs):
    in_refs, (sticks_ref, table_ref, out_ref) = refs[: s.devices], refs[s.devices :]
    me = me_ref[0]
    live = live_of(s, sticks_ref, me)
    for orbital in range(2):
        total = None
        for k in range(s.devices):
            parts = [in_refs[k][pl.ds(c * s.batch + orbital * s.planes, s.planes), :] for c in range(2)]
            high, low = split(jnp.concatenate(parts, 0))
            term = dot(table_ref[partner(me, k)], jnp.concatenate([high, high, low], 0))
            total = term if total is None else total + term
        for component in range(2):
            row = component * s.span_pad
            out_ref[0, 2 * orbital + component] = jnp.where(live, total[row : row + s.span], 0.0)


def places(s, sticks_ref, sources, x_ref, y_ref):
    at = 0
    for source in sources:
        columns = pl.ds(pl.multiple_of(source * s.sticks, s.sticks), s.sticks)
        shape = (s.rows_y, s.sticks)
        x_ref[:, at : at + s.sticks] = jnp.broadcast_to(sticks_ref[0:1, columns].astype(f32), shape).astype(bf16)
        row = lax.broadcasted_iota(jnp.int32, shape, 0) + 1 - s.radius
        hit = sticks_ref[1:2, columns] == row
        y_ref[:, at : at + s.sticks] = jnp.where(hit, 1.0, 0.0).astype(bf16)
        at += s.sticks


def one_hot(x, x_all, y_all):
    return jnp.where(x_all == jnp.asarray(x, bf16), y_all, jnp.zeros_like(y_all))


def plane_kernel(s, me_ref, *refs):
    in_refs, (sticks_ref, table_ref, out_ref, x_ref, y_ref, grid_ref, both_ref) = refs[: s.devices], refs[s.devices :]
    me = me_ref[0]
    places(s, sticks_ref, [partner(me, k) for k in range(s.devices)], x_ref, y_ref)
    rows = 2 * s.batch
    for k in range(s.devices):
        high, low = split(in_refs[k][...])
        both_ref[:rows, k * s.sticks : (k + 1) * s.sticks] = high
        both_ref[rows:, k * s.sticks : (k + 1) * s.sticks] = low
    lanes = 2 * s.rows_y
    for first in range(0, s.tiles, 2):
        count = min(2, s.tiles - first)
        hot = jnp.concatenate([one_hot(x, x_ref[...], y_ref[...]) for x in range(2 * first, 2 * (first + count))], 0)
        laid = lax.dot_general(both_ref[...], hot, (((1,), (1,)), ((), ())), preferred_element_type=f32)
        laid = laid[:rows] + laid[rows:]
        for t in range(count):
            for component in range(2):
                grid_ref[
                    pl.ds((first + t) * s.batch, s.batch), component * lanes : (component + 1) * lanes
                ] = laid[component * s.batch : (component + 1) * s.batch, t * lanes : (t + 1) * lanes]
    total = s.tiles * s.batch
    for start in range(0, total, 4 * s.batch):
        end = min(total, start + 4 * s.batch)
        high, low = split(grid_ref[start:end, :])
        moved = dot(jnp.concatenate([high, low, high], 1), table_ref[...])
        for t in range(4):
            out_ref[t, start:end, :] = moved[:, t * s.length : (t + 1) * s.length]
    for t in range(4):
        out_ref[t, total:, :] = jnp.zeros((s.even * s.batch - total, s.length), f32)


def space_kernel(s, bands, ids_ref, half_ref, *refs):
    slab_refs = refs[:bands]
    sticks_ref, x_ahead_ref, x_back_ref, y_back_ref = refs[bands : bands + 4]
    out_refs = refs[bands + 4 : bands + 4 + s.devices]
    field_ref, turned_ref, x_ref, y_ref, flat_ref, hot_ref = refs[bands + 4 + s.devices :]
    me = ids_ref[0]
    width = s.length // bands
    for r in range(bands):
        field_ref[:, pl.ds(pl.multiple_of(ids_ref[1 + r] * width, width), width), :] = slab_refs[r][...]
    total = s.tiles * s.batch
    for t in range(2, 4):
        turned_ref[t, s.odd * s.batch :, :] = jnp.zeros(((s.even - s.odd) * s.batch, s.length), f32)

    def plane(z, carry):
        parts = []
        for component in range(2):
            for parity in range(2):
                count = s.odd if parity else s.even
                parts.append(
                    jnp.concatenate(
                        [
                            half_ref[2 * parity + component, pl.ds(o * s.planes + z, count, stride=s.batch), :]
                            for o in range(2)
                        ],
                        1,
                    )
                )
        high, low = split(jnp.concatenate(parts, 0))
        real = dot(x_ahead_ref[...], jnp.concatenate([high, high, low], 0))
        field = field_ref[z]
        high, low = split(real * jnp.concatenate([field, field], 1))
        turned = dot(x_back_ref[...], jnp.concatenate([high, low], 0))
        turned = turned[: s.kept] + turned[s.kept :]
        at = 0
        for component in range(2):
            for parity in range(2):
                count = s.odd if parity else s.even
                for o in range(2):
                    turned_ref[2 * parity + component, pl.ds(o * s.planes + z, count, stride=s.batch), :] = turned[
                        at : at + count, o * s.length : (o + 1) * s.length
                    ]
                at += count
        return carry

    lax.fori_loop(0, s.planes, plane, 0, unroll=4)

    rows = 2 * s.batch
    lanes = 2 * s.rows_y
    for start in range(0, total, 4 * s.batch):
        end = min(total, start + 4 * s.batch)
        high, low = split(jnp.concatenate([turned_ref[t, start:end, :] for t in range(4)], 1))
        moved = dot(jnp.concatenate([high, low, high], 1), y_back_ref[...])
        high, low = split(moved)
        for t in range((end - start) // s.batch):
            column = (start // s.batch + t) * lanes
            for component in range(2):
                row = component * s.batch
                mine = slice(t * s.batch, (t + 1) * s.batch), slice(component * lanes, (component + 1) * lanes)
                flat_ref[row : row + s.batch, column : column + lanes] = high[mine]
                flat_ref[rows + row : rows + row + s.batch, column : column + lanes] = low[mine]

    places(s, sticks_ref, [partner(me, k) for k in range(s.devices)], x_ref, y_ref)
    for k in range(s.devices):
        columns = slice(k * s.sticks, (k + 1) * s.sticks)
        for x in range(2 * s.tiles):
            hot_ref[x * s.rows_y : (x + 1) * s.rows_y, :] = one_hot(x, x_ref[:, columns], y_ref[:, columns])
        found = dot(flat_ref[...], hot_ref[...])
        out_refs[k][...] = found[:rows] + found[rows:]


def ring_order(count):
    if count % 2:
        return list(range(count))
    return list(range(0, count, 2)) + list(range(count - 1, 0, -2))


def per_device(bands, coeffs, potential, stick_map):
    devices = stick_map.shape[1] // coeffs.shape[3]
    s = Sizes(coeffs.shape[2], coeffs.shape[3], potential.shape[2], potential.shape[0], devices)
    tab = {name: jnp.asarray(value) for name, value in tables(s).items()}
    me = lax.axis_index("plane")
    rows = 2 * s.batch
    block = jax.ShapeDtypeStruct((rows, s.sticks), f32)

    order = ring_order(bands)
    at = jnp.asarray(np.argsort(order), jnp.int32)[lax.axis_index("band")]
    path = jnp.asarray(order, jnp.int32)
    along = [(order[i], order[(i + 1) % bands]) for i in range(bands)]
    against = [(b, a) for a, b in along]
    offsets, slabs = [0], [potential]
    up = down = potential
    for step in range(1, bands // 2 + 1):
        up = lax.ppermute(up, "band", along)
        slabs.append(up)
        offsets.append(-step)
        if len(slabs) < bands:
            down = lax.ppermute(down, "band", against)
            slabs.append(down)
            offsets.append(step)
    ids = jnp.concatenate([me[None], path[jnp.mod(at + jnp.asarray(offsets, jnp.int32), bands)]]).astype(jnp.int32)

    def exchange(blocks):
        swaps = [[(i, i ^ k) for i in range(devices)] for k in range(devices)]
        return [blocks[0]] + [lax.ppermute(blocks[k], "plane", swaps[k]) for k in range(1, devices)]

    def kernel(body, inputs, out_shape, scratch_shapes=()):
        return pl.pallas_call(
            body,
            in_specs=[SMEM] + [VMEM] * (len(inputs) - 1),
            out_specs=jax.tree.map(lambda _: VMEM, out_shape),
            out_shape=out_shape,
            scratch_shapes=scratch_shapes,
        )(*inputs)

    total = devices * s.sticks
    results = []
    for pair in range(coeffs.shape[0]):
        sent = kernel(
            functools.partial(ahead_kernel, s),
            [ids, coeffs[pair : pair + 1], stick_map, tab["z_ahead"]],
            [block] * devices,
        )
        held = exchange(sent)
        half = kernel(
            functools.partial(plane_kernel, s),
            [ids, *held, stick_map, tab["y_ahead"]],
            jax.ShapeDtypeStruct((4, s.even * s.batch, s.length), f32),
            [
                pltpu.VMEM((s.rows_y, total), bf16),
                pltpu.VMEM((s.rows_y, total), bf16),
                pltpu.VMEM((s.tiles * s.batch, 4 * s.rows_y), f32),
                pltpu.VMEM((2 * rows, total), bf16),
            ],
        )
        mixed = kernel(
            functools.partial(space_kernel, s, bands),
            [ids, half, *slabs, stick_map, tab["x_ahead"], tab["x_back"], tab["y_back"]],
            [block] * devices,
            [
                pltpu.VMEM((s.planes, s.length, s.length), f32),
                pltpu.VMEM((4, s.even * s.batch, s.length), f32),
                pltpu.VMEM((s.rows_y, total), bf16),
                pltpu.VMEM((s.rows_y, total), bf16),
                pltpu.VMEM((2 * rows, 2 * s.tiles * s.rows_y), bf16),
                pltpu.VMEM((2 * s.tiles * s.rows_y, s.sticks), bf16),
            ],
        )
        returned = exchange(mixed)
        results.append(
            kernel(
                functools.partial(back_kernel, s),
                [ids, *returned, stick_map, tab["z_back"]],
                jax.ShapeDtypeStruct((1,) + coeffs.shape[1:], f32),
            )
        )
    return results[0] if len(results) == 1 else jnp.concatenate(results, 0)


def solution(mesh):
    placed = (P("band", None, None, "plane"), P("plane", "band", None), P())
    return jax.shard_map(
        functools.partial(per_device, mesh.shape["band"]),
        mesh=mesh,
        in_specs=placed,
        out_specs=P("band", None, None, "plane"),
        check_vma=False,
    )
```

```python
import functools
import math

import jax
import jax.numpy as jnp
import ml_dtypes
import numpy as np
from jax import lax
from jax.experimental import pallas as pl
from jax.experimental.pallas import tpu as pltpu
from jax.sharding import PartitionSpec as P


bf16 = jnp.bfloat16
f32 = jnp.float32
VMEM = pl.BlockSpec(memory_space=pltpu.VMEM)


def up8(n):
    return -(-n // 8) * 8


def halves(table):
    high = table.astype(ml_dtypes.bfloat16)
    return high, (table - high.astype(np.float64)).astype(ml_dtypes.bfloat16)


def split(value):
    high = value.astype(bf16)
    return high, (value - high.astype(f32)).astype(bf16)


class Sizes:
    def __init__(self, span, sticks, length, planes, devices):
        self.span, self.length, self.planes, self.devices = span, length, planes, devices
        self.sticks = sticks
        self.radius = (span - 1) // 2
        self.rows_y = 2 * self.radius
        self.tiles = self.radius // 2 + 1
        self.even = up8(self.tiles)
        self.odd = up8(self.radius // 2)
        self.kept = 2 * (self.even + self.odd)
        self.batch = 2 * planes
        self.step = self.batch + 1
        self.depth_rows = -(-4 * span // 16) * 16


def tables(s):
    turn = 2.0 * math.pi / s.length
    grid = np.arange(s.length)
    depth = np.arange(s.span) - s.radius
    y = np.arange(s.rows_y) + 1 - s.radius

    def trig(left, right):
        angle = turn * np.mod(np.outer(left, right), s.length)
        return np.cos(angle), np.sin(angle)

    cos, sin = trig(depth, grid)
    ahead = np.zeros((s.devices, 2, 2, s.planes, s.span, 2, 2))
    back = np.zeros((s.devices, s.span, 2, 2, 2, 2, s.planes))
    scale = 1.0 / float(s.length) ** 3
    for d in range(s.devices):
        own = slice(d * s.planes, (d + 1) * s.planes)
        c, n = cos[:, own], sin[:, own]
        for o in range(2):
            ahead[d, 0, o, :, :, o, 0] = c.T
            ahead[d, 0, o, :, :, o, 1] = -n.T
            ahead[d, 1, o, :, :, o, 0] = n.T
            ahead[d, 1, o, :, :, o, 1] = c.T
            back[d, :, o, 0, 0, o] = c * scale
            back[d, :, o, 0, 1, o] = n * scale
            back[d, :, o, 1, 0, o] = -n * scale
            back[d, :, o, 1, 1, o] = c * scale
    gap = s.depth_rows - 4 * s.span
    ahead = np.pad(ahead.reshape(s.devices, 2 * s.batch, 4 * s.span), ((0, 0), (0, 0), (0, gap)))
    back = np.pad(back.reshape(s.devices, 4 * s.span, 2 * s.batch), ((0, 0), (0, gap), (0, 0)))

    cos, sin = trig(y, grid)
    y_ahead = np.zeros((2, 2, s.rows_y, 2, 2, s.length))
    y_back = np.zeros((2, 2, s.length, 2, 2, s.rows_y))
    for parity in range(2):
        y_ahead[0, parity, :, parity, 0] = cos
        y_ahead[1, parity, :, parity, 0] = -sin
        y_ahead[0, parity, :, parity, 1] = sin
        y_ahead[1, parity, :, parity, 1] = cos
        y_back[parity, 0, :, 0, parity] = cos.T
        y_back[parity, 1, :, 0, parity] = sin.T
        y_back[parity, 0, :, 1, parity] = -sin.T
        y_back[parity, 1, :, 1, parity] = cos.T
    y_ahead = y_ahead.reshape(4 * s.rows_y, 4 * s.length)
    y_back = y_back.reshape(4 * s.length, 4 * s.rows_y)

    x_ahead = np.zeros((s.length, s.kept))
    x_back = np.zeros((s.kept, s.length))
    at = 0
    for component in range(2):
        for parity in range(2):
            count = s.tiles if parity == 0 else s.radius // 2
            cos, sin = trig(2 * np.arange(count) + parity, grid)
            x_ahead[:, at : at + count] = 2.0 * cos.T if component == 0 else -2.0 * sin.T
            x_back[at : at + count] = cos if component == 0 else -sin
            at += s.even if parity == 0 else s.odd

    def beside(table, axis, order):
        parts = halves(table)
        return np.concatenate([parts[i] for i in order], axis)

    zero = np.zeros(x_back.shape, ml_dtypes.bfloat16)
    high, low = halves(x_back)
    return dict(
        z_ahead=beside(ahead, 2, (0, 1, 0)),
        z_back=beside(back, 2, (0, 1)),
        y_ahead=np.stack(halves(y_ahead)),
        y_back=np.stack(halves(y_back)),
        x_ahead=beside(x_ahead, 1, (0, 1, 0)),
        x_back=np.concatenate([np.concatenate([high, high], 1), np.concatenate([low, zero], 1)], 0),
    )


def dot(left, right):
    return jnp.dot(left, right, preferred_element_type=f32)


def partner(me, k):
    return jnp.bitwise_xor(me, k)


def live_of(s, sticks_ref, source):
    columns = pl.ds(pl.multiple_of(source * s.sticks, s.sticks), s.sticks)
    depth = lax.broadcasted_iota(jnp.int32, (4 * s.span, s.sticks), 0) // 4 - s.radius
    return jnp.abs(depth) <= sticks_ref[2:3, columns]


def ahead_kernel(s, coeffs_ref, sticks_ref, table_ref, *out_refs):
    me = lax.axis_index("plane")
    data = jnp.where(live_of(s, sticks_ref, me), coeffs_ref[0].reshape(4 * s.span, s.sticks), 0.0)
    gap = jnp.zeros((s.depth_rows - 4 * s.span, s.sticks), f32)
    high, low = split(jnp.concatenate([data, gap], 0))
    data = jnp.concatenate([high, high, low], 0)
    for k in reversed(range(s.devices)):
        out_refs[k][...] = dot(table_ref[partner(me, k)], data)


def back_kernel(s, *refs):
    in_refs, (sticks_ref, table_ref, out_ref) = refs[: s.devices], refs[s.devices :]
    me = lax.axis_index("plane")
    total = None
    for k in range(s.devices):
        high, low = split(in_refs[k][...])
        table = table_ref[partner(me, k)]
        table = jnp.concatenate([table, table[:, : 2 * s.batch]], 1)
        term = dot(table, jnp.concatenate([high, high, low], 0))
        total = term if total is None else total + term
    total = jnp.where(live_of(s, sticks_ref, me), total[: 4 * s.span], 0.0)
    out_ref[0] = total.reshape(s.span, 4, s.sticks)


def places(s, sticks_ref, sources, x_ref, y_ref):
    at = 0
    for source in sources:
        columns = pl.ds(pl.multiple_of(source * s.sticks, s.sticks), s.sticks)
        shape = (s.rows_y, s.sticks)
        x_ref[:, at : at + s.sticks] = jnp.broadcast_to(sticks_ref[0:1, columns].astype(f32), shape).astype(bf16)
        row = lax.broadcasted_iota(jnp.int32, shape, 0) + 1 - s.radius
        hit = sticks_ref[1:2, columns] == row
        y_ref[:, at : at + s.sticks] = jnp.where(hit, 1.0, 0.0).astype(bf16)
        at += s.sticks


def one_hot(x, x_all, y_all):
    return jnp.where(x_all == jnp.asarray(x, bf16), y_all, jnp.zeros_like(y_all))


def plane_kernel(s, *refs):
    in_refs, (sticks_ref, table_ref, out_ref, x_ref, y_ref, grid_ref, both_ref) = refs[: s.devices], refs[s.devices :]
    me = lax.axis_index("plane")
    places(s, sticks_ref, [partner(me, k) for k in range(s.devices)], x_ref, y_ref)
    rows = 2 * s.batch
    for k in range(s.devices):
        high, low = split(in_refs[k][...])
        both_ref[:rows, k * s.sticks : (k + 1) * s.sticks] = high
        both_ref[rows:, k * s.sticks : (k + 1) * s.sticks] = low
    lanes = 2 * s.rows_y
    for first in range(0, s.tiles, 2):
        count = min(2, s.tiles - first)
        hot = jnp.concatenate([one_hot(x, x_ref[...], y_ref[...]) for x in range(2 * first, 2 * (first + count))], 0)
        laid = lax.dot_general(both_ref[...], hot, (((1,), (1,)), ((), ())), preferred_element_type=f32)
        laid = laid[:rows] + laid[rows:]
        for t in range(count):
            for component in range(2):
                grid_ref[
                    pl.ds((first + t) * s.batch, s.batch), component * lanes : (component + 1) * lanes
                ] = laid[component * s.batch : (component + 1) * s.batch, t * lanes : (t + 1) * lanes]
    total = s.tiles * s.batch
    table = jnp.concatenate([table_ref[0], table_ref[0], table_ref[1]], 0)
    for start in range(0, total, 4 * s.batch):
        end = min(total, start + 4 * s.batch)
        high, low = split(grid_ref[start:end, :])
        moved = dot(jnp.concatenate([high, low, high], 1), table)
        for t in range(4):
            for row in range(0, end - start, s.batch):
                at = (start + row) // s.batch * s.step
                out_ref[t, at : at + s.batch, :] = moved[row : row + s.batch, t * s.length : (t + 1) * s.length]
    for t in range(4):
        out_ref[t, s.tiles * s.step :, :] = jnp.zeros(((s.even - s.tiles) * s.step, s.length), f32)


def space_kernel(s, bands, half_ref, *refs):
    slab_refs = refs[:bands]
    x_ahead_ref, x_back_ref, y_back_ref, flat_ref, field_ref, turned_ref = refs[bands:]
    width = s.length // bands
    band = lax.axis_index("band")
    at = place_on_ring(band, bands)
    for r, offset in enumerate(ring_offsets(bands)):
        owner = band_on_ring(lax.rem(at + offset + bands, bands), bands)
        field_ref[:, pl.ds(pl.multiple_of(owner * width, width), width), :] = slab_refs[r][...]
    total = s.tiles * s.batch
    for t in range(2, 4):
        turned_ref[t, s.odd * s.step :, :] = jnp.zeros(((s.even - s.odd) * s.step, s.length), f32)

    def plane(z, carry):
        parts = []
        for component in range(2):
            for parity in range(2):
                count = s.odd if parity else s.even
                parts.append(
                    jnp.concatenate(
                        [
                            half_ref[2 * parity + component, pl.ds(o * s.planes + z, count, stride=s.step), :]
                            for o in range(2)
                        ],
                        1,
                    )
                )
        high, low = split(jnp.concatenate(parts, 0))
        real = dot(x_ahead_ref[...], jnp.concatenate([high, high, low], 0))
        field = field_ref[z]
        high, low = split(real * jnp.concatenate([field, field], 1))
        turned = dot(x_back_ref[...], jnp.concatenate([high, low], 0))
        turned = turned[: s.kept] + turned[s.kept :]
        at = 0
        for component in range(2):
            for parity in range(2):
                count = s.odd if parity else s.even
                for o in range(2):
                    turned_ref[2 * parity + component, pl.ds(o * s.planes + z, count, stride=s.step), :] = turned[
                        at : at + count, o * s.length : (o + 1) * s.length
                    ]
                at += count
        return carry

    lax.fori_loop(0, s.planes, plane, 0, unroll=4)

    rows = 2 * s.batch
    lanes = 2 * s.rows_y
    table = jnp.concatenate([y_back_ref[0], y_back_ref[0], y_back_ref[1]], 0)
    for start in range(0, total, 4 * s.batch):
        end = min(total, start + 4 * s.batch)
        parts = []
        for row in range(start // s.batch * s.step, end // s.batch * s.step, s.step):
            parts.append(jnp.concatenate([turned_ref[t, row : row + s.batch, :] for t in range(4)], 1))
        high, low = split(jnp.concatenate(parts, 0))
        moved = dot(jnp.concatenate([high, low, high], 1), table)
        high, low = split(moved)
        for t in range((end - start) // s.batch):
            column = (start // s.batch + t) * lanes
            for component in range(2):
                row = component * s.batch
                mine = slice(t * s.batch, (t + 1) * s.batch), slice(component * lanes, (component + 1) * lanes)
                flat_ref[row : row + s.batch, column : column + lanes] = high[mine]
                flat_ref[rows + row : rows + row + s.batch, column : column + lanes] = low[mine]


def pick_kernel(s, which, flat_ref, sticks_ref, *refs):
    out_refs, (x_ref, y_ref, hot_ref) = refs[: len(which)], refs[len(which) :]
    me = lax.axis_index("plane")
    places(s, sticks_ref, [partner(me, k) for k in which], x_ref, y_ref)
    rows = 2 * s.batch
    for i in range(len(which)):
        columns = slice(i * s.sticks, (i + 1) * s.sticks)
        for x in range(2 * s.tiles):
            hot_ref[x * s.rows_y : (x + 1) * s.rows_y, :] = one_hot(x, x_ref[:, columns], y_ref[:, columns])
        found = dot(flat_ref[...], hot_ref[...])
        out_refs[i][...] = found[:rows] + found[rows:]


def band_on_ring(place, count):
    if count % 2:
        return place
    return jnp.where(2 * place < count, 2 * place, 2 * (count - 1 - place) + 1)


def place_on_ring(band, count):
    if count % 2:
        return band
    return jnp.where(lax.rem(band, 2) == 0, band // 2, count - 1 - band // 2)


def ring_offsets(count):
    offsets = [0]
    for step in range(1, count // 2 + 1):
        offsets += [-step, step]
    return offsets[:count]


def per_device(bands, coeffs, potential, stick_map):
    devices = stick_map.shape[1] // coeffs.shape[3]
    s = Sizes(coeffs.shape[2], coeffs.shape[3], potential.shape[2], potential.shape[0], devices)
    tab = {name: jnp.asarray(value) for name, value in tables(s).items()}
    rows = 2 * s.batch
    block = jax.ShapeDtypeStruct((rows, s.sticks), f32)

    order = list(range(bands)) if bands % 2 else list(range(0, bands, 2)) + list(range(bands - 1, 0, -2))
    along = [(order[i], order[(i + 1) % bands]) for i in range(bands)]
    against = [(b, a) for a, b in along]
    slabs = [potential]
    up = down = potential
    for _ in range(1, bands // 2 + 1):
        up = lax.ppermute(up, "band", along)
        slabs.append(up)
        if len(slabs) < bands:
            down = lax.ppermute(down, "band", against)
            slabs.append(down)

    def exchange(blocks):
        out = [blocks[0]] + [None] * (devices - 1)
        for k in reversed(range(1, devices)):
            out[k] = lax.ppermute(blocks[k], "plane", [(i, i ^ k) for i in range(devices)])
        return out

    def kernel(body, inputs, out_shape, limit, flops, scratch_shapes=()):
        return pl.pallas_call(
            body,
            in_specs=[VMEM] * len(inputs),
            out_specs=jax.tree.map(lambda _: VMEM, out_shape),
            out_shape=out_shape,
            scratch_shapes=scratch_shapes,
            compiler_params=pltpu.CompilerParams(vmem_limit_bytes=limit << 20),
            cost_estimate=pl.CostEstimate(flops=flops, bytes_accessed=1 << 20, transcendentals=0),
        )(*inputs)

    total = devices * s.sticks
    positions = 2 * s.tiles * s.rows_y
    results = []
    for pair in range(coeffs.shape[0]):
        given = jnp.transpose(coeffs[pair : pair + 1], (0, 2, 1, 3))
        sent = kernel(
            functools.partial(ahead_kernel, s), [given, stick_map, tab["z_ahead"]], [block] * devices, 16, 1 << 31
        )
        held = exchange(sent)
        half = kernel(
            functools.partial(plane_kernel, s),
            [*held, stick_map, tab["y_ahead"]],
            jax.ShapeDtypeStruct((4, s.even * s.step, s.length), f32),
            28,
            1 << 32,
            [
                pltpu.VMEM((s.rows_y, total), bf16),
                pltpu.VMEM((s.rows_y, total), bf16),
                pltpu.VMEM((s.tiles * s.batch, 4 * s.rows_y), f32),
                pltpu.VMEM((2 * rows, total), bf16),
            ],
        )
        flat = kernel(
            functools.partial(space_kernel, s, bands),
            [half, *slabs, tab["x_ahead"], tab["x_back"], tab["y_back"]],
            jax.ShapeDtypeStruct((2 * rows, positions), bf16),
            32,
            1 << 32,
            [
                pltpu.VMEM((s.planes, s.length, s.length), f32),
                pltpu.VMEM((4, s.even * s.step, s.length), f32),
            ],
        )
        mixed = [None] * devices
        groups = [[k] for k in reversed(range(2, devices))] + [list(range(min(2, devices)))[::-1]]
        for which in groups:
            parts = kernel(
                functools.partial(pick_kernel, s, which),
                [flat, stick_map],
                [block] * len(which),
                16,
                1 << 31,
                [
                    pltpu.VMEM((s.rows_y, len(which) * s.sticks), bf16),
                    pltpu.VMEM((s.rows_y, len(which) * s.sticks), bf16),
                    pltpu.VMEM((positions, s.sticks), bf16),
                ],
            )
            for k, part in zip(which, parts, strict=True):
                mixed[k] = part
        returned = exchange(mixed)
        result = kernel(
            functools.partial(back_kernel, s),
            [*returned, stick_map, tab["z_back"]],
            jax.ShapeDtypeStruct((1,) + given.shape[1:], f32),
            16,
            1 << 31,
        )
        results.append(jnp.transpose(result, (0, 2, 1, 3)))
    return results[0] if len(results) == 1 else jnp.concatenate(results, 0)


def solution(mesh):
    placed = (P("band", None, None, "plane"), P("plane", "band", None), P())
    return jax.shard_map(
        functools.partial(per_device, mesh.shape["band"]),
        mesh=mesh,
        in_specs=placed,
        out_specs=P("band", None, None, "plane"),
        check_vma=False,
    )
```

```python
import functools
import math

import jax
import jax.numpy as jnp
import ml_dtypes
import numpy as np
from jax import lax
from jax.experimental import pallas as pl
from jax.experimental.pallas import tpu as pltpu
from jax.sharding import PartitionSpec as P


bf16 = jnp.bfloat16
f32 = jnp.float32
VMEM = pl.BlockSpec(memory_space=pltpu.VMEM)
HBM = pl.BlockSpec(memory_space=pltpu.HBM)


def up8(n):
    return -(-n // 8) * 8


def halves(table):
    high = table.astype(ml_dtypes.bfloat16)
    return high, (table - high.astype(np.float64)).astype(ml_dtypes.bfloat16)


def split(value):
    high = value.astype(bf16)
    return high, (value - high.astype(f32)).astype(bf16)


class Sizes:
    def __init__(self, span, sticks, length, planes, devices):
        self.span, self.length, self.planes, self.devices = span, length, planes, devices
        self.sticks = sticks
        self.radius = (span - 1) // 2
        self.rows_y = 2 * self.radius
        self.tiles = self.radius // 2 + 1
        self.even = up8(self.tiles)
        self.odd = up8(self.radius // 2)
        self.kept = 2 * (self.even + self.odd)
        self.batch = 2 * planes
        self.step = self.batch + 1
        self.depth_rows = -(-4 * span // 16) * 16


def tables(s):
    turn = 2.0 * math.pi / s.length
    grid = np.arange(s.length)
    depth = np.arange(s.span) - s.radius
    y = np.arange(s.rows_y) + 1 - s.radius

    def trig(left, right):
        angle = turn * np.mod(np.outer(left, right), s.length)
        return np.cos(angle), np.sin(angle)

    cos, sin = trig(depth, grid)
    ahead = np.zeros((s.devices, 2, 2, s.planes, s.span, 2, 2))
    back = np.zeros((s.devices, s.span, 2, 2, 2, 2, s.planes))
    scale = 1.0 / float(s.length) ** 3
    for d in range(s.devices):
        own = slice(d * s.planes, (d + 1) * s.planes)
        c, n = cos[:, own], sin[:, own]
        for o in range(2):
            ahead[d, 0, o, :, :, o, 0] = c.T
            ahead[d, 0, o, :, :, o, 1] = -n.T
            ahead[d, 1, o, :, :, o, 0] = n.T
            ahead[d, 1, o, :, :, o, 1] = c.T
            back[d, :, o, 0, 0, o] = c * scale
            back[d, :, o, 0, 1, o] = n * scale
            back[d, :, o, 1, 0, o] = -n * scale
            back[d, :, o, 1, 1, o] = c * scale
    gap = s.depth_rows - 4 * s.span
    ahead = np.pad(ahead.reshape(s.devices, 2 * s.batch, 4 * s.span), ((0, 0), (0, 0), (0, gap)))
    back = np.pad(back.reshape(s.devices, 4 * s.span, 2 * s.batch), ((0, 0), (0, gap), (0, 0)))

    cos, sin = trig(y, grid)
    y_ahead = np.zeros((2, 2, s.rows_y, 2, 2, s.length))
    y_back = np.zeros((2, 2, s.length, 2, 2, s.rows_y))
    for parity in range(2):
        y_ahead[0, parity, :, parity, 0] = cos
        y_ahead[1, parity, :, parity, 0] = -sin
        y_ahead[0, parity, :, parity, 1] = sin
        y_ahead[1, parity, :, parity, 1] = cos
        y_back[parity, 0, :, 0, parity] = cos.T
        y_back[parity, 1, :, 0, parity] = sin.T
        y_back[parity, 0, :, 1, parity] = -sin.T
        y_back[parity, 1, :, 1, parity] = cos.T
    y_ahead = y_ahead.reshape(4 * s.rows_y, 4 * s.length)
    y_back = y_back.reshape(4 * s.length, 4 * s.rows_y)

    x_ahead = np.zeros((s.length, s.kept))
    x_back = np.zeros((s.kept, s.length))
    at = 0
    for component in range(2):
        for parity in range(2):
            count = s.tiles if parity == 0 else s.radius // 2
            cos, sin = trig(2 * np.arange(count) + parity, grid)
            x_ahead[:, at : at + count] = 2.0 * cos.T if component == 0 else -2.0 * sin.T
            x_back[at : at + count] = cos if component == 0 else -sin
            at += s.even if parity == 0 else s.odd

    def beside(table, axis, order):
        parts = halves(table)
        return np.concatenate([parts[i] for i in order], axis)

    zero = np.zeros(x_back.shape, ml_dtypes.bfloat16)
    high, low = halves(x_back)
    return dict(
        z_ahead=beside(ahead, 2, (0, 1, 0)),
        z_back=beside(back, 2, (0, 1)),
        y_ahead=np.stack(halves(y_ahead)),
        y_back=np.stack(halves(y_back)),
        x_ahead=beside(x_ahead, 1, (0, 1, 0)),
        x_back=np.concatenate([np.concatenate([high, high], 1), np.concatenate([low, zero], 1)], 0),
    )


def dot(left, right):
    return jnp.dot(left, right, preferred_element_type=f32)


def partner(me, k):
    return jnp.bitwise_xor(me, k)


def live_of(s, sticks_ref, source):
    columns = pl.ds(pl.multiple_of(source * s.sticks, s.sticks), s.sticks)
    depth = lax.broadcasted_iota(jnp.int32, (4 * s.span, s.sticks), 0) // 4 - s.radius
    return jnp.abs(depth) <= sticks_ref[2:3, columns]


def ahead_kernel(s, coeffs_hbm, sticks_hbm, table_hbm, *refs):
    out_refs, (coeffs_ref, sticks_ref, table_ref, sems) = refs[: s.devices], refs[s.devices :]
    pairs = [(sticks_hbm, sticks_ref), (coeffs_hbm, coeffs_ref), (table_hbm, table_ref)]
    copies = [pltpu.make_async_copy(source, target, sems.at[i]) for i, (source, target) in enumerate(pairs)]
    for copy in copies:
        copy.start()
    me = lax.axis_index("plane")
    copies[0].wait()
    live = live_of(s, sticks_ref, me)
    copies[1].wait()
    data = jnp.where(live, coeffs_ref[0].reshape(4 * s.span, s.sticks), 0.0)
    gap = jnp.zeros((s.depth_rows - 4 * s.span, s.sticks), f32)
    high, low = split(jnp.concatenate([data, gap], 0))
    data = jnp.concatenate([high, high, low], 0)
    copies[2].wait()
    for k in reversed(range(s.devices)):
        out_refs[k][...] = dot(table_ref[partner(me, k)], data)


def back_kernel(s, *refs):
    in_refs, (sticks_ref, table_ref, out_ref) = refs[: s.devices], refs[s.devices :]
    me = lax.axis_index("plane")
    total = None
    for k in range(s.devices):
        high, low = split(in_refs[k][...])
        table = table_ref[partner(me, k)]
        table = jnp.concatenate([table, table[:, : 2 * s.batch]], 1)
        term = dot(table, jnp.concatenate([high, high, low], 0))
        total = term if total is None else total + term
    total = jnp.where(live_of(s, sticks_ref, me), total[: 4 * s.span], 0.0)
    out_ref[0] = total.reshape(s.span, 4, s.sticks)


def places(s, sticks_ref, sources, x_ref, y_ref):
    at = 0
    for source in sources:
        columns = pl.ds(pl.multiple_of(source * s.sticks, s.sticks), s.sticks)
        shape = (s.rows_y, s.sticks)
        x_ref[:, at : at + s.sticks] = jnp.broadcast_to(sticks_ref[0:1, columns].astype(f32), shape).astype(bf16)
        row = lax.broadcasted_iota(jnp.int32, shape, 0) + 1 - s.radius
        hit = sticks_ref[1:2, columns] == row
        y_ref[:, at : at + s.sticks] = jnp.where(hit, 1.0, 0.0).astype(bf16)
        at += s.sticks


def one_hot(x, x_all, y_all):
    return jnp.where(x_all == jnp.asarray(x, bf16), y_all, jnp.zeros_like(y_all))


def plane_kernel(s, *refs):
    in_refs, (sticks_ref, table_ref, out_ref, x_ref, y_ref, grid_ref, both_ref) = refs[: s.devices], refs[s.devices :]
    me = lax.axis_index("plane")
    places(s, sticks_ref, [partner(me, k) for k in range(s.devices)], x_ref, y_ref)
    rows = 2 * s.batch
    for k in range(s.devices):
        high, low = split(in_refs[k][...])
        both_ref[:rows, k * s.sticks : (k + 1) * s.sticks] = high
        both_ref[rows:, k * s.sticks : (k + 1) * s.sticks] = low
    lanes = 2 * s.rows_y
    for first in range(0, s.tiles, 2):
        count = min(2, s.tiles - first)
        hot = jnp.concatenate([one_hot(x, x_ref[...], y_ref[...]) for x in range(2 * first, 2 * (first + count))], 0)
        laid = lax.dot_general(both_ref[...], hot, (((1,), (1,)), ((), ())), preferred_element_type=f32)
        laid = laid[:rows] + laid[rows:]
        for t in range(count):
            for component in range(2):
                grid_ref[
                    pl.ds((first + t) * s.batch, s.batch), component * lanes : (component + 1) * lanes
                ] = laid[component * s.batch : (component + 1) * s.batch, t * lanes : (t + 1) * lanes]
    total = s.tiles * s.batch
    table = jnp.concatenate([table_ref[0], table_ref[0], table_ref[1]], 0)
    for start in range(0, total, 4 * s.batch):
        end = min(total, start + 4 * s.batch)
        high, low = split(grid_ref[start:end, :])
        moved = dot(jnp.concatenate([high, low, high], 1), table)
        for t in range(4):
            for row in range(0, end - start, s.batch):
                at = (start + row) // s.batch * s.step
                out_ref[t, at : at + s.batch, :] = moved[row : row + s.batch, t * s.length : (t + 1) * s.length]
    for t in range(4):
        out_ref[t, s.tiles * s.step :, :] = jnp.zeros(((s.even - s.tiles) * s.step, s.length), f32)


def space_kernel(s, bands, half_ref, *refs):
    offsets = ring_offsets(bands)
    slab_refs, refs = refs[: len(offsets)], refs[len(offsets) :]
    x_ahead_ref, x_back_ref, y_back_ref, flat_ref, field_ref, turned_ref = refs
    width = s.length // bands
    band = lax.axis_index("band")
    at = place_on_ring(band, bands)
    for (offset, first, last), slab_ref in zip(offsets, slab_refs, strict=True):
        owner = band_on_ring(lax.rem(at + offset + bands, bands), bands)
        own = slice(first * s.planes // 2, last * s.planes // 2)
        field_ref[own, pl.ds(pl.multiple_of(owner * width, width), width), :] = slab_ref[...]
    total = s.tiles * s.batch
    for t in range(2, 4):
        turned_ref[t, s.odd * s.step :, :] = jnp.zeros(((s.even - s.odd) * s.step, s.length), f32)

    def plane(z, carry):
        parts = []
        for component in range(2):
            for parity in range(2):
                count = s.odd if parity else s.even
                parts.append(
                    jnp.concatenate(
                        [
                            half_ref[2 * parity + component, pl.ds(o * s.planes + z, count, stride=s.step), :]
                            for o in range(2)
                        ],
                        1,
                    )
                )
        high, low = split(jnp.concatenate(parts, 0))
        real = dot(x_ahead_ref[...], jnp.concatenate([high, high, low], 0))
        field = field_ref[z]
        high, low = split(real * jnp.concatenate([field, field], 1))
        turned = dot(x_back_ref[...], jnp.concatenate([high, low], 0))
        turned = turned[: s.kept] + turned[s.kept :]
        at = 0
        for component in range(2):
            for parity in range(2):
                count = s.odd if parity else s.even
                for o in range(2):
                    turned_ref[2 * parity + component, pl.ds(o * s.planes + z, count, stride=s.step), :] = turned[
                        at : at + count, o * s.length : (o + 1) * s.length
                    ]
                at += count
        return carry

    lax.fori_loop(0, s.planes, plane, 0, unroll=4)

    rows = 2 * s.batch
    lanes = 2 * s.rows_y
    table = jnp.concatenate([y_back_ref[0], y_back_ref[0], y_back_ref[1]], 0)
    for start in range(0, total, 4 * s.batch):
        end = min(total, start + 4 * s.batch)
        parts = []
        for row in range(start // s.batch * s.step, end // s.batch * s.step, s.step):
            parts.append(jnp.concatenate([turned_ref[t, row : row + s.batch, :] for t in range(4)], 1))
        high, low = split(jnp.concatenate(parts, 0))
        moved = dot(jnp.concatenate([high, low, high], 1), table)
        high, low = split(moved)
        for t in range((end - start) // s.batch):
            column = (start // s.batch + t) * lanes
            for component in range(2):
                row = component * s.batch
                mine = slice(t * s.batch, (t + 1) * s.batch), slice(component * lanes, (component + 1) * lanes)
                flat_ref[row : row + s.batch, column : column + lanes] = high[mine]
                flat_ref[rows + row : rows + row + s.batch, column : column + lanes] = low[mine]


def pick_kernel(s, which, flat_ref, sticks_ref, *refs):
    out_refs, (x_ref, y_ref, hot_ref) = refs[: len(which)], refs[len(which) :]
    me = lax.axis_index("plane")
    places(s, sticks_ref, [partner(me, k) for k in which], x_ref, y_ref)
    rows = 2 * s.batch
    for i in range(len(which)):
        columns = slice(i * s.sticks, (i + 1) * s.sticks)
        for x in range(2 * s.tiles):
            hot_ref[x * s.rows_y : (x + 1) * s.rows_y, :] = one_hot(x, x_ref[:, columns], y_ref[:, columns])
        found = dot(flat_ref[...], hot_ref[...])
        out_refs[i][...] = found[:rows] + found[rows:]


def band_on_ring(place, count):
    if count % 2:
        return place
    return jnp.where(2 * place < count, 2 * place, 2 * (count - 1 - place) + 1)


def place_on_ring(band, count):
    if count % 2:
        return band
    return jnp.where(lax.rem(band, 2) == 0, band // 2, count - 1 - band // 2)


def ring_offsets(count):
    offsets = [(0, 0, 2)]
    for step in range(1, count // 2 + 1):
        last = 2 * step == count
        offsets += [(-step, 0, 1 if last else 2), (step, 1 if last else 0, 2)]
    return offsets


def per_device(bands, coeffs, potential, stick_map):
    devices = stick_map.shape[1] // coeffs.shape[3]
    s = Sizes(coeffs.shape[2], coeffs.shape[3], potential.shape[2], potential.shape[0], devices)
    tab = {name: jnp.asarray(value) for name, value in tables(s).items()}
    rows = 2 * s.batch
    block = jax.ShapeDtypeStruct((rows, s.sticks), f32)

    order = list(range(bands)) if bands % 2 else list(range(0, bands, 2)) + list(range(bands - 1, 0, -2))
    along = [(order[i], order[(i + 1) % bands]) for i in range(bands)]
    against = [(b, a) for a, b in along]

    def exchange(blocks):
        out = [blocks[0]] + [None] * (devices - 1)
        for k in reversed(range(1, devices)):
            out[k] = lax.ppermute(blocks[k], "plane", [(i, i ^ k) for i in range(devices)])
        return out

    def ring():
        slabs = [potential]
        up = down = potential
        for step in range(1, bands // 2 + 1):
            last = 2 * step == bands
            if last:
                up, down = up[: s.planes // 2], down[s.planes // 2 :]
            up = lax.ppermute(up, "band", along)
            down = lax.ppermute(down, "band", against)
            slabs += [up, down]
        return slabs

    def kernel(body, inputs, out_shape, limit, flops, scratch_shapes=(), place=VMEM):
        return pl.pallas_call(
            body,
            in_specs=[place] * len(inputs),
            out_specs=jax.tree.map(lambda _: VMEM, out_shape),
            out_shape=out_shape,
            scratch_shapes=scratch_shapes,
            compiler_params=pltpu.CompilerParams(vmem_limit_bytes=limit << 10),
            cost_estimate=pl.CostEstimate(flops=flops, bytes_accessed=1 << 20, transcendentals=0),
        )(*inputs)

    slabs = ring()
    total = devices * s.sticks
    positions = 2 * s.tiles * s.rows_y
    results = []
    for pair in range(coeffs.shape[0]):
        given = jnp.transpose(coeffs[pair : pair + 1], (0, 2, 1, 3))
        sent = kernel(
            functools.partial(ahead_kernel, s),
            [pltpu.with_memory_space_constraint(a, pltpu.HBM) for a in (given, stick_map, tab["z_ahead"])],
            [block] * devices,
            16 << 10,
            1 << 31,
            [
                pltpu.VMEM(given.shape, f32),
                pltpu.VMEM(stick_map.shape, jnp.int32),
                pltpu.VMEM(tab["z_ahead"].shape, bf16),
                pltpu.SemaphoreType.DMA((3,)),
            ],
            HBM,
        )
        held = exchange(sent)
        half = kernel(
            functools.partial(plane_kernel, s),
            [*held, stick_map, tab["y_ahead"]],
            jax.ShapeDtypeStruct((4, s.even * s.step, s.length), f32),
            28 << 10,
            1 << 32,
            [
                pltpu.VMEM((s.rows_y, total), bf16),
                pltpu.VMEM((s.rows_y, total), bf16),
                pltpu.VMEM((s.tiles * s.batch, 4 * s.rows_y), f32),
                pltpu.VMEM((2 * rows, total), bf16),
            ],
        )
        flat = kernel(
            functools.partial(space_kernel, s, bands),
            [half, *slabs, tab["x_ahead"], tab["x_back"], tab["y_back"]],
            jax.ShapeDtypeStruct((2 * rows, positions), bf16),
            32 << 10,
            1 << 32,
            [
                pltpu.VMEM((s.planes, s.length, s.length), f32),
                pltpu.VMEM((4, s.even * s.step, s.length), f32),
            ],
        )
        mixed = [None] * devices
        groups = [[k] for k in reversed(range(2, devices))] + [list(range(min(2, devices)))[::-1]]
        for which in groups:
            parts = kernel(
                functools.partial(pick_kernel, s, which),
                [flat, stick_map],
                [block] * len(which),
                16 << 10,
                1 << 31,
                [
                    pltpu.VMEM((s.rows_y, len(which) * s.sticks), bf16),
                    pltpu.VMEM((s.rows_y, len(which) * s.sticks), bf16),
                    pltpu.VMEM((positions, s.sticks), bf16),
                ],
            )
            for k, part in zip(which, parts, strict=True):
                mixed[k] = part
        returned = exchange(mixed)
        result = kernel(
            functools.partial(back_kernel, s),
            [*returned, stick_map, tab["z_back"]],
            jax.ShapeDtypeStruct((1,) + given.shape[1:], f32),
            16 << 10,
            1 << 31,
        )
        results.append(jnp.transpose(result, (0, 2, 1, 3)))
    return results[0] if len(results) == 1 else jnp.concatenate(results, 0)


def solution(mesh):
    placed = (P("band", None, None, "plane"), P("plane", "band", None), P())
    return jax.shard_map(
        functools.partial(per_device, mesh.shape["band"]),
        mesh=mesh,
        in_specs=placed,
        out_specs=P("band", None, None, "plane"),
        check_vma=False,
    )
```

```python
import functools
import math

import jax
import jax.numpy as jnp
import ml_dtypes
import numpy as np
from jax import lax
from jax.experimental import pallas as pl
from jax.experimental.pallas import tpu as pltpu
from jax.sharding import PartitionSpec as P


bf16 = jnp.bfloat16
f32 = jnp.float32
VMEM = pl.BlockSpec(memory_space=pltpu.VMEM)
HBM = pl.BlockSpec(memory_space=pltpu.HBM)


def up8(n):
    return -(-n // 8) * 8


def halves(table):
    high = table.astype(ml_dtypes.bfloat16)
    return high, (table - high.astype(np.float64)).astype(ml_dtypes.bfloat16)


def split(value):
    high = value.astype(bf16)
    return high, (value - high.astype(f32)).astype(bf16)


class Sizes:
    def __init__(self, span, sticks, length, planes, devices):
        self.span, self.length, self.planes, self.devices = span, length, planes, devices
        self.sticks = sticks
        self.radius = (span - 1) // 2
        self.rows_y = 2 * self.radius
        self.tiles = self.radius // 2 + 1
        self.even = up8(self.tiles)
        self.odd = up8(self.radius // 2)
        self.kept = 2 * (self.even + self.odd)
        self.batch = 2 * planes
        self.step = self.batch + 1
        self.depth_rows = -(-4 * span // 16) * 16


def tables(s, bands):
    turn = 2.0 * math.pi / s.length
    grid = np.arange(s.length)
    depth = np.arange(s.span) - s.radius
    y = np.arange(s.rows_y) + 1 - s.radius

    def trig(left, right):
        angle = turn * np.mod(np.outer(left, right), s.length)
        return np.cos(angle), np.sin(angle)

    cos, sin = trig(depth, grid)
    ahead = np.zeros((s.devices, 2, 2, s.planes, s.span, 2, 2))
    back = np.zeros((s.devices, s.span, 2, 2, 2, 2, s.planes))
    scale = 1.0 / float(s.length) ** 3
    for d in range(s.devices):
        own = slice(d * s.planes, (d + 1) * s.planes)
        c, n = cos[:, own], sin[:, own]
        for o in range(2):
            ahead[d, 0, o, :, :, o, 0] = c.T
            ahead[d, 0, o, :, :, o, 1] = -n.T
            ahead[d, 1, o, :, :, o, 0] = n.T
            ahead[d, 1, o, :, :, o, 1] = c.T
            back[d, :, o, 0, 0, o] = c * scale
            back[d, :, o, 0, 1, o] = n * scale
            back[d, :, o, 1, 0, o] = -n * scale
            back[d, :, o, 1, 1, o] = c * scale
    gap = s.depth_rows - 4 * s.span
    ahead = np.pad(ahead.reshape(s.devices, 2 * s.batch, 4 * s.span), ((0, 0), (0, 0), (0, gap)))
    back = np.pad(back.reshape(s.devices, 4 * s.span, 2 * s.batch), ((0, 0), (0, gap), (0, 0)))

    cos, sin = trig(y, grid)
    y_ahead = np.zeros((2, 2, s.rows_y, 2, 2, s.length))
    y_back = np.zeros((2, 2, s.length, 2, 2, s.rows_y))
    for parity in range(2):
        y_ahead[0, parity, :, parity, 0] = cos
        y_ahead[1, parity, :, parity, 0] = -sin
        y_ahead[0, parity, :, parity, 1] = sin
        y_ahead[1, parity, :, parity, 1] = cos
        y_back[parity, 0, :, 0, parity] = cos.T
        y_back[parity, 1, :, 0, parity] = sin.T
        y_back[parity, 0, :, 1, parity] = -sin.T
        y_back[parity, 1, :, 1, parity] = cos.T
    y_ahead = y_ahead.reshape(4 * s.rows_y, 4 * s.length)
    y_back = y_back.reshape(4 * s.length, 4 * s.rows_y)

    x_ahead = np.zeros((s.length, s.kept))
    x_back = np.zeros((s.kept, s.length))
    at = 0
    for component in range(2):
        for parity in range(2):
            count = s.tiles if parity == 0 else s.radius // 2
            cos, sin = trig(2 * np.arange(count) + parity, grid)
            x_ahead[:, at : at + count] = 2.0 * cos.T if component == 0 else -2.0 * sin.T
            x_back[at : at + count] = cos if component == 0 else -sin
            at += s.even if parity == 0 else s.odd

    def beside(table, axis, order):
        parts = halves(table)
        return np.concatenate([parts[i] for i in order], axis)

    zero = np.zeros(x_back.shape, ml_dtypes.bfloat16)
    high, low = halves(x_back)
    by_slab = x_back.reshape(s.kept, bands, s.length // bands).transpose(1, 0, 2)
    return dict(
        z_ahead=beside(ahead, 2, (0, 1, 0)),
        z_back=beside(back, 2, (0, 1)),
        y_ahead=np.stack(halves(y_ahead)),
        y_back=np.stack(halves(y_back)),
        x_ahead=beside(x_ahead, 1, (0, 1, 0)),
        x_last=beside(by_slab, 2, (0, 0, 1)),
        x_back=np.concatenate([np.concatenate([high, high], 1), np.concatenate([low, zero], 1)], 0),
    )


def dot(left, right):
    return jnp.dot(left, right, preferred_element_type=f32)


def partner(me, k):
    return jnp.bitwise_xor(me, k)


def live_of(s, sticks_ref, source):
    columns = pl.ds(pl.multiple_of(source * s.sticks, s.sticks), s.sticks)
    depth = lax.broadcasted_iota(jnp.int32, (4 * s.span, s.sticks), 0) // 4 - s.radius
    return jnp.abs(depth) <= sticks_ref[2:3, columns]


def ahead_kernel(s, coeffs_hbm, sticks_hbm, table_hbm, *refs):
    out_refs, (coeffs_ref, sticks_ref, table_ref, sems) = refs[: s.devices], refs[s.devices :]
    pairs = [(sticks_hbm, sticks_ref), (coeffs_hbm, coeffs_ref), (table_hbm, table_ref)]
    copies = [pltpu.make_async_copy(source, target, sems.at[i]) for i, (source, target) in enumerate(pairs)]
    for copy in copies:
        copy.start()
    me = lax.axis_index("plane")
    copies[0].wait()
    live = live_of(s, sticks_ref, me)
    copies[1].wait()
    data = jnp.where(live, coeffs_ref[0].reshape(4 * s.span, s.sticks), 0.0)
    gap = jnp.zeros((s.depth_rows - 4 * s.span, s.sticks), f32)
    high, low = split(jnp.concatenate([data, gap], 0))
    data = jnp.concatenate([high, high, low], 0)
    copies[2].wait()
    for k in reversed(range(s.devices)):
        out_refs[k][...] = dot(table_ref[partner(me, k)], data)


def back_kernel(s, which, started, ended, *refs):
    in_refs, refs = refs[: len(which)], refs[len(which) :]
    table_ref, out_ref = refs[-2:]
    me = lax.axis_index("plane")
    total = refs[0][...] if started else None
    for i, k in enumerate(which):
        high, low = split(in_refs[i][...])
        table = table_ref[partner(me, k)]
        table = jnp.concatenate([table, table[:, : 2 * s.batch]], 1)
        term = dot(table, jnp.concatenate([high, high, low], 0))
        total = term if total is None else total + term
    if ended:
        total = jnp.where(live_of(s, refs[-3], me), total[: 4 * s.span], 0.0)
        out_ref[0] = total.reshape(s.span, 4, s.sticks)
    else:
        out_ref[...] = total


def places(s, sticks_ref, sources, x_ref, y_ref):
    at = 0
    for source in sources:
        columns = pl.ds(pl.multiple_of(source * s.sticks, s.sticks), s.sticks)
        shape = (s.rows_y, s.sticks)
        x_ref[:, at : at + s.sticks] = jnp.broadcast_to(sticks_ref[0:1, columns].astype(f32), shape).astype(bf16)
        row = lax.broadcasted_iota(jnp.int32, shape, 0) + 1 - s.radius
        hit = sticks_ref[1:2, columns] == row
        y_ref[:, at : at + s.sticks] = jnp.where(hit, 1.0, 0.0).astype(bf16)
        at += s.sticks


def one_hot(x, x_all, y_all):
    return jnp.where(x_all == jnp.asarray(x, bf16), y_all, jnp.zeros_like(y_all))


def plane_kernel(s, *refs):
    in_refs, (sticks_ref, table_ref, out_ref, x_ref, y_ref, grid_ref, both_ref) = refs[: s.devices], refs[s.devices :]
    me = lax.axis_index("plane")
    places(s, sticks_ref, [partner(me, k) for k in range(s.devices)], x_ref, y_ref)
    rows = 2 * s.batch
    for k in range(s.devices):
        high, low = split(in_refs[k][...])
        both_ref[:rows, k * s.sticks : (k + 1) * s.sticks] = high
        both_ref[rows:, k * s.sticks : (k + 1) * s.sticks] = low
    lanes = 2 * s.rows_y
    for first in range(0, s.tiles, 2):
        count = min(2, s.tiles - first)
        hot = jnp.concatenate([one_hot(x, x_ref[...], y_ref[...]) for x in range(2 * first, 2 * (first + count))], 0)
        laid = lax.dot_general(both_ref[...], hot, (((1,), (1,)), ((), ())), preferred_element_type=f32)
        laid = laid[:rows] + laid[rows:]
        for t in range(count):
            for component in range(2):
                grid_ref[
                    pl.ds((first + t) * s.batch, s.batch), component * lanes : (component + 1) * lanes
                ] = laid[component * s.batch : (component + 1) * s.batch, t * lanes : (t + 1) * lanes]
    total = s.tiles * s.batch
    table = jnp.concatenate([table_ref[0], table_ref[0], table_ref[1]], 0)
    for start in range(0, total, 4 * s.batch):
        end = min(total, start + 4 * s.batch)
        high, low = split(grid_ref[start:end, :])
        moved = dot(jnp.concatenate([high, low, high], 1), table)
        for t in range(4):
            for row in range(0, end - start, s.batch):
                at = (start + row) // s.batch * s.step
                out_ref[t, at : at + s.batch, :] = moved[row : row + s.batch, t * s.length : (t + 1) * s.length]
    for t in range(4):
        out_ref[t, s.tiles * s.step :, :] = jnp.zeros(((s.even - s.tiles) * s.step, s.length), f32)


def space_kernel(s, bands, half_ref, *refs):
    offsets = ring_offsets(bands)[:-2]
    slab_refs, (x_ahead_ref, x_back_ref, turned_ref, real_ref, field_ref) = refs[: len(offsets)], refs[len(offsets) :]
    width = s.length // bands
    band = lax.axis_index("band")
    at = place_on_ring(band, bands)
    for (offset, _, _), slab_ref in zip(offsets, slab_refs, strict=True):
        owner = band_on_ring(lax.rem(at + offset + bands, bands), bands)
        field_ref[:, pl.ds(pl.multiple_of(owner * width, width), width), :] = slab_ref[...]
    last = pl.ds(pl.multiple_of(last_owner(bands) * width, width), width)
    field_ref[:, last, :] = jnp.zeros((s.planes, width, s.length), f32)
    for t in range(2, 4):
        turned_ref[t, s.odd * s.step :, :] = jnp.zeros(((s.even - s.odd) * s.step, s.length), f32)
    table = jnp.concatenate([x_ahead_ref[...], x_ahead_ref[last, :]], 0)

    def plane(z, carry):
        parts = []
        for component in range(2):
            for parity in range(2):
                count = s.odd if parity else s.even
                parts.append(
                    jnp.concatenate(
                        [
                            half_ref[2 * parity + component, pl.ds(o * s.planes + z, count, stride=s.step), :]
                            for o in range(2)
                        ],
                        1,
                    )
                )
        high, low = split(jnp.concatenate(parts, 0))
        real = dot(table, jnp.concatenate([high, high, low], 0))
        real_ref[z] = real[s.length :]
        field = field_ref[z]
        high, low = split(real[: s.length] * jnp.concatenate([field, field], 1))
        turned = dot(x_back_ref[...], jnp.concatenate([high, low], 0))
        keep_turned(s, turned_ref, z, turned[: s.kept] + turned[s.kept :])
        return carry

    lax.fori_loop(0, s.planes, plane, 0, unroll=4)


def keep_turned(s, turned_ref, z, turned):
    at = 0
    for component in range(2):
        for parity in range(2):
            count = s.odd if parity else s.even
            for o in range(2):
                turned_ref[2 * parity + component, pl.ds(o * s.planes + z, count, stride=s.step), :] = turned[
                    at : at + count, o * s.length : (o + 1) * s.length
                ]
            at += count


def finish_kernel(s, bands, first_ref, real_ref, up_ref, down_ref, x_last_ref, y_back_ref, flat_ref, turned_ref):
    total = s.tiles * s.batch
    for t in range(2, 4):
        turned_ref[t, s.odd * s.step :, :] = jnp.zeros(((s.even - s.odd) * s.step, s.length), f32)
    x_last = x_last_ref[last_owner(bands)]
    part = s.planes // 2
    for slab_ref, start in ((up_ref, 0), (down_ref, part)):

        def plane(z, carry, slab_ref=slab_ref, start=start):
            field = slab_ref[z]
            high, low = split(real_ref[start + z] * jnp.concatenate([field, field], 1))
            keep_turned(s, turned_ref, start + z, dot(x_last, jnp.concatenate([high, low, high], 0)))
            return carry

        lax.fori_loop(0, part, plane, 0, unroll=4)

    rows = 2 * s.batch
    lanes = 2 * s.rows_y
    table = jnp.concatenate([y_back_ref[0], y_back_ref[0], y_back_ref[1]], 0)
    for start in range(0, total, 4 * s.batch):
        end = min(total, start + 4 * s.batch)
        parts = []
        for row in range(start // s.batch * s.step, end // s.batch * s.step, s.step):
            own = slice(row, row + s.batch)
            parts.append(jnp.concatenate([first_ref[t, own, :] + turned_ref[t, own, :] for t in range(4)], 1))
        high, low = split(jnp.concatenate(parts, 0))
        moved = dot(jnp.concatenate([high, low, high], 1), table)
        high, low = split(moved)
        for t in range((end - start) // s.batch):
            column = (start // s.batch + t) * lanes
            for component in range(2):
                row = component * s.batch
                mine = slice(t * s.batch, (t + 1) * s.batch), slice(component * lanes, (component + 1) * lanes)
                flat_ref[row : row + s.batch, column : column + lanes] = high[mine]
                flat_ref[rows + row : rows + row + s.batch, column : column + lanes] = low[mine]


def pick_kernel(s, which, flat_ref, sticks_ref, *refs):
    out_refs, (x_ref, y_ref, hot_ref) = refs[: len(which)], refs[len(which) :]
    me = lax.axis_index("plane")
    places(s, sticks_ref, [partner(me, k) for k in which], x_ref, y_ref)
    rows = 2 * s.batch
    for i in range(len(which)):
        columns = slice(i * s.sticks, (i + 1) * s.sticks)
        for x in range(2 * s.tiles):
            hot_ref[x * s.rows_y : (x + 1) * s.rows_y, :] = one_hot(x, x_ref[:, columns], y_ref[:, columns])
        found = dot(flat_ref[...], hot_ref[...])
        out_refs[i][...] = found[:rows] + found[rows:]


def band_on_ring(place, count):
    return jnp.where(2 * place < count, 2 * place, 2 * (count - 1 - place) + 1)


def place_on_ring(band, count):
    return jnp.where(lax.rem(band, 2) == 0, band // 2, count - 1 - band // 2)


def last_owner(count):
    return band_on_ring(lax.rem(place_on_ring(lax.axis_index("band"), count) + count // 2, count), count)


def ring_offsets(count):
    offsets = [(0, 0, 2)]
    for step in range(1, count // 2 + 1):
        last = 2 * step == count
        offsets += [(-step, 0, 1 if last else 2), (step, 1 if last else 0, 2)]
    return offsets


def per_device(bands, coeffs, potential, stick_map):
    devices = stick_map.shape[1] // coeffs.shape[3]
    s = Sizes(coeffs.shape[2], coeffs.shape[3], potential.shape[2], potential.shape[0], devices)
    tab = {name: jnp.asarray(value) for name, value in tables(s, bands).items()}
    rows = 2 * s.batch
    block = jax.ShapeDtypeStruct((rows, s.sticks), f32)

    order = list(range(0, bands, 2)) + list(range(bands - 1, 0, -2))
    along = [(order[i], order[(i + 1) % bands]) for i in range(bands)]
    against = [(b, a) for a, b in along]

    def exchange(blocks):
        out = [blocks[0]] + [None] * (devices - 1)
        for k in reversed(range(1, devices)):
            out[k] = lax.ppermute(blocks[k], "plane", [(i, i ^ k) for i in range(devices)])
        return out

    def ring():
        slabs = [potential]
        up = down = potential
        for step in range(1, bands // 2 + 1):
            last = 2 * step == bands
            if last:
                up, down = up[: s.planes // 2], down[s.planes // 2 :]
            up = lax.ppermute(up, "band", along)
            down = lax.ppermute(down, "band", against)
            slabs += [up, down]
        return slabs

    def kernel(body, inputs, out_shape, limit, flops, scratch_shapes=(), place=VMEM):
        return pl.pallas_call(
            body,
            in_specs=[place] * len(inputs),
            out_specs=jax.tree.map(lambda _: VMEM, out_shape),
            out_shape=out_shape,
            scratch_shapes=scratch_shapes,
            compiler_params=pltpu.CompilerParams(vmem_limit_bytes=limit << 10),
            cost_estimate=pl.CostEstimate(flops=flops, bytes_accessed=1 << 20, transcendentals=0),
        )(*inputs)

    slabs = ring()
    total = devices * s.sticks
    positions = 2 * s.tiles * s.rows_y
    results = []
    for pair in range(coeffs.shape[0]):
        given = jnp.transpose(coeffs[pair : pair + 1], (0, 2, 1, 3))
        sent = kernel(
            functools.partial(ahead_kernel, s),
            [pltpu.with_memory_space_constraint(a, pltpu.HBM) for a in (given, stick_map, tab["z_ahead"])],
            [block] * devices,
            16 << 10,
            1 << 31,
            [
                pltpu.VMEM(given.shape, f32),
                pltpu.VMEM(stick_map.shape, jnp.int32),
                pltpu.VMEM(tab["z_ahead"].shape, bf16),
                pltpu.SemaphoreType.DMA((3,)),
            ],
            HBM,
        )
        held = exchange(sent)
        half = kernel(
            functools.partial(plane_kernel, s),
            [*held, stick_map, tab["y_ahead"]],
            jax.ShapeDtypeStruct((4, s.even * s.step, s.length), f32),
            28 << 10,
            1 << 32,
            [
                pltpu.VMEM((s.rows_y, total), bf16),
                pltpu.VMEM((s.rows_y, total), bf16),
                pltpu.VMEM((s.tiles * s.batch, 4 * s.rows_y), f32),
                pltpu.VMEM((2 * rows, total), bf16),
            ],
        )
        turned_shape = (4, s.even * s.step, s.length)
        turned, real = kernel(
            functools.partial(space_kernel, s, bands),
            [half, *slabs[:-2], tab["x_ahead"], tab["x_back"]],
            [
                jax.ShapeDtypeStruct(turned_shape, f32),
                jax.ShapeDtypeStruct((s.planes, s.length // bands, 2 * s.length), f32),
            ],
            16 << 10,
            1 << 32,
            [pltpu.VMEM((s.planes, s.length, s.length), f32)],
        )
        flat = kernel(
            functools.partial(finish_kernel, s, bands),
            [turned, real, *slabs[-2:], tab["x_last"], tab["y_back"]],
            jax.ShapeDtypeStruct((2 * rows, positions), bf16),
            24 << 10,
            1 << 32,
            [pltpu.VMEM(turned_shape, f32)],
        )
        mixed = [None] * devices
        groups = [[k] for k in reversed(range(2, devices))] + [list(range(min(2, devices)))[::-1]]
        for which in groups:
            parts = kernel(
                functools.partial(pick_kernel, s, which),
                [flat, stick_map],
                [block] * len(which),
                16 << 10,
                1 << 31,
                [
                    pltpu.VMEM((s.rows_y, len(which) * s.sticks), bf16),
                    pltpu.VMEM((s.rows_y, len(which) * s.sticks), bf16),
                    pltpu.VMEM((positions, s.sticks), bf16),
                ],
            )
            for k, part in zip(which, parts, strict=True):
                mixed[k] = part
        returned = exchange(mixed)
        early = [k for k in range(devices) if k != 2]
        begun = kernel(
            functools.partial(back_kernel, s, early, False, False),
            [*(returned[k] for k in early), tab["z_back"]],
            jax.ShapeDtypeStruct((s.depth_rows, s.sticks), f32),
            16 << 10,
            1 << 31,
        )
        result = kernel(
            functools.partial(back_kernel, s, [2], True, True),
            [returned[2], begun, stick_map, tab["z_back"]],
            jax.ShapeDtypeStruct((1,) + given.shape[1:], f32),
            16 << 10,
            1 << 31,
        )
        results.append(jnp.transpose(result, (0, 2, 1, 3)))
    return results[0] if len(results) == 1 else jnp.concatenate(results, 0)


def solution(mesh):
    placed = (P("band", None, None, "plane"), P("plane", "band", None), P())
    return jax.shard_map(
        functools.partial(per_device, mesh.shape["band"]),
        mesh=mesh,
        in_specs=placed,
        out_specs=P("band", None, None, "plane"),
        check_vma=False,
    )
```

```python
import functools
import math

import jax
import jax.numpy as jnp
import ml_dtypes
import numpy as np
from jax import lax
from jax.experimental import pallas as pl
from jax.experimental.pallas import tpu as pltpu
from jax.sharding import PartitionSpec as P


bf16 = jnp.bfloat16
f32 = jnp.float32
VMEM = pl.BlockSpec(memory_space=pltpu.VMEM)
HBM = pl.BlockSpec(memory_space=pltpu.HBM)


def up8(n):
    return -(-n // 8) * 8


def halves(table):
    high = table.astype(ml_dtypes.bfloat16)
    return high, (table - high.astype(np.float64)).astype(ml_dtypes.bfloat16)


def split(value):
    high = value.astype(bf16)
    return high, (value - high.astype(f32)).astype(bf16)


class Sizes:
    def __init__(self, span, sticks, length, planes, devices):
        self.span, self.length, self.planes, self.devices = span, length, planes, devices
        self.sticks = sticks
        self.radius = (span - 1) // 2
        self.rows_y = 2 * self.radius
        self.tiles = self.radius // 2 + 1
        self.even = up8(self.tiles)
        self.odd = up8(self.radius // 2)
        self.kept = 2 * (self.even + self.odd)
        self.batch = 2 * planes
        self.step = self.batch + 1
        self.depth_rows = -(-4 * span // 16) * 16


def tables(s, bands):
    turn = 2.0 * math.pi / s.length
    grid = np.arange(s.length)
    depth = np.arange(s.span) - s.radius
    y = np.arange(s.rows_y) + 1 - s.radius

    def trig(left, right):
        angle = turn * np.mod(np.outer(left, right), s.length)
        return np.cos(angle), np.sin(angle)

    cos, sin = trig(depth, grid)
    ahead = np.zeros((s.devices, 2, 2, s.planes, s.span, 2, 2))
    back = np.zeros((s.devices, s.span, 2, 2, 2, 2, s.planes))
    scale = 1.0 / float(s.length) ** 3
    for d in range(s.devices):
        own = slice(d * s.planes, (d + 1) * s.planes)
        c, n = cos[:, own], sin[:, own]
        for o in range(2):
            ahead[d, 0, o, :, :, o, 0] = c.T
            ahead[d, 0, o, :, :, o, 1] = -n.T
            ahead[d, 1, o, :, :, o, 0] = n.T
            ahead[d, 1, o, :, :, o, 1] = c.T
            back[d, :, o, 0, 0, o] = c * scale
            back[d, :, o, 0, 1, o] = n * scale
            back[d, :, o, 1, 0, o] = -n * scale
            back[d, :, o, 1, 1, o] = c * scale
    gap = s.depth_rows - 4 * s.span
    ahead = np.pad(ahead.reshape(s.devices, 2 * s.batch, 4 * s.span), ((0, 0), (0, 0), (0, gap)))
    back = np.pad(back.reshape(s.devices, 4 * s.span, 2 * s.batch), ((0, 0), (0, gap), (0, 0)))

    cos, sin = trig(y, grid)
    y_ahead = np.zeros((2, 2, s.rows_y, 2, 2, s.length))
    y_back = np.zeros((2, 2, s.length, 2, 2, s.rows_y))
    for parity in range(2):
        y_ahead[0, parity, :, parity, 0] = cos
        y_ahead[1, parity, :, parity, 0] = -sin
        y_ahead[0, parity, :, parity, 1] = sin
        y_ahead[1, parity, :, parity, 1] = cos
        y_back[parity, 0, :, 0, parity] = cos.T
        y_back[parity, 1, :, 0, parity] = sin.T
        y_back[parity, 0, :, 1, parity] = -sin.T
        y_back[parity, 1, :, 1, parity] = cos.T
    y_ahead = y_ahead.reshape(4 * s.rows_y, 4 * s.length)
    y_back = y_back.reshape(4 * s.length, 4 * s.rows_y)

    x_ahead = np.zeros((s.length, s.kept))
    x_back = np.zeros((s.kept, s.length))
    at = 0
    for component in range(2):
        for parity in range(2):
            count = s.tiles if parity == 0 else s.radius // 2
            cos, sin = trig(2 * np.arange(count) + parity, grid)
            x_ahead[:, at : at + count] = 2.0 * cos.T if component == 0 else -2.0 * sin.T
            x_back[at : at + count] = cos if component == 0 else -sin
            at += s.even if parity == 0 else s.odd

    def beside(table, axis, order):
        parts = halves(table)
        return np.concatenate([parts[i] for i in order], axis)

    zero = np.zeros(x_back.shape, ml_dtypes.bfloat16)
    high, low = halves(x_back)
    by_slab = x_back.reshape(s.kept, bands, s.length // bands).transpose(1, 0, 2)
    return dict(
        z_ahead=beside(ahead, 2, (0, 1, 0)),
        z_back=beside(back, 2, (0, 1)),
        y_ahead=np.stack(halves(y_ahead)),
        y_back=np.stack(halves(y_back)),
        x_ahead=beside(x_ahead, 1, (0, 1, 0)),
        x_last=beside(by_slab, 2, (0, 0, 1)),
        x_back=np.concatenate([np.concatenate([high, high], 1), np.concatenate([low, zero], 1)], 0),
    )


def dot(left, right):
    return jnp.dot(left, right, preferred_element_type=f32)


def partner(me, k):
    return jnp.bitwise_xor(me, k)


def live_of(s, sticks_ref, source):
    columns = pl.ds(pl.multiple_of(source * s.sticks, s.sticks), s.sticks)
    depth = lax.broadcasted_iota(jnp.int32, (4 * s.span, s.sticks), 0) // 4 - s.radius
    return jnp.abs(depth) <= sticks_ref[2:3, columns]


def ahead_kernel(s, coeffs_hbm, sticks_hbm, table_hbm, *refs):
    out_refs, (coeffs_ref, sticks_ref, table_ref, sems) = refs[: s.devices], refs[s.devices :]
    pairs = [(sticks_hbm, sticks_ref), (coeffs_hbm, coeffs_ref), (table_hbm, table_ref)]
    copies = [pltpu.make_async_copy(source, target, sems.at[i]) for i, (source, target) in enumerate(pairs)]
    for copy in copies:
        copy.start()
    me = lax.axis_index("plane")
    copies[0].wait()
    live = live_of(s, sticks_ref, me)
    copies[1].wait()
    data = jnp.where(live, coeffs_ref[0].reshape(4 * s.span, s.sticks), 0.0)
    gap = jnp.zeros((s.depth_rows - 4 * s.span, s.sticks), f32)
    high, low = split(jnp.concatenate([data, gap], 0))
    data = jnp.concatenate([high, high, low], 0)
    copies[2].wait()
    for k in [*partners(s.devices), 0]:
        out_refs[k][...] = dot(table_ref[partner(me, k)], data)


def back_kernel(s, which, started, ended, *refs):
    in_refs, refs = refs[: len(which)], refs[len(which) :]
    table_ref, out_ref = refs[-2:]
    me = lax.axis_index("plane")
    total = refs[0][...] if started else None
    for i, k in enumerate(which):
        high, low = split(in_refs[i][...])
        table = table_ref[partner(me, k)]
        table = jnp.concatenate([table, table[:, : 2 * s.batch]], 1)
        term = dot(table, jnp.concatenate([high, high, low], 0))
        total = term if total is None else total + term
    if ended:
        total = jnp.where(live_of(s, refs[-3], me), total[: 4 * s.span], 0.0)
        out_ref[0] = total.reshape(s.span, 4, s.sticks)
    else:
        out_ref[...] = total


def places(s, sticks_ref, sources, x_ref, y_ref):
    at = 0
    for source in sources:
        columns = pl.ds(pl.multiple_of(source * s.sticks, s.sticks), s.sticks)
        shape = (s.rows_y, s.sticks)
        x_ref[:, at : at + s.sticks] = jnp.broadcast_to(sticks_ref[0:1, columns].astype(f32), shape).astype(bf16)
        row = lax.broadcasted_iota(jnp.int32, shape, 0) + 1 - s.radius
        hit = sticks_ref[1:2, columns] == row
        y_ref[:, at : at + s.sticks] = jnp.where(hit, 1.0, 0.0).astype(bf16)
        at += s.sticks


def one_hot(x, x_all, y_all):
    return jnp.where(x_all == jnp.asarray(x, bf16), y_all, jnp.zeros_like(y_all))


def lay_kernel(s, which, started, ended, *refs):
    in_refs, refs = refs[: len(which)], refs[len(which) :]
    before_ref, refs = (refs[0], refs[1:]) if started else (None, refs)
    sticks_ref, refs = refs[0], refs[1:]
    table_ref, out_ref, grid_ref = refs[:3] if ended else (None, None, refs[0])
    x_ref, y_ref, both_ref = refs[-3:]
    me = lax.axis_index("plane")
    places(s, sticks_ref, [partner(me, k) for k in which], x_ref, y_ref)
    rows = 2 * s.batch
    for i in range(len(which)):
        high, low = split(in_refs[i][...])
        both_ref[:rows, i * s.sticks : (i + 1) * s.sticks] = high
        both_ref[rows:, i * s.sticks : (i + 1) * s.sticks] = low
    lanes = 2 * s.rows_y
    for first in range(0, s.tiles, 2):
        count = min(2, s.tiles - first)
        hot = jnp.concatenate([one_hot(x, x_ref[...], y_ref[...]) for x in range(2 * first, 2 * (first + count))], 0)
        laid = lax.dot_general(both_ref[...], hot, (((1,), (1,)), ((), ())), preferred_element_type=f32)
        laid = laid[:rows] + laid[rows:]
        for t in range(count):
            for component in range(2):
                own = pl.ds((first + t) * s.batch, s.batch), slice(component * lanes, (component + 1) * lanes)
                part = laid[component * s.batch : (component + 1) * s.batch, t * lanes : (t + 1) * lanes]
                grid_ref[own] = part + before_ref[own] if started else part
    if not ended:
        return
    total = s.tiles * s.batch
    table = jnp.concatenate([table_ref[0], table_ref[0], table_ref[1]], 0)
    for start in range(0, total, 4 * s.batch):
        end = min(total, start + 4 * s.batch)
        high, low = split(grid_ref[start:end, :])
        moved = dot(jnp.concatenate([high, low, high], 1), table)
        for t in range(4):
            for row in range(0, end - start, s.batch):
                at = (start + row) // s.batch * s.step
                out_ref[t, at : at + s.batch, :] = moved[row : row + s.batch, t * s.length : (t + 1) * s.length]
    for t in range(4):
        out_ref[t, s.tiles * s.step :, :] = jnp.zeros(((s.even - s.tiles) * s.step, s.length), f32)


def space_kernel(s, bands, half_ref, *refs):
    offsets = ring_offsets(bands)[:-2]
    slab_refs, (x_ahead_ref, x_back_ref, turned_ref, real_ref, field_ref) = refs[: len(offsets)], refs[len(offsets) :]
    width = s.length // bands
    band = lax.axis_index("band")
    at = place_on_ring(band, bands)
    for (offset, _, _), slab_ref in zip(offsets, slab_refs, strict=True):
        owner = band_on_ring(lax.rem(at + offset + bands, bands), bands)
        field_ref[:, pl.ds(pl.multiple_of(owner * width, width), width), :] = slab_ref[...]
    last = pl.ds(pl.multiple_of(last_owner(bands) * width, width), width)
    field_ref[:, last, :] = jnp.zeros((s.planes, width, s.length), f32)
    for t in range(2, 4):
        turned_ref[t, s.odd * s.step :, :] = jnp.zeros(((s.even - s.odd) * s.step, s.length), f32)
    table = jnp.concatenate([x_ahead_ref[...], x_ahead_ref[last, :]], 0)

    def plane(z, carry):
        parts = []
        for component in range(2):
            for parity in range(2):
                count = s.odd if parity else s.even
                parts.append(
                    jnp.concatenate(
                        [
                            half_ref[2 * parity + component, pl.ds(o * s.planes + z, count, stride=s.step), :]
                            for o in range(2)
                        ],
                        1,
                    )
                )
        high, low = split(jnp.concatenate(parts, 0))
        real = dot(table, jnp.concatenate([high, high, low], 0))
        real_ref[z] = real[s.length :]
        field = field_ref[z]
        high, low = split(real[: s.length] * jnp.concatenate([field, field], 1))
        turned = dot(x_back_ref[...], jnp.concatenate([high, low], 0))
        keep_turned(s, turned_ref, z, turned[: s.kept] + turned[s.kept :])
        return carry

    lax.fori_loop(0, s.planes, plane, 0, unroll=4)


def keep_turned(s, turned_ref, z, turned):
    at = 0
    for component in range(2):
        for parity in range(2):
            count = s.odd if parity else s.even
            for o in range(2):
                turned_ref[2 * parity + component, pl.ds(o * s.planes + z, count, stride=s.step), :] = turned[
                    at : at + count, o * s.length : (o + 1) * s.length
                ]
            at += count


def finish_kernel(s, bands, first_ref, real_ref, up_ref, down_ref, x_last_ref, y_back_ref, flat_ref, turned_ref):
    total = s.tiles * s.batch
    for t in range(2, 4):
        turned_ref[t, s.odd * s.step :, :] = jnp.zeros(((s.even - s.odd) * s.step, s.length), f32)
    x_last = x_last_ref[last_owner(bands)]
    part = s.planes // 2
    for slab_ref, start in ((up_ref, 0), (down_ref, part)):

        def plane(z, carry, slab_ref=slab_ref, start=start):
            field = slab_ref[z]
            high, low = split(real_ref[start + z] * jnp.concatenate([field, field], 1))
            keep_turned(s, turned_ref, start + z, dot(x_last, jnp.concatenate([high, low, high], 0)))
            return carry

        lax.fori_loop(0, part, plane, 0, unroll=4)

    rows = 2 * s.batch
    lanes = 2 * s.rows_y
    table = jnp.concatenate([y_back_ref[0], y_back_ref[0], y_back_ref[1]], 0)
    for start in range(0, total, 4 * s.batch):
        end = min(total, start + 4 * s.batch)
        parts = []
        for row in range(start // s.batch * s.step, end // s.batch * s.step, s.step):
            own = slice(row, row + s.batch)
            parts.append(jnp.concatenate([first_ref[t, own, :] + turned_ref[t, own, :] for t in range(4)], 1))
        high, low = split(jnp.concatenate(parts, 0))
        moved = dot(jnp.concatenate([high, low, high], 1), table)
        high, low = split(moved)
        for t in range((end - start) // s.batch):
            column = (start // s.batch + t) * lanes
            for component in range(2):
                row = component * s.batch
                mine = slice(t * s.batch, (t + 1) * s.batch), slice(component * lanes, (component + 1) * lanes)
                flat_ref[row : row + s.batch, column : column + lanes] = high[mine]
                flat_ref[rows + row : rows + row + s.batch, column : column + lanes] = low[mine]


def pick_kernel(s, which, flat_ref, sticks_ref, *refs):
    out_refs, (x_ref, y_ref, hot_ref) = refs[: len(which)], refs[len(which) :]
    me = lax.axis_index("plane")
    places(s, sticks_ref, [partner(me, k) for k in which], x_ref, y_ref)
    rows = 2 * s.batch
    for i in range(len(which)):
        columns = slice(i * s.sticks, (i + 1) * s.sticks)
        for x in range(2 * s.tiles):
            hot_ref[x * s.rows_y : (x + 1) * s.rows_y, :] = one_hot(x, x_ref[:, columns], y_ref[:, columns])
        found = dot(flat_ref[...], hot_ref[...])
        out_refs[i][...] = found[:rows] + found[rows:]


def band_on_ring(place, count):
    return jnp.where(2 * place < count, 2 * place, 2 * (count - 1 - place) + 1)


def place_on_ring(band, count):
    return jnp.where(lax.rem(band, 2) == 0, band // 2, count - 1 - band // 2)


def last_owner(count):
    return band_on_ring(lax.rem(place_on_ring(lax.axis_index("band"), count) + count // 2, count), count)


def ring_offsets(count):
    offsets = [(0, 0, 2)]
    for step in range(1, count // 2 + 1):
        last = 2 * step == count
        offsets += [(-step, 0, 1 if last else 2), (step, 1 if last else 0, 2)]
    return offsets


def partners(devices):
    return sorted(range(1, devices), key=lambda k: (k == 1, k % 2, k))


def stages(devices):
    far = partners(devices)[:-1]
    return [("lay1", [0, 1]), ("lay2", far[:-1]), ("lay3", far[-1:])]


def per_device(bands, coeffs, potential, stick_map):
    devices = stick_map.shape[1] // coeffs.shape[3]
    s = Sizes(coeffs.shape[2], coeffs.shape[3], potential.shape[2], potential.shape[0], devices)
    tab = {name: jnp.asarray(value) for name, value in tables(s, bands).items()}
    rows = 2 * s.batch
    block = jax.ShapeDtypeStruct((rows, s.sticks), f32)

    order = list(range(0, bands, 2)) + list(range(bands - 1, 0, -2))
    along = [(order[i], order[(i + 1) % bands]) for i in range(bands)]
    against = [(b, a) for a, b in along]

    def exchange(blocks):
        out = [blocks[0]] + [None] * (devices - 1)
        for k in partners(devices):
            out[k] = lax.ppermute(blocks[k], "plane", [(i, i ^ k) for i in range(devices)])
        return out

    def ring():
        slabs = [potential]
        up = down = potential
        for step in range(1, bands // 2 + 1):
            last = 2 * step == bands
            if last:
                up, down = up[: s.planes // 2], down[s.planes // 2 :]
            up = lax.ppermute(up, "band", along)
            down = lax.ppermute(down, "band", against)
            slabs += [up, down]
        return slabs

    def kernel(body, inputs, out_shape, limit, flops, scratch_shapes=(), place=VMEM):
        return pl.pallas_call(
            body,
            in_specs=[place] * len(inputs),
            out_specs=jax.tree.map(lambda _: VMEM, out_shape),
            out_shape=out_shape,
            scratch_shapes=scratch_shapes,
            compiler_params=pltpu.CompilerParams(vmem_limit_bytes=limit << 10),
            cost_estimate=pl.CostEstimate(flops=flops, bytes_accessed=1 << 20, transcendentals=0),
        )(*inputs)

    slabs = ring()
    positions = 2 * s.tiles * s.rows_y
    results = []
    for pair in range(coeffs.shape[0]):
        given = jnp.transpose(coeffs[pair : pair + 1], (0, 2, 1, 3))
        sent = kernel(
            functools.partial(ahead_kernel, s),
            [pltpu.with_memory_space_constraint(a, pltpu.HBM) for a in (given, stick_map, tab["z_ahead"])],
            [block] * devices,
            16 << 10,
            1 << 31,
            [
                pltpu.VMEM(given.shape, f32),
                pltpu.VMEM(stick_map.shape, jnp.int32),
                pltpu.VMEM(tab["z_ahead"].shape, bf16),
                pltpu.SemaphoreType.DMA((3,)),
            ],
            HBM,
        )
        held = exchange(sent)
        half = None
        grid_shape = (s.tiles * s.batch, 4 * s.rows_y)
        for name, which in stages(devices):
            started, ended = half is not None, name == "lay3"
            shape = (4, s.even * s.step, s.length) if ended else grid_shape
            own = [pltpu.VMEM((s.rows_y, len(which) * s.sticks), bf16)] * 2
            own.append(pltpu.VMEM((2 * rows, len(which) * s.sticks), bf16))
            half = kernel(
                functools.partial(lay_kernel, s, which, started, ended),
                [held[k] for k in which] + [half] * started + [stick_map] + [tab["y_ahead"]] * ended,
                jax.ShapeDtypeStruct(shape, f32),
                24 << 10,
                1 << 31,
                [pltpu.VMEM(grid_shape, f32)] * ended + own,
            )
        turned_shape = (4, s.even * s.step, s.length)
        turned, real = kernel(
            functools.partial(space_kernel, s, bands),
            [half, *slabs[:-2], tab["x_ahead"], tab["x_back"]],
            [
                jax.ShapeDtypeStruct(turned_shape, f32),
                jax.ShapeDtypeStruct((s.planes, s.length // bands, 2 * s.length), f32),
            ],
            16 << 10,
            1 << 32,
            [pltpu.VMEM((s.planes, s.length, s.length), f32)],
        )
        flat = kernel(
            functools.partial(finish_kernel, s, bands),
            [turned, real, *slabs[-2:], tab["x_last"], tab["y_back"]],
            jax.ShapeDtypeStruct((2 * rows, positions), bf16),
            24 << 10,
            1 << 32,
            [pltpu.VMEM(turned_shape, f32)],
        )
        mixed = [None] * devices
        groups = [[k] for k in partners(devices)[:-1]] + [[1, 0]]
        for which in groups:
            parts = kernel(
                functools.partial(pick_kernel, s, which),
                [flat, stick_map],
                [block] * len(which),
                16 << 10,
                1 << 31,
                [
                    pltpu.VMEM((s.rows_y, len(which) * s.sticks), bf16),
                    pltpu.VMEM((s.rows_y, len(which) * s.sticks), bf16),
                    pltpu.VMEM((positions, s.sticks), bf16),
                ],
            )
            for k, part in zip(which, parts, strict=True):
                mixed[k] = part
        returned = exchange(mixed)
        late = partners(devices)[-2]
        early = [k for k in range(devices) if k != late]
        begun = kernel(
            functools.partial(back_kernel, s, early, False, False),
            [*(returned[k] for k in early), tab["z_back"]],
            jax.ShapeDtypeStruct((s.depth_rows, s.sticks), f32),
            16 << 10,
            1 << 31,
        )
        result = kernel(
            functools.partial(back_kernel, s, [late], True, True),
            [returned[late], begun, stick_map, tab["z_back"]],
            jax.ShapeDtypeStruct((1,) + given.shape[1:], f32),
            16 << 10,
            1 << 31,
        )
        results.append(jnp.transpose(result, (0, 2, 1, 3)))
    return results[0] if len(results) == 1 else jnp.concatenate(results, 0)


def solution(mesh):
    placed = (P("band", None, None, "plane"), P("plane", "band", None), P())
    return jax.shard_map(
        functools.partial(per_device, mesh.shape["band"]),
        mesh=mesh,
        in_specs=placed,
        out_specs=P("band", None, None, "plane"),
        check_vma=False,
    )
```

```python
import functools
import math

import jax
import jax.numpy as jnp
import ml_dtypes
import numpy as np
from jax import lax
from jax.experimental import pallas as pl
from jax.experimental.pallas import tpu as pltpu
from jax.sharding import PartitionSpec as P


bf16 = jnp.bfloat16
f32 = jnp.float32
VMEM = pl.BlockSpec(memory_space=pltpu.VMEM)
HBM = pl.BlockSpec(memory_space=pltpu.HBM)


def up8(n):
    return -(-n // 8) * 8


def halves(table):
    high = table.astype(ml_dtypes.bfloat16)
    return high, (table - high.astype(np.float64)).astype(ml_dtypes.bfloat16)


def split(value):
    high = value.astype(bf16)
    return high, (value - high.astype(f32)).astype(bf16)


class Sizes:
    def __init__(self, span, sticks, length, planes, devices):
        self.span, self.length, self.planes, self.devices = span, length, planes, devices
        self.sticks = sticks
        self.radius = (span - 1) // 2
        self.rows_y = 2 * self.radius
        self.tiles = self.radius // 2 + 1
        self.even = up8(self.tiles)
        self.odd = up8(self.radius // 2)
        self.kept = 2 * (self.even + self.odd)
        self.batch = 2 * planes
        self.step = self.batch + 1
        self.depth_rows = -(-4 * span // 16) * 16


def tables(s, bands):
    turn = 2.0 * math.pi / s.length
    grid = np.arange(s.length)
    depth = np.arange(s.span) - s.radius
    y = np.arange(s.rows_y) + 1 - s.radius

    def trig(left, right):
        angle = turn * np.mod(np.outer(left, right), s.length)
        return np.cos(angle), np.sin(angle)

    cos, sin = trig(depth, grid)
    ahead = np.zeros((s.devices, 2, 2, s.planes, s.span, 2, 2))
    back = np.zeros((s.devices, s.span, 2, 2, 2, 2, s.planes))
    scale = 1.0 / float(s.length) ** 3
    for d in range(s.devices):
        own = slice(d * s.planes, (d + 1) * s.planes)
        c, n = cos[:, own], sin[:, own]
        for o in range(2):
            ahead[d, 0, o, :, :, o, 0] = c.T
            ahead[d, 0, o, :, :, o, 1] = -n.T
            ahead[d, 1, o, :, :, o, 0] = n.T
            ahead[d, 1, o, :, :, o, 1] = c.T
            back[d, :, o, 0, 0, o] = c * scale
            back[d, :, o, 0, 1, o] = n * scale
            back[d, :, o, 1, 0, o] = -n * scale
            back[d, :, o, 1, 1, o] = c * scale
    gap = s.depth_rows - 4 * s.span
    ahead = np.pad(ahead.reshape(s.devices, 2 * s.batch, 4 * s.span), ((0, 0), (0, 0), (0, gap)))
    back = back.reshape(s.devices, 4 * s.span, 4, 2, s.planes // 2).transpose(0, 1, 3, 2, 4)
    back = np.pad(back.reshape(s.devices, 4 * s.span, 2 * s.batch), ((0, 0), (0, gap), (0, 0)))

    cos, sin = trig(y, grid)
    y_ahead = np.zeros((2, 2, s.rows_y, 2, 2, s.length))
    y_back = np.zeros((2, 2, s.length, 2, 2, s.rows_y))
    for parity in range(2):
        y_ahead[0, parity, :, parity, 0] = cos
        y_ahead[1, parity, :, parity, 0] = -sin
        y_ahead[0, parity, :, parity, 1] = sin
        y_ahead[1, parity, :, parity, 1] = cos
        y_back[parity, 0, :, 0, parity] = cos.T
        y_back[parity, 1, :, 0, parity] = sin.T
        y_back[parity, 0, :, 1, parity] = -sin.T
        y_back[parity, 1, :, 1, parity] = cos.T
    y_ahead = y_ahead.reshape(4 * s.rows_y, 4 * s.length)
    y_back = y_back.reshape(4 * s.length, 4 * s.rows_y)

    x_ahead = np.zeros((s.length, s.kept))
    x_back = np.zeros((s.kept, s.length))
    at = 0
    for component in range(2):
        for parity in range(2):
            count = s.tiles if parity == 0 else s.radius // 2
            cos, sin = trig(2 * np.arange(count) + parity, grid)
            x_ahead[:, at : at + count] = 2.0 * cos.T if component == 0 else -2.0 * sin.T
            x_back[at : at + count] = cos if component == 0 else -sin
            at += s.even if parity == 0 else s.odd

    def beside(table, axis, order):
        parts = halves(table)
        return np.concatenate([parts[i] for i in order], axis)

    zero = np.zeros(x_back.shape, ml_dtypes.bfloat16)
    high, low = halves(x_back)
    by_slab = x_back.reshape(s.kept, bands, s.length // bands).transpose(1, 0, 2)
    return dict(
        z_ahead=beside(ahead, 2, (0, 1, 0)),
        z_back=beside(back, 2, (0, 1)),
        y_ahead=np.stack(halves(y_ahead)),
        y_back=np.stack(halves(y_back)),
        x_ahead=beside(x_ahead, 1, (0, 1, 0)),
        x_last=beside(by_slab, 2, (0, 0, 1)),
        x_back=np.concatenate([np.concatenate([high, high], 1), np.concatenate([low, zero], 1)], 0),
    )


def dot(left, right):
    return jnp.dot(left, right, preferred_element_type=f32)


def partner(me, k):
    return jnp.bitwise_xor(me, k)


def live_of(s, sticks_ref, source):
    columns = pl.ds(pl.multiple_of(source * s.sticks, s.sticks), s.sticks)
    depth = lax.broadcasted_iota(jnp.int32, (4 * s.span, s.sticks), 0) // 4 - s.radius
    return jnp.abs(depth) <= sticks_ref[2:3, columns]


def ahead_kernel(s, coeffs_hbm, sticks_hbm, table_hbm, *refs):
    out_refs, (coeffs_ref, sticks_ref, table_ref, sems) = refs[: s.devices], refs[s.devices :]
    pairs = [(sticks_hbm, sticks_ref), (coeffs_hbm, coeffs_ref), (table_hbm, table_ref)]
    copies = [pltpu.make_async_copy(source, target, sems.at[i]) for i, (source, target) in enumerate(pairs)]
    for copy in copies:
        copy.start()
    me = lax.axis_index("plane")
    copies[0].wait()
    live = live_of(s, sticks_ref, me)
    copies[1].wait()
    data = jnp.where(live, coeffs_ref[0].reshape(4 * s.span, s.sticks), 0.0)
    gap = jnp.zeros((s.depth_rows - 4 * s.span, s.sticks), f32)
    high, low = split(jnp.concatenate([data, gap], 0))
    data = jnp.concatenate([high, high, low], 0)
    copies[2].wait()
    for k in [*partners(s.devices), 0]:
        out_refs[k][...] = dot(table_ref[partner(me, k)], data)


def back_kernel(s, which, started, ended, *refs):
    in_refs, refs = refs[: sum(which.values())], refs[sum(which.values()) :]
    table_ref, out_ref = refs[-2:]
    me = lax.axis_index("plane")
    total = refs[0][...] if started else None
    at = 0
    for k, count in which.items():
        high, low = split(jnp.concatenate([ref[...] for ref in in_refs[at : at + count]], 0))
        at += count
        table = table_ref[partner(me, k)]
        table = jnp.concatenate([table, table[:, : 2 * s.batch]], 1)
        term = dot(table, jnp.concatenate([high, high, low], 0))
        total = term if total is None else total + term
    if ended:
        total = jnp.where(live_of(s, refs[-3], me), total[: 4 * s.span], 0.0)
        out_ref[0] = total.reshape(s.span, 4, s.sticks)
    else:
        out_ref[...] = total


def fetching_kernel(body, inputs, outs, count, *refs):
    sources, targets = refs[inputs : inputs + count], refs[inputs + count + outs : inputs + 2 * count + outs]
    copies = [pltpu.make_async_copy(sources[i], targets[i], refs[-1].at[i]) for i in range(count)]
    for copy in copies:
        copy.start()
    body(*refs[:inputs], *refs[inputs + count : inputs + count + outs], *refs[inputs + 2 * count + outs : -1])
    for copy in copies:
        copy.wait()


def places(s, sticks_ref, sources, x_ref, y_ref):
    at = 0
    for source in sources:
        columns = pl.ds(pl.multiple_of(source * s.sticks, s.sticks), s.sticks)
        shape = (s.rows_y, s.sticks)
        x_ref[:, at : at + s.sticks] = jnp.broadcast_to(sticks_ref[0:1, columns].astype(f32), shape).astype(bf16)
        row = lax.broadcasted_iota(jnp.int32, shape, 0) + 1 - s.radius
        hit = sticks_ref[1:2, columns] == row
        y_ref[:, at : at + s.sticks] = jnp.where(hit, 1.0, 0.0).astype(bf16)
        at += s.sticks


def one_hot(x, x_all, y_all):
    return jnp.where(x_all == jnp.asarray(x, bf16), y_all, jnp.zeros_like(y_all))


def lay_kernel(s, which, started, ended, *refs):
    in_refs, refs = refs[: len(which)], refs[len(which) :]
    before_ref, refs = (refs[0], refs[1:]) if started else (None, refs)
    sticks_ref, refs = refs[0], refs[1:]
    table_ref, out_ref, grid_ref = refs[:3] if ended else (None, None, refs[0])
    x_ref, y_ref, both_ref = refs[-3:]
    me = lax.axis_index("plane")
    places(s, sticks_ref, [partner(me, k) for k in which], x_ref, y_ref)
    rows = 2 * s.batch
    for i in range(len(which)):
        high, low = split(in_refs[i][...])
        both_ref[:rows, i * s.sticks : (i + 1) * s.sticks] = high
        both_ref[rows:, i * s.sticks : (i + 1) * s.sticks] = low
    lanes = 2 * s.rows_y
    for first in range(0, s.tiles, 2):
        count = min(2, s.tiles - first)
        hot = jnp.concatenate([one_hot(x, x_ref[...], y_ref[...]) for x in range(2 * first, 2 * (first + count))], 0)
        laid = lax.dot_general(both_ref[...], hot, (((1,), (1,)), ((), ())), preferred_element_type=f32)
        laid = laid[:rows] + laid[rows:]
        for t in range(count):
            for component in range(2):
                own = pl.ds((first + t) * s.batch, s.batch), slice(component * lanes, (component + 1) * lanes)
                part = laid[component * s.batch : (component + 1) * s.batch, t * lanes : (t + 1) * lanes]
                grid_ref[own] = part + before_ref[own] if started else part
    if not ended:
        return
    total = s.tiles * s.batch
    table = jnp.concatenate([table_ref[0], table_ref[0], table_ref[1]], 0)
    for start in range(0, total, 4 * s.batch):
        end = min(total, start + 4 * s.batch)
        high, low = split(grid_ref[start:end, :])
        moved = dot(jnp.concatenate([high, low, high], 1), table)
        for t in range(4):
            for row in range(0, end - start, s.batch):
                at = (start + row) // s.batch * s.step
                out_ref[t, at : at + s.batch, :] = moved[row : row + s.batch, t * s.length : (t + 1) * s.length]
    for t in range(4):
        out_ref[t, s.tiles * s.step :, :] = jnp.zeros(((s.even - s.tiles) * s.step, s.length), f32)


def turn_kernel(s, bands, half_ref, x_ahead_ref, real_ref):
    width = s.length // bands
    last = pl.ds(pl.multiple_of(last_owner(bands) * width, width), width)
    table = jnp.concatenate([x_ahead_ref[...], x_ahead_ref[last, :]], 0)

    def plane(z, carry):
        parts = []
        for component in range(2):
            for parity in range(2):
                count = s.odd if parity else s.even
                parts.append(
                    jnp.concatenate(
                        [
                            half_ref[2 * parity + component, pl.ds(o * s.planes + z, count, stride=s.step), :]
                            for o in range(2)
                        ],
                        1,
                    )
                )
        high, low = split(jnp.concatenate(parts, 0))
        real_ref[z] = dot(table, jnp.concatenate([high, high, low], 0))
        return carry

    lax.fori_loop(0, s.planes, plane, 0, unroll=4)


def space_kernel(s, bands, real_ref, *refs):
    offsets = ring_offsets(bands)[:-2]
    slab_refs, (x_back_ref, turned_ref, field_ref) = refs[: len(offsets)], refs[len(offsets) :]
    width = s.length // bands
    band = lax.axis_index("band")
    at = place_on_ring(band, bands)
    for (offset, _, _), slab_ref in zip(offsets, slab_refs, strict=True):
        owner = band_on_ring(lax.rem(at + offset + bands, bands), bands)
        field_ref[:, pl.ds(pl.multiple_of(owner * width, width), width), :] = slab_ref[...]
    last = pl.ds(pl.multiple_of(last_owner(bands) * width, width), width)
    field_ref[:, last, :] = jnp.zeros((s.planes, width, s.length), f32)
    for t in range(2, 4):
        turned_ref[t, s.odd * s.step :, :] = jnp.zeros(((s.even - s.odd) * s.step, s.length), f32)

    def plane(z, carry):
        field = field_ref[z]
        high, low = split(real_ref[z, : s.length, :] * jnp.concatenate([field, field], 1))
        turned = dot(x_back_ref[...], jnp.concatenate([high, low], 0))
        keep_turned(s, turned_ref, z, turned[: s.kept] + turned[s.kept :])
        return carry

    lax.fori_loop(0, s.planes, plane, 0, unroll=4)


def keep_turned(s, turned_ref, z, turned):
    at = 0
    for component in range(2):
        for parity in range(2):
            count = s.odd if parity else s.even
            for o in range(2):
                turned_ref[2 * parity + component, pl.ds(o * s.planes + z, count, stride=s.step), :] = turned[
                    at : at + count, o * s.length : (o + 1) * s.length
                ]
            at += count


def finish_kernel(s, bands, half, first_ref, real_ref, slab_ref, x_last_ref, y_back_ref, flat_ref, turned_ref):
    for t in range(2, 4):
        turned_ref[t, s.odd * s.step :, :] = jnp.zeros(((s.even - s.odd) * s.step, s.length), f32)
    x_last = x_last_ref[last_owner(bands)]
    part = s.planes // 2

    def plane(z, carry):
        field = slab_ref[z]
        high, low = split(real_ref[half * part + z, s.length :, :] * jnp.concatenate([field, field], 1))
        keep_turned(s, turned_ref, half * part + z, dot(x_last, jnp.concatenate([high, low, high], 0)))
        return carry

    lax.fori_loop(0, part, plane, 0, unroll=4)

    lanes = 2 * s.rows_y
    table = jnp.concatenate([y_back_ref[0], y_back_ref[0], y_back_ref[1]], 0)
    for start in range(0, s.tiles, 8):
        end = min(s.tiles, start + 8)
        parts = []
        for tile in range(start, end):
            for o in range(2):
                row = tile * s.step + o * s.planes + half * part
                own = slice(row, row + part)
                parts.append(jnp.concatenate([first_ref[t, own, :] + turned_ref[t, own, :] for t in range(4)], 1))
        high, low = split(jnp.concatenate(parts, 0))
        moved = dot(jnp.concatenate([high, low, high], 1), table)
        high, low = split(moved)
        for tile in range(start, end):
            at = (tile - start) * s.planes
            for component in range(2):
                mine = slice(at, at + s.planes), slice(component * lanes, (component + 1) * lanes)
                for row, value in ((component, high), (2 + component, low)):
                    flat_ref[row * s.planes : (row + 1) * s.planes, tile * lanes : (tile + 1) * lanes] = value[mine]


def pick_kernel(s, which, count, *refs):
    flat_refs, sticks_ref, refs = refs[:count], refs[count], refs[count + 1 :]
    out_refs, (x_ref, y_ref, hot_ref) = refs[: len(which)], refs[len(which) :]
    me = lax.axis_index("plane")
    places(s, sticks_ref, [partner(me, k) for k in which], x_ref, y_ref)
    rows = 2 * s.planes
    flat = jnp.concatenate([flat_ref[...] for flat_ref in flat_refs], 0)
    for i in range(len(which)):
        columns = slice(i * s.sticks, (i + 1) * s.sticks)
        for x in range(2 * s.tiles):
            hot_ref[x * s.rows_y : (x + 1) * s.rows_y, :] = one_hot(x, x_ref[:, columns], y_ref[:, columns])
        found = dot(flat, hot_ref[...])
        for h in range(count):
            row = 2 * h * rows
            out_refs[i][h * rows : (h + 1) * rows, :] = found[row : row + rows] + found[row + rows : row + 2 * rows]


def band_on_ring(place, count):
    return jnp.where(2 * place < count, 2 * place, 2 * (count - 1 - place) + 1)


def place_on_ring(band, count):
    return jnp.where(lax.rem(band, 2) == 0, band // 2, count - 1 - band // 2)


def last_owner(count):
    return band_on_ring(lax.rem(place_on_ring(lax.axis_index("band"), count) + count // 2, count), count)


def ring_offsets(count):
    offsets = [(0, 0, 2)]
    for step in range(1, count // 2 + 1):
        last = 2 * step == count
        offsets += [(-step, 0, 1 if last else 2), (step, 1 if last else 0, 2)]
    return offsets


def partners(devices):
    return sorted(range(1, devices), key=lambda k: (k == 1, k % 2, k))


def stages(devices):
    far = partners(devices)[:-1]
    return [("lay1", [0, 1]), ("lay2", far[:-1]), ("lay3", far[-1:])]


def per_device(bands, coeffs, potential, stick_map):
    devices = stick_map.shape[1] // coeffs.shape[3]
    s = Sizes(coeffs.shape[2], coeffs.shape[3], potential.shape[2], potential.shape[0], devices)
    tab = {name: jnp.asarray(value) for name, value in tables(s, bands).items()}
    rows = 2 * s.batch
    block = jax.ShapeDtypeStruct((rows, s.sticks), f32)

    order = list(range(0, bands, 2)) + list(range(bands - 1, 0, -2))
    along = [(order[i], order[(i + 1) % bands]) for i in range(bands)]
    against = [(b, a) for a, b in along]

    def exchange(blocks):
        out = [blocks[0]] + [None] * (devices - 1)
        for k in partners(devices):
            out[k] = lax.ppermute(blocks[k], "plane", [(i, i ^ k) for i in range(devices)])
        return out

    def ring():
        slabs = [potential]
        up = down = potential
        for step in range(1, bands // 2 + 1):
            last = 2 * step == bands
            if last:
                up, down = up[: s.planes // 2], down[s.planes // 2 :]
            up = lax.ppermute(up, "band", along)
            down = lax.ppermute(down, "band", against)
            slabs += [up, down]
        return slabs

    def kernel(body, inputs, out_shape, limit, flops, scratch_shapes=(), place=VMEM, fetched=()):
        single = not isinstance(out_shape, list)
        outs = [out_shape] if single else out_shape
        extra = [jax.ShapeDtypeStruct(a.shape, a.dtype) for a in fetched]
        if fetched:
            body = functools.partial(fetching_kernel, body, len(inputs), len(outs), len(fetched))
        results = pl.pallas_call(
            body,
            in_specs=[place] * len(inputs) + [HBM] * len(fetched),
            out_specs=[VMEM] * (len(outs) + len(fetched)),
            out_shape=outs + extra,
            scratch_shapes=[*scratch_shapes] + [pltpu.SemaphoreType.DMA((len(fetched),))] * bool(fetched),
            compiler_params=pltpu.CompilerParams(vmem_limit_bytes=limit << 10),
            cost_estimate=pl.CostEstimate(flops=flops, bytes_accessed=1 << 20, transcendentals=0),
        )(*inputs, *(pltpu.with_memory_space_constraint(a, pltpu.HBM) for a in fetched))
        if fetched:
            return results[: len(outs)], results[len(outs) :]
        return results[0] if single else results

    slabs = ring()
    positions = 2 * s.tiles * s.rows_y
    results = []
    for pair in range(coeffs.shape[0]):
        given = jnp.transpose(coeffs[pair : pair + 1], (0, 2, 1, 3))
        sent = kernel(
            functools.partial(ahead_kernel, s),
            [pltpu.with_memory_space_constraint(a, pltpu.HBM) for a in (given, stick_map, tab["z_ahead"])],
            [block] * devices,
            16 << 10,
            1 << 31,
            [
                pltpu.VMEM(given.shape, f32),
                pltpu.VMEM(stick_map.shape, jnp.int32),
                pltpu.VMEM(tab["z_ahead"].shape, bf16),
                pltpu.SemaphoreType.DMA((3,)),
            ],
            HBM,
        )
        held = exchange(sent)
        half = None
        ready = results
        later = ["y_ahead", "x_ahead", "x_back", "x_last", "y_back", "z_back"]
        grid_shape = (s.tiles * s.batch, 4 * s.rows_y)
        for name, which in stages(devices):
            started, ended = half is not None, name == "lay3"
            shape = (4, s.even * s.step, s.length) if ended else grid_shape
            own = [pltpu.VMEM((s.rows_y, len(which) * s.sticks), bf16)] * 2
            own.append(pltpu.VMEM((2 * rows, len(which) * s.sticks), bf16))
            fetch = [] if started or ready else [tab[key] for key in later] + [potential]
            half = kernel(
                functools.partial(lay_kernel, s, which, started, ended),
                [held[k] for k in which] + [half] * started + [stick_map] + [tab["y_ahead"]] * ended,
                jax.ShapeDtypeStruct(shape, f32),
                24 << 10,
                1 << 31,
                [pltpu.VMEM(grid_shape, f32)] * ended + own,
                fetched=fetch,
            )
            if fetch:
                (half,), (*ready, slabs[0]) = half
                tab.update(zip(later, ready, strict=True))
        turned_shape = (4, s.even * s.step, s.length)
        real = kernel(
            functools.partial(turn_kernel, s, bands),
            [half, tab["x_ahead"]],
            jax.ShapeDtypeStruct((s.planes, s.length + s.length // bands, 2 * s.length), f32),
            16 << 10,
            1 << 31,
        )
        turned = kernel(
            functools.partial(space_kernel, s, bands),
            [real, *slabs[:-2], tab["x_back"]],
            jax.ShapeDtypeStruct(turned_shape, f32),
            16 << 10,
            1 << 31,
            [pltpu.VMEM((s.planes, s.length, s.length), f32)],
        )
        flats = [
            kernel(
                functools.partial(finish_kernel, s, bands, half),
                [turned, real, slabs[half - 2], tab["x_last"], tab["y_back"]],
                jax.ShapeDtypeStruct((4 * s.planes, positions), bf16),
                20 << 10,
                1 << 31,
                [pltpu.VMEM(turned_shape, f32)],
            )
            for half in range(2)
        ]

        def pick(which, flats):
            return kernel(
                functools.partial(pick_kernel, s, which, len(flats)),
                [*flats, stick_map],
                [jax.ShapeDtypeStruct((len(flats) * 2 * s.planes, s.sticks), f32)] * len(which),
                16 << 10,
                1 << 31,
                [
                    pltpu.VMEM((s.rows_y, len(which) * s.sticks), bf16),
                    pltpu.VMEM((s.rows_y, len(which) * s.sticks), bf16),
                    pltpu.VMEM((positions, s.sticks), bf16),
                ],
            )

        def send(k, block):
            return lax.ppermute(block, "plane", [(i, i ^ k) for i in range(devices)])

        soon, *far, near = partners(devices)
        returned = {soon: [send(soon, *pick([soon], [flats[h]])) for h in range(2)]}
        for k in far:
            returned[k] = [send(k, *pick([k], flats))]
        beside, own = pick([near, 0], flats)
        returned |= {near: [send(near, beside)], 0: [own]}
        late = far[-1]
        counts = {k: len(blocks) for k, blocks in returned.items() if k != late}
        begun = kernel(
            functools.partial(back_kernel, s, counts, False, False),
            [*(block for k in counts for block in returned[k]), tab["z_back"]],
            jax.ShapeDtypeStruct((s.depth_rows, s.sticks), f32),
            16 << 10,
            1 << 31,
        )
        result = kernel(
            functools.partial(back_kernel, s, {late: 1}, True, True),
            [*returned[late], begun, stick_map, tab["z_back"]],
            jax.ShapeDtypeStruct((1,) + given.shape[1:], f32),
            16 << 10,
            1 << 31,
        )
        results.append(jnp.transpose(result, (0, 2, 1, 3)))
    return results[0] if len(results) == 1 else jnp.concatenate(results, 0)


def solution(mesh):
    placed = (P("band", None, None, "plane"), P("plane", "band", None), P())
    return jax.shard_map(
        functools.partial(per_device, mesh.shape["band"]),
        mesh=mesh,
        in_specs=placed,
        out_specs=P("band", None, None, "plane"),
        check_vma=False,
    )
```

```python
import functools
import math

import jax
import jax.numpy as jnp
import ml_dtypes
import numpy as np
from jax import lax
from jax.experimental import pallas as pl
from jax.experimental.pallas import tpu as pltpu
from jax.sharding import PartitionSpec as P


bf16 = jnp.bfloat16
f32 = jnp.float32
VMEM = pl.BlockSpec(memory_space=pltpu.VMEM)
HBM = pl.BlockSpec(memory_space=pltpu.HBM)


def up8(n):
    return -(-n // 8) * 8


def halves(table):
    high = table.astype(ml_dtypes.bfloat16)
    return high, (table - high.astype(np.float64)).astype(ml_dtypes.bfloat16)


def split(value):
    high = value.astype(bf16)
    return high, (value - high.astype(f32)).astype(bf16)


class Sizes:
    def __init__(self, span, sticks, length, planes, devices):
        self.span, self.length, self.planes, self.devices = span, length, planes, devices
        self.sticks = sticks
        self.radius = (span - 1) // 2
        self.rows_y = 2 * self.radius
        self.tiles = self.radius // 2 + 1
        self.even = up8(self.tiles)
        self.odd = up8(self.radius // 2)
        self.kept = 2 * (self.even + self.odd)
        self.batch = 2 * planes
        self.step = self.batch + 1
        self.depth_rows = -(-4 * span // 16) * 16


def tables(s, bands):
    turn = 2.0 * math.pi / s.length
    grid = np.arange(s.length)
    depth = np.arange(s.span) - s.radius
    y = np.arange(s.rows_y) + 1 - s.radius

    def trig(left, right):
        angle = turn * np.mod(np.outer(left, right), s.length)
        return np.cos(angle), np.sin(angle)

    cos, sin = trig(depth, grid)
    ahead = np.zeros((s.devices, 2, 2, s.planes, s.span, 2, 2))
    back = np.zeros((s.devices, s.span, 2, 2, 2, 2, s.planes))
    scale = 1.0 / float(s.length) ** 3
    for d in range(s.devices):
        own = slice(d * s.planes, (d + 1) * s.planes)
        c, n = cos[:, own], sin[:, own]
        for o in range(2):
            ahead[d, 0, o, :, :, o, 0] = c.T
            ahead[d, 0, o, :, :, o, 1] = -n.T
            ahead[d, 1, o, :, :, o, 0] = n.T
            ahead[d, 1, o, :, :, o, 1] = c.T
            back[d, :, o, 0, 0, o] = c * scale
            back[d, :, o, 0, 1, o] = n * scale
            back[d, :, o, 1, 0, o] = -n * scale
            back[d, :, o, 1, 1, o] = c * scale
    gap = s.depth_rows - 4 * s.span
    ahead = np.pad(ahead.reshape(s.devices, 2 * s.batch, 4 * s.span), ((0, 0), (0, 0), (0, gap)))
    back = back.reshape(s.devices, 4 * s.span, 4, 2, s.planes // 2).transpose(0, 1, 3, 2, 4)
    back = np.pad(back.reshape(s.devices, 4 * s.span, 2 * s.batch), ((0, 0), (0, gap), (0, 0)))

    cos, sin = trig(y, grid)
    y_ahead = np.zeros((2, 2, s.rows_y, 2, 2, s.length))
    y_back = np.zeros((2, 2, s.length, 2, 2, s.rows_y))
    for parity in range(2):
        y_ahead[0, parity, :, parity, 0] = cos
        y_ahead[1, parity, :, parity, 0] = -sin
        y_ahead[0, parity, :, parity, 1] = sin
        y_ahead[1, parity, :, parity, 1] = cos
        y_back[parity, 0, :, 0, parity] = cos.T
        y_back[parity, 1, :, 0, parity] = sin.T
        y_back[parity, 0, :, 1, parity] = -sin.T
        y_back[parity, 1, :, 1, parity] = cos.T
    y_ahead = y_ahead.reshape(4 * s.rows_y, 4 * s.length)
    y_back = y_back.reshape(4 * s.length, 4 * s.rows_y)

    x_ahead = np.zeros((s.length, s.kept))
    x_back = np.zeros((s.kept, s.length))
    at = 0
    for component in range(2):
        for parity in range(2):
            count = s.tiles if parity == 0 else s.radius // 2
            cos, sin = trig(2 * np.arange(count) + parity, grid)
            x_ahead[:, at : at + count] = 2.0 * cos.T if component == 0 else -2.0 * sin.T
            x_back[at : at + count] = cos if component == 0 else -sin
            at += s.even if parity == 0 else s.odd

    def beside(table, axis, order):
        parts = halves(table)
        return np.concatenate([parts[i] for i in order], axis)

    zero = np.zeros(x_back.shape, ml_dtypes.bfloat16)
    high, low = halves(x_back)
    by_slab = x_back.reshape(s.kept, bands, s.length // bands).transpose(1, 0, 2)
    return dict(
        z_ahead=beside(ahead, 2, (0, 1, 0)),
        z_back=beside(back, 2, (0, 1)),
        y_ahead=np.stack(halves(y_ahead)),
        y_back=np.stack(halves(y_back)),
        x_ahead=beside(x_ahead, 1, (0, 1, 0)),
        x_last=beside(by_slab, 2, (0, 0, 1)),
        x_back=np.concatenate([np.concatenate([high, high], 1), np.concatenate([low, zero], 1)], 0),
    )


def dot(left, right):
    return jnp.dot(left, right, preferred_element_type=f32)


def partner(me, k):
    return jnp.bitwise_xor(me, k)


def live_of(s, sticks_ref, source):
    columns = pl.ds(pl.multiple_of(source * s.sticks, s.sticks), s.sticks)
    depth = lax.broadcasted_iota(jnp.int32, (4 * s.span, s.sticks), 0) // 4 - s.radius
    return jnp.abs(depth) <= sticks_ref[2:3, columns]


def ahead_kernel(s, coeffs_hbm, sticks_hbm, table_hbm, *refs):
    out_refs, (coeffs_ref, sticks_ref, table_ref, sems) = refs[: s.devices], refs[s.devices :]
    pairs = [(sticks_hbm, sticks_ref), (coeffs_hbm, coeffs_ref), (table_hbm, table_ref)]
    copies = [pltpu.make_async_copy(source, target, sems.at[i]) for i, (source, target) in enumerate(pairs)]
    for copy in copies:
        copy.start()
    me = lax.axis_index("plane")
    copies[0].wait()
    live = live_of(s, sticks_ref, me)
    copies[1].wait()
    data = jnp.where(live, coeffs_ref[0].reshape(4 * s.span, s.sticks), 0.0)
    gap = jnp.zeros((s.depth_rows - 4 * s.span, s.sticks), f32)
    high, low = split(jnp.concatenate([data, gap], 0))
    data = jnp.concatenate([high, high, low], 0)
    copies[2].wait()
    for k in [*partners(s.devices), 0]:
        out_refs[k][...] = dot(table_ref[partner(me, k)], data)


def back_kernel(s, which, started, ended, *refs):
    in_refs, refs = refs[: len(which)], refs[len(which) :]
    table_ref, out_ref = refs[-2:]
    part = jnp.zeros((s.batch, s.sticks), f32)
    me = lax.axis_index("plane")
    total = refs[0][...] if started else None
    blocks = {}
    for (k, half, row), ref in zip(which, in_refs, strict=True):
        if half is None:
            blocks[k] = ref[...]
        else:
            blocks.setdefault(k, [part, part])[half] = ref[row : row + s.batch, :]
    for k, block in blocks.items():
        high, low = split(jnp.concatenate(block, 0) if isinstance(block, list) else block)
        table = table_ref[partner(me, k)]
        table = jnp.concatenate([table, table[:, : 2 * s.batch]], 1)
        term = dot(table, jnp.concatenate([high, high, low], 0))
        total = term if total is None else total + term
    if ended:
        total = jnp.where(live_of(s, refs[-3], me), total[: 4 * s.span], 0.0)
        out_ref[0] = total.reshape(s.span, 4, s.sticks)
    else:
        out_ref[...] = total


def fetching_kernel(body, inputs, outs, count, *refs):
    sources, targets = refs[inputs : inputs + count], refs[inputs + count + outs : inputs + 2 * count + outs]
    copies = [pltpu.make_async_copy(sources[i], targets[i], refs[-1].at[i]) for i in range(count)]
    for copy in copies:
        copy.start()
    body(*refs[:inputs], *refs[inputs + count : inputs + count + outs], *refs[inputs + 2 * count + outs : -1])
    for copy in copies:
        copy.wait()


def places(s, sticks_ref, sources, x_ref, y_ref):
    at = 0
    for source in sources:
        columns = pl.ds(pl.multiple_of(source * s.sticks, s.sticks), s.sticks)
        shape = (s.rows_y, s.sticks)
        x_ref[:, at : at + s.sticks] = jnp.broadcast_to(sticks_ref[0:1, columns].astype(f32), shape).astype(bf16)
        row = lax.broadcasted_iota(jnp.int32, shape, 0) + 1 - s.radius
        hit = sticks_ref[1:2, columns] == row
        y_ref[:, at : at + s.sticks] = jnp.where(hit, 1.0, 0.0).astype(bf16)
        at += s.sticks


def one_hot(x, x_all, y_all):
    return jnp.where(x_all == jnp.asarray(x, bf16), y_all, jnp.zeros_like(y_all))


def lay_kernel(s, which, started, ended, *refs):
    in_refs, refs = refs[: len(which)], refs[len(which) :]
    before_ref, refs = (refs[0], refs[1:]) if started else (None, refs)
    sticks_ref, refs = refs[0], refs[1:]
    table_ref, out_ref, grid_ref = refs[:3] if ended else (None, None, refs[0])
    x_ref, y_ref, both_ref = refs[-3:]
    me = lax.axis_index("plane")
    places(s, sticks_ref, [partner(me, k) for k in which], x_ref, y_ref)
    rows = 2 * s.batch
    for i in range(len(which)):
        high, low = split(in_refs[i][...])
        both_ref[:rows, i * s.sticks : (i + 1) * s.sticks] = high
        both_ref[rows:, i * s.sticks : (i + 1) * s.sticks] = low
    lanes = 2 * s.rows_y
    for first in range(0, s.tiles, 2):
        count = min(2, s.tiles - first)
        hot = jnp.concatenate([one_hot(x, x_ref[...], y_ref[...]) for x in range(2 * first, 2 * (first + count))], 0)
        laid = lax.dot_general(both_ref[...], hot, (((1,), (1,)), ((), ())), preferred_element_type=f32)
        laid = laid[:rows] + laid[rows:]
        for t in range(count):
            for component in range(2):
                own = pl.ds((first + t) * s.batch, s.batch), slice(component * lanes, (component + 1) * lanes)
                part = laid[component * s.batch : (component + 1) * s.batch, t * lanes : (t + 1) * lanes]
                grid_ref[own] = part + before_ref[own] if started else part
    if not ended:
        return
    total = s.tiles * s.batch
    table = jnp.concatenate([table_ref[0], table_ref[0], table_ref[1]], 0)
    for start in range(0, total, 4 * s.batch):
        end = min(total, start + 4 * s.batch)
        high, low = split(grid_ref[start:end, :])
        moved = dot(jnp.concatenate([high, low, high], 1), table)
        for t in range(4):
            for row in range(0, end - start, s.batch):
                at = (start + row) // s.batch * s.step
                out_ref[t, at : at + s.batch, :] = moved[row : row + s.batch, t * s.length : (t + 1) * s.length]
    for t in range(4):
        out_ref[t, s.tiles * s.step :, :] = jnp.zeros(((s.even - s.tiles) * s.step, s.length), f32)


def turn_kernel(s, bands, half_ref, x_ahead_ref, real_ref):
    width = s.length // bands
    last = pl.ds(pl.multiple_of(last_owner(bands) * width, width), width)
    table = jnp.concatenate([x_ahead_ref[...], x_ahead_ref[last, :]], 0)

    def plane(z, carry):
        parts = []
        for component in range(2):
            for parity in range(2):
                count = s.odd if parity else s.even
                parts.append(
                    jnp.concatenate(
                        [
                            half_ref[2 * parity + component, pl.ds(o * s.planes + z, count, stride=s.step), :]
                            for o in range(2)
                        ],
                        1,
                    )
                )
        high, low = split(jnp.concatenate(parts, 0))
        real_ref[z] = dot(table, jnp.concatenate([high, high, low], 0))
        return carry

    lax.fori_loop(0, s.planes, plane, 0, unroll=4)


def space_kernel(s, bands, real_ref, *refs):
    offsets = ring_offsets(bands)[:-2]
    slab_refs, (x_back_ref, turned_ref, field_ref) = refs[: len(offsets)], refs[len(offsets) :]
    width = s.length // bands
    band = lax.axis_index("band")
    at = place_on_ring(band, bands)
    for (offset, _, _), slab_ref in zip(offsets, slab_refs, strict=True):
        owner = band_on_ring(lax.rem(at + offset + bands, bands), bands)
        field_ref[:, pl.ds(pl.multiple_of(owner * width, width), width), :] = slab_ref[...]
    last = pl.ds(pl.multiple_of(last_owner(bands) * width, width), width)
    field_ref[:, last, :] = jnp.zeros((s.planes, width, s.length), f32)
    for t in range(2, 4):
        turned_ref[t, s.odd * s.step :, :] = jnp.zeros(((s.even - s.odd) * s.step, s.length), f32)

    def plane(z, carry):
        field = field_ref[z]
        high, low = split(real_ref[z, : s.length, :] * jnp.concatenate([field, field], 1))
        turned = dot(x_back_ref[...], jnp.concatenate([high, low], 0))
        keep_turned(s, turned_ref, z, turned[: s.kept] + turned[s.kept :])
        return carry

    lax.fori_loop(0, s.planes, plane, 0, unroll=4)


def keep_turned(s, turned_ref, z, turned):
    at = 0
    for component in range(2):
        for parity in range(2):
            count = s.odd if parity else s.even
            for o in range(2):
                turned_ref[2 * parity + component, pl.ds(o * s.planes + z, count, stride=s.step), :] = turned[
                    at : at + count, o * s.length : (o + 1) * s.length
                ]
            at += count


def finish_kernel(s, bands, half, first_ref, real_ref, slab_ref, x_last_ref, y_back_ref, flat_ref, turned_ref):
    for t in range(2, 4):
        turned_ref[t, s.odd * s.step :, :] = jnp.zeros(((s.even - s.odd) * s.step, s.length), f32)
    x_last = x_last_ref[last_owner(bands)]
    part = s.planes // 2

    def plane(z, carry):
        field = slab_ref[z]
        high, low = split(real_ref[half * part + z, s.length :, :] * jnp.concatenate([field, field], 1))
        keep_turned(s, turned_ref, half * part + z, dot(x_last, jnp.concatenate([high, low, high], 0)))
        return carry

    lax.fori_loop(0, part, plane, 0, unroll=4)

    lanes = 2 * s.rows_y
    table = jnp.concatenate([y_back_ref[0], y_back_ref[0], y_back_ref[1]], 0)
    for start in range(0, s.tiles, 8):
        end = min(s.tiles, start + 8)
        parts = []
        for tile in range(start, end):
            for o in range(2):
                row = tile * s.step + o * s.planes + half * part
                own = slice(row, row + part)
                parts.append(jnp.concatenate([first_ref[t, own, :] + turned_ref[t, own, :] for t in range(4)], 1))
        high, low = split(jnp.concatenate(parts, 0))
        moved = dot(jnp.concatenate([high, low, high], 1), table)
        high, low = split(moved)
        for tile in range(start, end):
            at = (tile - start) * s.planes
            for component in range(2):
                mine = slice(at, at + s.planes), slice(component * lanes, (component + 1) * lanes)
                for row, value in ((component, high), (2 + component, low)):
                    flat_ref[row * s.planes : (row + 1) * s.planes, tile * lanes : (tile + 1) * lanes] = value[mine]


def pick_kernel(s, which, count, joined, *refs):
    flat_refs, sticks_ref, refs = refs[:count], refs[count], refs[count + 1 :]
    out_refs, (x_ref, y_ref, hot_ref) = refs[:-3], refs[-3:]
    me = lax.axis_index("plane")
    places(s, sticks_ref, [partner(me, k) for k in which], x_ref, y_ref)
    rows = 2 * s.planes
    flat = jnp.concatenate([flat_ref[...] for flat_ref in flat_refs], 0)
    for i in range(len(which)):
        columns = slice(i * s.sticks, (i + 1) * s.sticks)
        for x in range(2 * s.tiles):
            hot_ref[x * s.rows_y : (x + 1) * s.rows_y, :] = one_hot(x, x_ref[:, columns], y_ref[:, columns])
        found = dot(flat, hot_ref[...])
        for h in range(count):
            row = 2 * h * rows
            out_ref, at = (out_refs[0], (i * count + h) * rows) if joined else (out_refs[i], h * rows)
            out_ref[at : at + rows, :] = found[row : row + rows] + found[row + rows : row + 2 * rows]


def band_on_ring(place, count):
    return jnp.where(2 * place < count, 2 * place, 2 * (count - 1 - place) + 1)


def place_on_ring(band, count):
    return jnp.where(lax.rem(band, 2) == 0, band // 2, count - 1 - band // 2)


def last_owner(count):
    return band_on_ring(lax.rem(place_on_ring(lax.axis_index("band"), count) + count // 2, count), count)


def ring_offsets(count):
    offsets = [(0, 0, 2)]
    for step in range(1, count // 2 + 1):
        last = 2 * step == count
        offsets += [(-step, 0, 1 if last else 2), (step, 1 if last else 0, 2)]
    return offsets


def partners(devices):
    return sorted(range(1, devices), key=lambda k: (k == 1, k % 2, k))


def send_groups(devices):
    soon, *others, near = partners(devices)
    return [[soon, soon ^ 1], *(k for k in others if k != soon ^ 1), near]


def stages(devices):
    far = partners(devices)[:-1]
    return [("lay1", [0, 1]), ("lay2", far[:-1]), ("lay3", far[-1:])]


def per_device(bands, coeffs, potential, stick_map):
    devices = stick_map.shape[1] // coeffs.shape[3]
    s = Sizes(coeffs.shape[2], coeffs.shape[3], potential.shape[2], potential.shape[0], devices)
    tab = {name: jnp.asarray(value) for name, value in tables(s, bands).items()}
    rows = 2 * s.batch
    block = jax.ShapeDtypeStruct((rows, s.sticks), f32)

    order = list(range(0, bands, 2)) + list(range(bands - 1, 0, -2))
    along = [(order[i], order[(i + 1) % bands]) for i in range(bands)]
    against = [(b, a) for a, b in along]

    def exchange(blocks):
        out = [blocks[0]] + [None] * (devices - 1)
        for k in partners(devices):
            out[k] = lax.ppermute(blocks[k], "plane", [(i, i ^ k) for i in range(devices)])
        return out

    def ring():
        slabs = [potential]
        up = down = potential
        for step in range(1, bands // 2 + 1):
            last = 2 * step == bands
            if last:
                up, down = up[: s.planes // 2], down[s.planes // 2 :]
            up = lax.ppermute(up, "band", along)
            down = lax.ppermute(down, "band", against)
            slabs += [up, down]
        return slabs

    def kernel(body, inputs, out_shape, limit, flops, scratch_shapes=(), place=VMEM, fetched=()):
        single = not isinstance(out_shape, list)
        outs = [out_shape] if single else out_shape
        extra = [jax.ShapeDtypeStruct(a.shape, a.dtype) for a in fetched]
        if fetched:
            body = functools.partial(fetching_kernel, body, len(inputs), len(outs), len(fetched))
        results = pl.pallas_call(
            body,
            in_specs=[place] * len(inputs) + [HBM] * len(fetched),
            out_specs=[VMEM] * (len(outs) + len(fetched)),
            out_shape=outs + extra,
            scratch_shapes=[*scratch_shapes] + [pltpu.SemaphoreType.DMA((len(fetched),))] * bool(fetched),
            compiler_params=pltpu.CompilerParams(vmem_limit_bytes=limit << 10),
            cost_estimate=pl.CostEstimate(flops=flops, bytes_accessed=1 << 20, transcendentals=0),
        )(*inputs, *(pltpu.with_memory_space_constraint(a, pltpu.HBM) for a in fetched))
        if fetched:
            return results[: len(outs)], results[len(outs) :]
        return results[0] if single else results

    slabs = ring()
    positions = 2 * s.tiles * s.rows_y
    results = []
    for pair in range(coeffs.shape[0]):
        given = jnp.transpose(coeffs[pair : pair + 1], (0, 2, 1, 3))
        sent = kernel(
            functools.partial(ahead_kernel, s),
            [pltpu.with_memory_space_constraint(a, pltpu.HBM) for a in (given, stick_map, tab["z_ahead"])],
            [block] * devices,
            16 << 10,
            1 << 31,
            [
                pltpu.VMEM(given.shape, f32),
                pltpu.VMEM(stick_map.shape, jnp.int32),
                pltpu.VMEM(tab["z_ahead"].shape, bf16),
                pltpu.SemaphoreType.DMA((3,)),
            ],
            HBM,
        )
        held = exchange(sent)
        half = None
        ready = results
        later = ["y_ahead", "x_ahead", "x_back", "x_last", "y_back", "z_back"]
        grid_shape = (s.tiles * s.batch, 4 * s.rows_y)
        for name, which in stages(devices):
            started, ended = half is not None, name == "lay3"
            shape = (4, s.even * s.step, s.length) if ended else grid_shape
            own = [pltpu.VMEM((s.rows_y, len(which) * s.sticks), bf16)] * 2
            own.append(pltpu.VMEM((2 * rows, len(which) * s.sticks), bf16))
            fetch = [] if started or ready else [tab[key] for key in later] + [potential]
            half = kernel(
                functools.partial(lay_kernel, s, which, started, ended),
                [held[k] for k in which] + [half] * started + [stick_map] + [tab["y_ahead"]] * ended,
                jax.ShapeDtypeStruct(shape, f32),
                24 << 10,
                1 << 31,
                [pltpu.VMEM(grid_shape, f32)] * ended + own,
                fetched=fetch,
            )
            if fetch:
                (half,), (*ready, slabs[0]) = half
                tab.update(zip(later, ready, strict=True))
        turned_shape = (4, s.even * s.step, s.length)
        real = kernel(
            functools.partial(turn_kernel, s, bands),
            [half, tab["x_ahead"]],
            jax.ShapeDtypeStruct((s.planes, s.length + s.length // bands, 2 * s.length), f32),
            16 << 10,
            1 << 31,
        )
        turned = kernel(
            functools.partial(space_kernel, s, bands),
            [real, *slabs[:-2], tab["x_back"]],
            jax.ShapeDtypeStruct(turned_shape, f32),
            16 << 10,
            1 << 31,
            [pltpu.VMEM((s.planes, s.length, s.length), f32)],
        )
        flats = [
            kernel(
                functools.partial(finish_kernel, s, bands, half),
                [turned, real, slabs[half - 2], tab["x_last"], tab["y_back"]],
                jax.ShapeDtypeStruct((4 * s.planes, positions), bf16),
                20 << 10,
                1 << 31,
                [pltpu.VMEM(turned_shape, f32)],
            )
            for half in range(2)
        ]

        def pick(which, flats, joined=False):
            size = len(flats) * 2 * s.planes
            shape = jax.ShapeDtypeStruct((size * len(which) if joined else size, s.sticks), f32)
            return kernel(
                functools.partial(pick_kernel, s, which, len(flats), joined),
                [*flats, stick_map],
                [shape] if joined else [shape] * len(which),
                16 << 10,
                1 << 31,
                [
                    pltpu.VMEM((s.rows_y, len(which) * s.sticks), bf16),
                    pltpu.VMEM((s.rows_y, len(which) * s.sticks), bf16),
                    pltpu.VMEM((positions, s.sticks), bf16),
                ],
            )

        def send(k, block):
            return lax.ppermute(block, "plane", [(i, i ^ k) for i in range(devices)])

        (soon, across), *others, near = send_groups(devices)
        both = send(soon, *pick([across, soon], [flats[0]], True))
        hop, last = pick([across, soon], [flats[1]])
        hop = send(soon, hop)
        last = send(soon, last)
        returned = [(k, None, 0, send(k, *pick([k], flats))) for k in others]
        beside, own = pick([near, 0], flats)
        returned += [(near, None, 0, send(near, beside)), (0, None, 0, own), (soon, 0, s.batch, both)]
        returned.append((across, 0, 0, send(near, both[: s.batch])))
        late = [(across, 1, 0, send(near, hop)), (soon, 1, 0, last)]
        begun = kernel(
            functools.partial(back_kernel, s, [block[:3] for block in returned], False, False),
            [*(block[3] for block in returned), tab["z_back"]],
            jax.ShapeDtypeStruct((s.depth_rows, s.sticks), f32),
            16 << 10,
            1 << 31,
        )
        result = kernel(
            functools.partial(back_kernel, s, [block[:3] for block in late], True, True),
            [*(block[3] for block in late), begun, stick_map, tab["z_back"]],
            jax.ShapeDtypeStruct((1,) + given.shape[1:], f32),
            16 << 10,
            1 << 31,
        )
        results.append(jnp.transpose(result, (0, 2, 1, 3)))
    return results[0] if len(results) == 1 else jnp.concatenate(results, 0)


def solution(mesh):
    placed = (P("band", None, None, "plane"), P("plane", "band", None), P())
    return jax.shard_map(
        functools.partial(per_device, mesh.shape["band"]),
        mesh=mesh,
        in_specs=placed,
        out_specs=P("band", None, None, "plane"),
        check_vma=False,
    )
```

```python
import functools
import math

import jax
import jax.numpy as jnp
import ml_dtypes
import numpy as np
from jax import lax
from jax.experimental import pallas as pl
from jax.experimental.pallas import tpu as pltpu
from jax.sharding import PartitionSpec as P


bf16 = jnp.bfloat16
f32 = jnp.float32
VMEM = pl.BlockSpec(memory_space=pltpu.VMEM)
HBM = pl.BlockSpec(memory_space=pltpu.HBM)


def up8(n):
    return -(-n // 8) * 8


def halves(table):
    high = table.astype(ml_dtypes.bfloat16)
    return high, (table - high.astype(np.float64)).astype(ml_dtypes.bfloat16)


def split(value):
    high = value.astype(bf16)
    return high, (value - high.astype(f32)).astype(bf16)


class Sizes:
    def __init__(self, span, sticks, length, planes, devices):
        self.span, self.length, self.planes, self.devices = span, length, planes, devices
        self.sticks = sticks
        self.radius = (span - 1) // 2
        self.rows_y = 2 * self.radius
        self.tiles = self.radius // 2 + 1
        self.even = up8(self.tiles)
        self.odd = up8(self.radius // 2)
        self.kept = 2 * (self.even + self.odd)
        self.batch = 2 * planes
        self.step = self.batch + 1
        self.depths = span - 2
        self.depth_rows = -(-4 * self.depths // 16) * 16


def tables(s, bands):
    turn = 2.0 * math.pi / s.length
    grid = np.arange(s.length)
    depth = np.arange(s.depths) + 1 - s.radius
    y = np.arange(s.rows_y) + 1 - s.radius

    def trig(left, right):
        angle = turn * np.mod(np.outer(left, right), s.length)
        return np.cos(angle), np.sin(angle)

    cos, sin = trig(depth, grid)
    ahead = np.zeros((s.devices, 2, 2, s.planes, s.depths, 2, 2))
    back = np.zeros((s.devices, s.depths, 2, 2, 2, 2, s.planes))
    scale = 1.0 / float(s.length) ** 3
    for d in range(s.devices):
        own = slice(d * s.planes, (d + 1) * s.planes)
        c, n = cos[:, own], sin[:, own]
        for o in range(2):
            ahead[d, 0, o, :, :, o, 0] = c.T
            ahead[d, 0, o, :, :, o, 1] = -n.T
            ahead[d, 1, o, :, :, o, 0] = n.T
            ahead[d, 1, o, :, :, o, 1] = c.T
            back[d, :, o, 0, 0, o] = c * scale
            back[d, :, o, 0, 1, o] = n * scale
            back[d, :, o, 1, 0, o] = -n * scale
            back[d, :, o, 1, 1, o] = c * scale
    gap = s.depth_rows - 4 * s.depths
    ahead = np.pad(ahead.reshape(s.devices, 2 * s.batch, 4 * s.depths), ((0, 0), (0, 0), (0, gap)))
    back = back.reshape(s.devices, 4 * s.depths, 4, 2, s.planes // 2).transpose(0, 1, 3, 2, 4)
    back = np.pad(back.reshape(s.devices, 4 * s.depths, 2 * s.batch), ((0, 0), (0, gap), (0, 0)))

    cos, sin = trig(y, grid)
    y_ahead = np.zeros((2, 2, s.rows_y, 2, 2, s.length))
    y_back = np.zeros((2, 2, s.length, 2, 2, s.rows_y))
    for parity in range(2):
        y_ahead[0, parity, :, parity, 0] = cos
        y_ahead[1, parity, :, parity, 0] = -sin
        y_ahead[0, parity, :, parity, 1] = sin
        y_ahead[1, parity, :, parity, 1] = cos
        y_back[parity, 0, :, 0, parity] = cos.T
        y_back[parity, 1, :, 0, parity] = sin.T
        y_back[parity, 0, :, 1, parity] = -sin.T
        y_back[parity, 1, :, 1, parity] = cos.T
    y_ahead = y_ahead.reshape(4 * s.rows_y, 4 * s.length)
    y_back = y_back.reshape(4 * s.length, 4 * s.rows_y)

    x_ahead = np.zeros((s.length, s.kept))
    x_back = np.zeros((s.kept, s.length))
    at = 0
    for component in range(2):
        for parity in range(2):
            count = s.tiles if parity == 0 else s.radius // 2
            cos, sin = trig(2 * np.arange(count) + parity, grid)
            x_ahead[:, at : at + count] = 2.0 * cos.T if component == 0 else -2.0 * sin.T
            x_back[at : at + count] = cos if component == 0 else -sin
            at += s.even if parity == 0 else s.odd

    def beside(table, axis, order):
        parts = halves(table)
        return np.concatenate([parts[i] for i in order], axis)

    zero = np.zeros(x_back.shape, ml_dtypes.bfloat16)
    high, low = halves(x_back)
    by_slab = x_back.reshape(s.kept, bands, s.length // bands).transpose(1, 0, 2)
    return dict(
        z_ahead=beside(ahead, 2, (0, 1)),
        z_back=beside(back, 2, (0, 1)),
        y_ahead=np.stack(halves(y_ahead)),
        y_back=np.stack(halves(y_back)),
        x_ahead=beside(x_ahead, 1, (0, 1, 0)),
        x_last=beside(by_slab, 2, (0, 0, 1)),
        x_back=np.concatenate([np.concatenate([high, high], 1), np.concatenate([low, zero], 1)], 0),
    )


def dot(left, right):
    return jnp.dot(left, right, preferred_element_type=f32)


def partner(me, k):
    return jnp.bitwise_xor(me, k)


def live_of(s, sticks_ref, source):
    columns = pl.ds(pl.multiple_of(source * s.sticks, s.sticks), s.sticks)
    depth = lax.broadcasted_iota(jnp.int32, (4 * s.depths, s.sticks), 0) // 4 + 1 - s.radius
    return jnp.abs(depth) <= sticks_ref[2:3, columns]


def ahead_kernel(s, coeffs_hbm, sticks_hbm, table_hbm, *refs):
    out_refs, (coeffs_ref, sticks_ref, table_ref, sems) = refs[: s.devices], refs[s.devices :]
    pairs = [(sticks_hbm, sticks_ref), (coeffs_hbm, coeffs_ref), (table_hbm, table_ref)]
    copies = [pltpu.make_async_copy(source, target, sems.at[i]) for i, (source, target) in enumerate(pairs)]
    for copy in copies:
        copy.start()
    me = lax.axis_index("plane")
    copies[0].wait()
    live = live_of(s, sticks_ref, me)
    copies[1].wait()
    data = jnp.where(live, coeffs_ref[0, 1 : s.span - 1].reshape(4 * s.depths, s.sticks), 0.0)
    gap = jnp.zeros((s.depth_rows - 4 * s.depths, s.sticks), f32)
    high, low = split(jnp.concatenate([data, gap], 0))
    data = jnp.concatenate([high, high, low], 0)
    copies[2].wait()
    for k in [*partners(s.devices), 0]:
        table = table_ref[partner(me, k)]
        out_refs[k][...] = dot(jnp.concatenate([table, table[:, : s.depth_rows]], 1), data)


def back_kernel(s, which, started, ended, *refs):
    in_refs, refs = refs[: len(which)], refs[len(which) :]
    table_ref, out_ref = refs[-2:]
    part = jnp.zeros((s.batch, s.sticks), f32)
    me = lax.axis_index("plane")
    total = refs[0][...] if started else None
    blocks = {}
    for (k, half, row), ref in zip(which, in_refs, strict=True):
        if half is None:
            blocks[k] = ref[...]
        else:
            blocks.setdefault(k, [part, part])[half] = ref[row : row + s.batch, :]
    for k, block in blocks.items():
        high, low = split(jnp.concatenate(block, 0) if isinstance(block, list) else block)
        table = table_ref[partner(me, k)]
        table = jnp.concatenate([table, table[:, : 2 * s.batch]], 1)
        term = dot(table, jnp.concatenate([high, high, low], 0))
        total = term if total is None else total + term
    if ended:
        total = jnp.where(live_of(s, refs[-3], me), total[: 4 * s.depths], 0.0)
        out_ref[0, 1 : s.span - 1] = total.reshape(s.depths, 4, s.sticks)
        for depth in (0, s.span - 1):
            out_ref[0, depth] = jnp.zeros((4, s.sticks), f32)
    else:
        out_ref[...] = total


def fetching_kernel(body, inputs, outs, count, *refs):
    sources, targets = refs[inputs : inputs + count], refs[inputs + count + outs : inputs + 2 * count + outs]
    copies = [pltpu.make_async_copy(sources[i], targets[i], refs[-1].at[i]) for i in range(count)]
    for copy in copies:
        copy.start()
    body(*refs[:inputs], *refs[inputs + count : inputs + count + outs], *refs[inputs + 2 * count + outs : -1])
    for copy in copies:
        copy.wait()


def places(s, sticks_ref, sources, x_ref, y_ref):
    at = 0
    for source in sources:
        columns = pl.ds(pl.multiple_of(source * s.sticks, s.sticks), s.sticks)
        shape = (s.rows_y, s.sticks)
        x_ref[:, at : at + s.sticks] = jnp.broadcast_to(sticks_ref[0:1, columns].astype(f32), shape).astype(bf16)
        row = lax.broadcasted_iota(jnp.int32, shape, 0) + 1 - s.radius
        hit = sticks_ref[1:2, columns] == row
        y_ref[:, at : at + s.sticks] = jnp.where(hit, 1.0, 0.0).astype(bf16)
        at += s.sticks


def one_hot(x, x_all, y_all):
    return jnp.where(x_all == jnp.asarray(x, bf16), y_all, jnp.zeros_like(y_all))


def lay_kernel(s, which, started, ended, *refs):
    in_refs, refs = refs[: len(which)], refs[len(which) :]
    before_ref, refs = (refs[0], refs[1:]) if started else (None, refs)
    sticks_ref, refs = refs[0], refs[1:]
    table_ref, out_ref, grid_ref = refs[:3] if ended else (None, None, refs[0])
    x_ref, y_ref, both_ref = refs[-3:]
    me = lax.axis_index("plane")
    places(s, sticks_ref, [partner(me, k) for k in which], x_ref, y_ref)
    rows = 2 * s.batch
    for i in range(len(which)):
        high, low = split(in_refs[i][...])
        both_ref[:rows, i * s.sticks : (i + 1) * s.sticks] = high
        both_ref[rows:, i * s.sticks : (i + 1) * s.sticks] = low
    lanes = 2 * s.rows_y
    for first in range(0, s.tiles, 2):
        count = min(2, s.tiles - first)
        hot = jnp.concatenate([one_hot(x, x_ref[...], y_ref[...]) for x in range(2 * first, 2 * (first + count))], 0)
        laid = lax.dot_general(both_ref[...], hot, (((1,), (1,)), ((), ())), preferred_element_type=f32)
        laid = laid[:rows] + laid[rows:]
        for t in range(count):
            for component in range(2):
                own = pl.ds((first + t) * s.batch, s.batch), slice(component * lanes, (component + 1) * lanes)
                part = laid[component * s.batch : (component + 1) * s.batch, t * lanes : (t + 1) * lanes]
                grid_ref[own] = part + before_ref[own] if started else part
    if not ended:
        return
    total = s.tiles * s.batch
    table = jnp.concatenate([table_ref[0], table_ref[0], table_ref[1]], 0)
    for start in range(0, total, 4 * s.batch):
        end = min(total, start + 4 * s.batch)
        high, low = split(grid_ref[start:end, :])
        moved = dot(jnp.concatenate([high, low, high], 1), table)
        for t in range(4):
            for row in range(0, end - start, s.batch):
                at = (start + row) // s.batch * s.step
                out_ref[t, at : at + s.batch, :] = moved[row : row + s.batch, t * s.length : (t + 1) * s.length]
    for t in range(4):
        out_ref[t, s.tiles * s.step :, :] = jnp.zeros(((s.even - s.tiles) * s.step, s.length), f32)


def turn_kernel(s, bands, half_ref, x_ahead_ref, real_ref):
    width = s.length // bands
    last = pl.ds(pl.multiple_of(last_owner(bands) * width, width), width)
    table = jnp.concatenate([x_ahead_ref[...], x_ahead_ref[last, :]], 0)

    def plane(z, carry):
        parts = []
        for component in range(2):
            for parity in range(2):
                count = s.odd if parity else s.even
                parts.append(
                    jnp.concatenate(
                        [
                            half_ref[2 * parity + component, pl.ds(o * s.planes + z, count, stride=s.step), :]
                            for o in range(2)
                        ],
                        1,
                    )
                )
        high, low = split(jnp.concatenate(parts, 0))
        real_ref[z] = dot(table, jnp.concatenate([high, high, low], 0))
        return carry

    lax.fori_loop(0, s.planes, plane, 0, unroll=4)


def space_kernel(s, bands, real_ref, *refs):
    offsets = ring_offsets(bands)[:-2]
    slab_refs, (x_back_ref, turned_ref, field_ref) = refs[: len(offsets)], refs[len(offsets) :]
    width = s.length // bands
    band = lax.axis_index("band")
    at = place_on_ring(band, bands)
    for (offset, _, _), slab_ref in zip(offsets, slab_refs, strict=True):
        owner = band_on_ring(lax.rem(at + offset + bands, bands), bands)
        field_ref[:, pl.ds(pl.multiple_of(owner * width, width), width), :] = slab_ref[...]
    last = pl.ds(pl.multiple_of(last_owner(bands) * width, width), width)
    field_ref[:, last, :] = jnp.zeros((s.planes, width, s.length), f32)
    for t in range(2, 4):
        turned_ref[t, s.odd * s.step :, :] = jnp.zeros(((s.even - s.odd) * s.step, s.length), f32)

    def plane(z, carry):
        field = field_ref[z]
        high, low = split(real_ref[z, : s.length, :] * jnp.concatenate([field, field], 1))
        turned = dot(x_back_ref[...], jnp.concatenate([high, low], 0))
        keep_turned(s, turned_ref, z, turned[: s.kept] + turned[s.kept :])
        return carry

    lax.fori_loop(0, s.planes, plane, 0, unroll=4)


def keep_turned(s, turned_ref, z, turned):
    at = 0
    for component in range(2):
        for parity in range(2):
            count = s.odd if parity else s.even
            for o in range(2):
                turned_ref[2 * parity + component, pl.ds(o * s.planes + z, count, stride=s.step), :] = turned[
                    at : at + count, o * s.length : (o + 1) * s.length
                ]
            at += count


def finish_kernel(s, bands, half, first_ref, real_ref, slab_ref, x_last_ref, y_back_ref, flat_ref, turned_ref):
    for t in range(2, 4):
        turned_ref[t, s.odd * s.step :, :] = jnp.zeros(((s.even - s.odd) * s.step, s.length), f32)
    x_last = x_last_ref[last_owner(bands)]
    part = s.planes // 2

    def plane(z, carry):
        field = slab_ref[z]
        high, low = split(real_ref[half * part + z, s.length :, :] * jnp.concatenate([field, field], 1))
        keep_turned(s, turned_ref, half * part + z, dot(x_last, jnp.concatenate([high, low, high], 0)))
        return carry

    lax.fori_loop(0, part, plane, 0, unroll=4)

    lanes = 2 * s.rows_y
    table = jnp.concatenate([y_back_ref[0], y_back_ref[0], y_back_ref[1]], 0)
    for start in range(0, s.tiles, 8):
        end = min(s.tiles, start + 8)
        parts = []
        for tile in range(start, end):
            for o in range(2):
                row = tile * s.step + o * s.planes + half * part
                own = slice(row, row + part)
                parts.append(jnp.concatenate([first_ref[t, own, :] + turned_ref[t, own, :] for t in range(4)], 1))
        high, low = split(jnp.concatenate(parts, 0))
        moved = dot(jnp.concatenate([high, low, high], 1), table)
        high, low = split(moved)
        for tile in range(start, end):
            at = (tile - start) * s.planes
            for component in range(2):
                mine = slice(at, at + s.planes), slice(component * lanes, (component + 1) * lanes)
                for row, value in ((component, high), (2 + component, low)):
                    flat_ref[row * s.planes : (row + 1) * s.planes, tile * lanes : (tile + 1) * lanes] = value[mine]


def pick_kernel(s, which, count, joined, *refs):
    flat_refs, sticks_ref, refs = refs[:count], refs[count], refs[count + 1 :]
    out_refs, (x_ref, y_ref, hot_ref) = refs[:-3], refs[-3:]
    me = lax.axis_index("plane")
    places(s, sticks_ref, [partner(me, k) for k in which], x_ref, y_ref)
    rows = 2 * s.planes
    flat = jnp.concatenate([flat_ref[...] for flat_ref in flat_refs], 0)
    for i in range(len(which)):
        columns = slice(i * s.sticks, (i + 1) * s.sticks)
        for x in range(2 * s.tiles):
            hot_ref[x * s.rows_y : (x + 1) * s.rows_y, :] = one_hot(x, x_ref[:, columns], y_ref[:, columns])
        found = dot(flat, hot_ref[...])
        for h in range(count):
            row = 2 * h * rows
            out_ref, at = (out_refs[0], (i * count + h) * rows) if joined else (out_refs[i], h * rows)
            out_ref[at : at + rows, :] = found[row : row + rows] + found[row + rows : row + 2 * rows]


def band_on_ring(place, count):
    return jnp.where(2 * place < count, 2 * place, 2 * (count - 1 - place) + 1)


def place_on_ring(band, count):
    return jnp.where(lax.rem(band, 2) == 0, band // 2, count - 1 - band // 2)


def last_owner(count):
    return band_on_ring(lax.rem(place_on_ring(lax.axis_index("band"), count) + count // 2, count), count)


def ring_offsets(count):
    offsets = [(0, 0, 2)]
    for step in range(1, count // 2 + 1):
        last = 2 * step == count
        offsets += [(-step, 0, 1 if last else 2), (step, 1 if last else 0, 2)]
    return offsets


def partners(devices):
    return sorted(range(1, devices), key=lambda k: (k == 1, k % 2, k))


def send_groups(devices):
    soon, *others, near = partners(devices)
    return [[soon, soon ^ 1], *(k for k in others if k != soon ^ 1), near]


def stages(devices):
    far = partners(devices)[:-1]
    return [("lay1", [0, 1]), ("lay2", far[:-1]), ("lay3", far[-1:])]


def per_device(bands, coeffs, potential, stick_map):
    devices = stick_map.shape[1] // coeffs.shape[3]
    s = Sizes(coeffs.shape[2], coeffs.shape[3], potential.shape[2], potential.shape[0], devices)
    tab = {name: jnp.asarray(value) for name, value in tables(s, bands).items()}
    rows = 2 * s.batch
    block = jax.ShapeDtypeStruct((rows, s.sticks), f32)

    order = list(range(0, bands, 2)) + list(range(bands - 1, 0, -2))
    along = [(order[i], order[(i + 1) % bands]) for i in range(bands)]
    against = [(b, a) for a, b in along]

    def exchange(blocks):
        out = [blocks[0]] + [None] * (devices - 1)
        for k in partners(devices):
            out[k] = lax.ppermute(blocks[k], "plane", [(i, i ^ k) for i in range(devices)])
        return out

    def ring():
        slabs = [potential]
        up = down = potential
        for step in range(1, bands // 2 + 1):
            last = 2 * step == bands
            if last:
                up, down = up[: s.planes // 2], down[s.planes // 2 :]
            up = lax.ppermute(up, "band", along)
            down = lax.ppermute(down, "band", against)
            slabs += [up, down]
        return slabs

    def kernel(body, inputs, out_shape, limit, flops, scratch_shapes=(), place=VMEM, fetched=()):
        single = not isinstance(out_shape, list)
        outs = [out_shape] if single else out_shape
        extra = [jax.ShapeDtypeStruct(a.shape, a.dtype) for a in fetched]
        if fetched:
            body = functools.partial(fetching_kernel, body, len(inputs), len(outs), len(fetched))
        results = pl.pallas_call(
            body,
            in_specs=[place] * len(inputs) + [HBM] * len(fetched),
            out_specs=[VMEM] * (len(outs) + len(fetched)),
            out_shape=outs + extra,
            scratch_shapes=[*scratch_shapes] + [pltpu.SemaphoreType.DMA((len(fetched),))] * bool(fetched),
            compiler_params=pltpu.CompilerParams(vmem_limit_bytes=limit << 10),
            cost_estimate=pl.CostEstimate(flops=flops, bytes_accessed=1 << 20, transcendentals=0),
        )(*inputs, *(pltpu.with_memory_space_constraint(a, pltpu.HBM) for a in fetched))
        if fetched:
            return results[: len(outs)], results[len(outs) :]
        return results[0] if single else results

    slabs = ring()
    positions = 2 * s.tiles * s.rows_y
    results = []
    for pair in range(coeffs.shape[0]):
        given = jnp.transpose(coeffs[pair : pair + 1], (0, 2, 1, 3))
        sent = kernel(
            functools.partial(ahead_kernel, s),
            [pltpu.with_memory_space_constraint(a, pltpu.HBM) for a in (given, stick_map, tab["z_ahead"])],
            [block] * devices,
            16 << 10,
            1 << 31,
            [
                pltpu.VMEM(given.shape, f32),
                pltpu.VMEM(stick_map.shape, jnp.int32),
                pltpu.VMEM(tab["z_ahead"].shape, bf16),
                pltpu.SemaphoreType.DMA((3,)),
            ],
            HBM,
        )
        held = exchange(sent)
        half = None
        ready = results
        later = ["y_ahead", "x_ahead", "x_back", "x_last", "y_back", "z_back"]
        grid_shape = (s.tiles * s.batch, 4 * s.rows_y)
        for name, which in stages(devices):
            started, ended = half is not None, name == "lay3"
            shape = (4, s.even * s.step, s.length) if ended else grid_shape
            own = [pltpu.VMEM((s.rows_y, len(which) * s.sticks), bf16)] * 2
            own.append(pltpu.VMEM((2 * rows, len(which) * s.sticks), bf16))
            fetch = [] if started or ready else [tab[key] for key in later] + [potential]
            half = kernel(
                functools.partial(lay_kernel, s, which, started, ended),
                [held[k] for k in which] + [half] * started + [stick_map] + [tab["y_ahead"]] * ended,
                jax.ShapeDtypeStruct(shape, f32),
                24 << 10,
                1 << 31,
                [pltpu.VMEM(grid_shape, f32)] * ended + own,
                fetched=fetch,
            )
            if fetch:
                (half,), (*ready, slabs[0]) = half
                tab.update(zip(later, ready, strict=True))
        turned_shape = (4, s.even * s.step, s.length)
        real = kernel(
            functools.partial(turn_kernel, s, bands),
            [half, tab["x_ahead"]],
            jax.ShapeDtypeStruct((s.planes, s.length + s.length // bands, 2 * s.length), f32),
            16 << 10,
            1 << 31,
        )
        turned = kernel(
            functools.partial(space_kernel, s, bands),
            [real, *slabs[:-2], tab["x_back"]],
            jax.ShapeDtypeStruct(turned_shape, f32),
            16 << 10,
            1 << 31,
            [pltpu.VMEM((s.planes, s.length, s.length), f32)],
        )
        flats = [
            kernel(
                functools.partial(finish_kernel, s, bands, half),
                [turned, real, slabs[half - 2], tab["x_last"], tab["y_back"]],
                jax.ShapeDtypeStruct((4 * s.planes, positions), bf16),
                20 << 10,
                1 << 31,
                [pltpu.VMEM(turned_shape, f32)],
            )
            for half in range(2)
        ]

        def pick(which, flats, joined=False):
            size = len(flats) * 2 * s.planes
            shape = jax.ShapeDtypeStruct((size * len(which) if joined else size, s.sticks), f32)
            return kernel(
                functools.partial(pick_kernel, s, which, len(flats), joined),
                [*flats, stick_map],
                [shape] if joined else [shape] * len(which),
                16 << 10,
                1 << 31,
                [
                    pltpu.VMEM((s.rows_y, len(which) * s.sticks), bf16),
                    pltpu.VMEM((s.rows_y, len(which) * s.sticks), bf16),
                    pltpu.VMEM((positions, s.sticks), bf16),
                ],
            )

        def send(k, block):
            return lax.ppermute(block, "plane", [(i, i ^ k) for i in range(devices)])

        (soon, across), *others, near = send_groups(devices)
        both = send(soon, *pick([across, soon], [flats[0]], True))
        hop, last = pick([across, soon], [flats[1]])
        hop = send(across, hop)
        last = send(soon, last)
        returned = [(k, None, 0, send(k, *pick([k], flats))) for k in others]
        beside, own = pick([near, 0], flats)
        returned += [(near, None, 0, send(near, beside)), (0, None, 0, own), (soon, 0, s.batch, both)]
        late = [(across, 0, 0, send(near, both[: s.batch]))]
        late += [(across, 1, 0, hop), (soon, 1, 0, last)]
        begun = kernel(
            functools.partial(back_kernel, s, [block[:3] for block in returned], False, False),
            [*(block[3] for block in returned), tab["z_back"]],
            jax.ShapeDtypeStruct((s.depth_rows, s.sticks), f32),
            16 << 10,
            1 << 31,
        )
        result = kernel(
            functools.partial(back_kernel, s, [block[:3] for block in late], True, True),
            [*(block[3] for block in late), begun, stick_map, tab["z_back"]],
            jax.ShapeDtypeStruct((1,) + given.shape[1:], f32),
            16 << 10,
            1 << 31,
        )
        results.append(jnp.transpose(result, (0, 2, 1, 3)))
    return results[0] if len(results) == 1 else jnp.concatenate(results, 0)


def solution(mesh):
    placed = (P("band", None, None, "plane"), P("plane", "band", None), P())
    return jax.shard_map(
        functools.partial(per_device, mesh.shape["band"]),
        mesh=mesh,
        in_specs=placed,
        out_specs=P("band", None, None, "plane"),
        check_vma=False,
    )
```

```python
import functools
import math

import jax
import jax.numpy as jnp
import ml_dtypes
import numpy as np
from jax import lax
from jax.experimental import pallas as pl
from jax.experimental.pallas import tpu as pltpu
from jax.sharding import PartitionSpec as P


bf16 = jnp.bfloat16
f32 = jnp.float32
VMEM = pl.BlockSpec(memory_space=pltpu.VMEM)
HBM = pl.BlockSpec(memory_space=pltpu.HBM)


def up8(n):
    return -(-n // 8) * 8


def halves(table):
    high = table.astype(ml_dtypes.bfloat16)
    return high, (table - high.astype(np.float64)).astype(ml_dtypes.bfloat16)


def split(value):
    high = value.astype(bf16)
    return high, (value - high.astype(f32)).astype(bf16)


class Sizes:
    def __init__(self, span, sticks, length, planes, devices):
        self.span, self.length, self.planes, self.devices = span, length, planes, devices
        self.sticks = sticks
        self.radius = (span - 1) // 2
        self.rows_y = 2 * self.radius
        self.tiles = self.radius // 2 + 1
        self.even = up8(self.tiles)
        self.odd = up8(self.radius // 2)
        self.kept = 2 * (self.even + self.odd)
        self.batch = 2 * planes
        self.step = self.batch + 1
        self.depths = span - 2
        self.depth_rows = -(-4 * self.depths // 16) * 16


def tables(s, bands):
    turn = 2.0 * math.pi / s.length
    grid = np.arange(s.length)
    depth = np.arange(s.depths) + 1 - s.radius
    y = np.arange(s.rows_y) + 1 - s.radius

    def trig(left, right):
        angle = turn * np.mod(np.outer(left, right), s.length)
        return np.cos(angle), np.sin(angle)

    cos, sin = trig(depth, grid)
    ahead = np.zeros((s.devices, 2, 2, s.planes, s.depths, 2, 2))
    back = np.zeros((s.devices, s.depths, 2, 2, 2, 2, s.planes))
    scale = 1.0 / float(s.length) ** 3
    for d in range(s.devices):
        own = slice(d * s.planes, (d + 1) * s.planes)
        c, n = cos[:, own], sin[:, own]
        for o in range(2):
            ahead[d, 0, o, :, :, o, 0] = c.T
            ahead[d, 0, o, :, :, o, 1] = -n.T
            ahead[d, 1, o, :, :, o, 0] = n.T
            ahead[d, 1, o, :, :, o, 1] = c.T
            back[d, :, o, 0, 0, o] = c * scale
            back[d, :, o, 0, 1, o] = n * scale
            back[d, :, o, 1, 0, o] = -n * scale
            back[d, :, o, 1, 1, o] = c * scale
    gap = s.depth_rows - 4 * s.depths
    ahead = np.pad(ahead.reshape(s.devices, 2 * s.batch, 4 * s.depths), ((0, 0), (0, 0), (0, gap)))
    back = back.reshape(s.devices, 4 * s.depths, 4, 2, s.planes // 2).transpose(0, 1, 3, 2, 4)
    back = np.pad(back.reshape(s.devices, 4 * s.depths, 2 * s.batch), ((0, 0), (0, gap), (0, 0)))

    cos, sin = trig(y, grid)
    y_ahead = np.stack([np.stack([cos, sin], 1), np.stack([-sin, cos], 1)]).reshape(2 * s.rows_y, 2 * s.length)
    y_back = np.stack([np.stack([cos.T, -sin.T], 1), np.stack([sin.T, cos.T], 1)]).reshape(2 * s.length, 2 * s.rows_y)

    x_ahead = np.zeros((s.length, s.kept))
    x_back = np.zeros((s.kept, s.length))
    at = 0
    for component in range(2):
        for parity in range(2):
            count = s.tiles if parity == 0 else s.radius // 2
            cos, sin = trig(2 * np.arange(count) + parity, grid)
            x_ahead[:, at : at + count] = 2.0 * cos.T if component == 0 else -2.0 * sin.T
            x_back[at : at + count] = cos if component == 0 else -sin
            at += s.even if parity == 0 else s.odd

    def beside(table, axis, order):
        parts = halves(table)
        return np.concatenate([parts[i] for i in order], axis)

    def folded(table, axis):
        high, low = halves(table)
        zero = np.zeros(table.shape, ml_dtypes.bfloat16)
        first, second = (high, high), (low, zero)
        return np.concatenate([np.concatenate(first, 1 - axis), np.concatenate(second, 1 - axis)], axis)

    by_slab = x_back.reshape(s.kept, bands, s.length // bands).transpose(1, 0, 2)
    return dict(
        z_ahead=beside(ahead, 2, (0, 1)),
        z_back=beside(back, 2, (0, 1)),
        y_ahead=np.stack(halves(y_ahead)),
        y_back=folded(y_back, 1),
        x_ahead=beside(x_ahead, 1, (0, 1, 0)),
        x_last=beside(by_slab, 2, (0, 0, 1)),
        x_back=folded(x_back, 0),
    )


def braid(left, right):
    half = left.shape[1] // 2
    first = lax.broadcasted_iota(jnp.int32, left.shape, 1) < half
    return jnp.where(first, left, pltpu.roll(right, half, 1)), jnp.where(first, pltpu.roll(left, half, 1), right)


def dot(left, right):
    return jnp.dot(left, right, preferred_element_type=f32)


def partner(me, k):
    return jnp.bitwise_xor(me, k)


def live_of(s, sticks_ref, source):
    columns = pl.ds(pl.multiple_of(source * s.sticks, s.sticks), s.sticks)
    depth = lax.broadcasted_iota(jnp.int32, (4 * s.depths, s.sticks), 0) // 4 + 1 - s.radius
    return jnp.abs(depth) <= sticks_ref[2:3, columns]


def ahead_kernel(s, coeffs_hbm, sticks_hbm, table_hbm, *refs):
    out_refs, (coeffs_ref, sticks_ref, table_ref, sems) = refs[: s.devices], refs[s.devices :]
    pairs = [(sticks_hbm, sticks_ref), (coeffs_hbm, coeffs_ref), (table_hbm, table_ref)]
    copies = [pltpu.make_async_copy(source, target, sems.at[i]) for i, (source, target) in enumerate(pairs)]
    for copy in copies:
        copy.start()
    me = lax.axis_index("plane")
    copies[0].wait()
    live = live_of(s, sticks_ref, me)
    copies[1].wait()
    data = jnp.where(live, coeffs_ref[0, 1 : s.span - 1].reshape(4 * s.depths, s.sticks), 0.0)
    gap = jnp.zeros((s.depth_rows - 4 * s.depths, s.sticks), f32)
    high, low = split(jnp.concatenate([data, gap], 0))
    data = jnp.concatenate([high, high, low], 0)
    copies[2].wait()
    for k in [*partners(s.devices), 0]:
        table = table_ref[partner(me, k)]
        out_refs[k][...] = dot(jnp.concatenate([table, table[:, : s.depth_rows]], 1), data)


def back_kernel(s, which, started, ended, *refs):
    in_refs, refs = refs[: len(which)], refs[len(which) :]
    table_ref, out_ref = refs[-2:]
    part = jnp.zeros((s.batch, s.sticks), f32)
    me = lax.axis_index("plane")
    total = refs[0][...] if started else None
    blocks = {}
    for (k, half, row), ref in zip(which, in_refs, strict=True):
        if half is None:
            blocks[k] = ref[...]
        else:
            blocks.setdefault(k, [part, part])[half] = ref[row : row + s.batch, :]
    for k, block in blocks.items():
        high, low = split(jnp.concatenate(block, 0) if isinstance(block, list) else block)
        table = table_ref[partner(me, k)]
        table = jnp.concatenate([table, table[:, : 2 * s.batch]], 1)
        term = dot(table, jnp.concatenate([high, high, low], 0))
        total = term if total is None else total + term
    if ended:
        total = jnp.where(live_of(s, refs[-3], me), total[: 4 * s.depths], 0.0)
        out_ref[0, 1 : s.span - 1] = total.reshape(s.depths, 4, s.sticks)
        for depth in (0, s.span - 1):
            out_ref[0, depth] = jnp.zeros((4, s.sticks), f32)
    else:
        out_ref[...] = total


def fetching_kernel(body, inputs, outs, count, *refs):
    sources, targets = refs[inputs : inputs + count], refs[inputs + count + outs : inputs + 2 * count + outs]
    copies = [pltpu.make_async_copy(sources[i], targets[i], refs[-1].at[i]) for i in range(count)]
    for copy in copies:
        copy.start()
    body(*refs[:inputs], *refs[inputs + count : inputs + count + outs], *refs[inputs + 2 * count + outs : -1])
    for copy in copies:
        copy.wait()


def places(s, sticks_ref, sources, x_ref, y_ref):
    at = 0
    for source in sources:
        columns = pl.ds(pl.multiple_of(source * s.sticks, s.sticks), s.sticks)
        shape = (s.rows_y, s.sticks)
        x_ref[:, at : at + s.sticks] = jnp.broadcast_to(sticks_ref[0:1, columns].astype(f32), shape).astype(bf16)
        row = lax.broadcasted_iota(jnp.int32, shape, 0) + 1 - s.radius
        hit = sticks_ref[1:2, columns] == row
        y_ref[:, at : at + s.sticks] = jnp.where(hit, 1.0, 0.0).astype(bf16)
        at += s.sticks


def one_hot(x, x_all, y_all):
    return jnp.where(x_all == jnp.asarray(x, bf16), y_all, jnp.zeros_like(y_all))


def lay_kernel(s, which, started, ended, *refs):
    in_refs, refs = refs[: len(which)], refs[len(which) :]
    before_ref, refs = (refs[0], refs[1:]) if started else (None, refs)
    sticks_ref, refs = refs[0], refs[1:]
    table_ref, out_ref, grid_ref = refs[:3] if ended else (None, None, refs[0])
    x_ref, y_ref, both_ref = refs[-3:]
    me = lax.axis_index("plane")
    places(s, sticks_ref, [partner(me, k) for k in which], x_ref, y_ref)
    rows = 2 * s.batch
    for i in range(len(which)):
        high, low = split(in_refs[i][...])
        both_ref[:rows, i * s.sticks : (i + 1) * s.sticks] = high
        both_ref[rows:, i * s.sticks : (i + 1) * s.sticks] = low
    lanes = 2 * s.rows_y
    for first in range(0, s.tiles, 2):
        count = min(2, s.tiles - first)
        hot = jnp.concatenate([one_hot(x, x_ref[...], y_ref[...]) for x in range(2 * first, 2 * (first + count))], 0)
        laid = lax.dot_general(both_ref[...], hot, (((1,), (1,)), ((), ())), preferred_element_type=f32)
        laid = laid[:rows] + laid[rows:]
        for t in range(count):
            for component in range(2):
                own = pl.ds((first + t) * s.batch, s.batch), slice(component * lanes, (component + 1) * lanes)
                part = laid[component * s.batch : (component + 1) * s.batch, t * lanes : (t + 1) * lanes]
                grid_ref[own] = part + before_ref[own] if started else part
    if not ended:
        return
    total = s.tiles * s.batch
    table = jnp.concatenate([table_ref[0], table_ref[0], table_ref[1]], 0)
    for start in range(0, total, 4 * s.batch):
        end = min(total, start + 4 * s.batch)
        sides = braid(grid_ref[start:end, :lanes], grid_ref[start:end, lanes:])
        high, low = split(jnp.concatenate(sides, 0))
        moved = dot(jnp.concatenate([high, low, high], 1), table)
        for t in range(4):
            for row in range(0, end - start, s.batch):
                at = (start + row) // s.batch * s.step
                own = t // 2 * (end - start) + row
                part = moved[own : own + s.batch, t % 2 * s.length : (t % 2 + 1) * s.length]
                out_ref[t, at : at + s.batch, :] = part
    for t in range(4):
        out_ref[t, s.tiles * s.step :, :] = jnp.zeros(((s.even - s.tiles) * s.step, s.length), f32)


def turn_kernel(s, bands, half_ref, x_ahead_ref, real_ref):
    width = s.length // bands
    last = pl.ds(pl.multiple_of(last_owner(bands) * width, width), width)
    table = jnp.concatenate([x_ahead_ref[...], x_ahead_ref[last, :]], 0)

    def plane(z, carry):
        parts = []
        for component in range(2):
            for parity in range(2):
                count = s.odd if parity else s.even
                parts.append(
                    jnp.concatenate(
                        [
                            half_ref[2 * parity + component, pl.ds(o * s.planes + z, count, stride=s.step), :]
                            for o in range(2)
                        ],
                        1,
                    )
                )
        high, low = split(jnp.concatenate(parts, 0))
        real_ref[z] = dot(table, jnp.concatenate([high, high, low], 0))
        return carry

    lax.fori_loop(0, s.planes, plane, 0, unroll=4)


def space_kernel(s, bands, real_ref, *refs):
    offsets = ring_offsets(bands)[:-2]
    slab_refs, (x_back_ref, turned_ref, field_ref) = refs[: len(offsets)], refs[len(offsets) :]
    width = s.length // bands
    band = lax.axis_index("band")
    at = place_on_ring(band, bands)
    for (offset, _, _), slab_ref in zip(offsets, slab_refs, strict=True):
        owner = band_on_ring(lax.rem(at + offset + bands, bands), bands)
        field_ref[:, pl.ds(pl.multiple_of(owner * width, width), width), :] = slab_ref[...]
    last = pl.ds(pl.multiple_of(last_owner(bands) * width, width), width)
    field_ref[:, last, :] = jnp.zeros((s.planes, width, s.length), f32)
    for t in range(2, 4):
        turned_ref[t, s.odd * s.step :, :] = jnp.zeros(((s.even - s.odd) * s.step, s.length), f32)

    def plane(z, carry):
        field = field_ref[z]
        high, low = split(real_ref[z, : s.length, :] * jnp.concatenate([field, field], 1))
        turned = dot(x_back_ref[...], jnp.concatenate([high, low], 0))
        keep_turned(s, turned_ref, z, turned[: s.kept] + turned[s.kept :])
        return carry

    lax.fori_loop(0, s.planes, plane, 0, unroll=4)


def keep_turned(s, turned_ref, z, turned):
    at = 0
    for component in range(2):
        for parity in range(2):
            count = s.odd if parity else s.even
            for o in range(2):
                turned_ref[2 * parity + component, pl.ds(o * s.planes + z, count, stride=s.step), :] = turned[
                    at : at + count, o * s.length : (o + 1) * s.length
                ]
            at += count


def finish_kernel(s, bands, half, first_ref, real_ref, slab_ref, x_last_ref, y_back_ref, flat_ref, turned_ref):
    for t in range(2, 4):
        turned_ref[t, s.odd * s.step :, :] = jnp.zeros(((s.even - s.odd) * s.step, s.length), f32)
    x_last = x_last_ref[last_owner(bands)]
    part = s.planes // 2

    def plane(z, carry):
        field = slab_ref[z]
        high, low = split(real_ref[half * part + z, s.length :, :] * jnp.concatenate([field, field], 1))
        keep_turned(s, turned_ref, half * part + z, dot(x_last, jnp.concatenate([high, low, high], 0)))
        return carry

    lax.fori_loop(0, part, plane, 0, unroll=4)

    lanes = 2 * s.rows_y
    for start in range(0, s.tiles, 8):
        end = min(s.tiles, start + 8)
        parts = []
        for parity in range(2):
            for tile in range(start, end):
                for o in range(2):
                    row = tile * s.step + o * s.planes + half * part
                    own = slice(row, row + part)
                    both = [first_ref[t, own, :] + turned_ref[t, own, :] for t in (2 * parity, 2 * parity + 1)]
                    parts.append(jnp.concatenate(both, 1))
        high, low = split(jnp.concatenate(parts, 0))
        moved = dot(jnp.concatenate([high, low], 1), y_back_ref[...])
        moved = moved[:, :lanes] + moved[:, lanes:]
        count = (end - start) * s.planes
        for component, value in enumerate(braid(moved[:count], moved[count:])):
            for row, piece in zip((component, 2 + component), split(value), strict=True):
                for tile in range(start, end):
                    at = (tile - start) * s.planes
                    flat_ref[row * s.planes : (row + 1) * s.planes, tile * lanes : (tile + 1) * lanes] = piece[
                        at : at + s.planes
                    ]


def pick_kernel(s, which, count, joined, *refs):
    flat_refs, sticks_ref, refs = refs[:count], refs[count], refs[count + 1 :]
    out_refs, (x_ref, y_ref, hot_ref) = refs[:-3], refs[-3:]
    me = lax.axis_index("plane")
    places(s, sticks_ref, [partner(me, k) for k in which], x_ref, y_ref)
    rows = 2 * s.planes
    flat = jnp.concatenate([flat_ref[...] for flat_ref in flat_refs], 0)
    for i in range(len(which)):
        columns = slice(i * s.sticks, (i + 1) * s.sticks)
        for x in range(2 * s.tiles):
            hot_ref[x * s.rows_y : (x + 1) * s.rows_y, :] = one_hot(x, x_ref[:, columns], y_ref[:, columns])
        found = dot(flat, hot_ref[...])
        for h in range(count):
            row = 2 * h * rows
            out_ref, at = (out_refs[0], (i * count + h) * rows) if joined else (out_refs[i], h * rows)
            out_ref[at : at + rows, :] = found[row : row + rows] + found[row + rows : row + 2 * rows]


def band_on_ring(place, count):
    return jnp.where(2 * place < count, 2 * place, 2 * (count - 1 - place) + 1)


def place_on_ring(band, count):
    return jnp.where(lax.rem(band, 2) == 0, band // 2, count - 1 - band // 2)


def last_owner(count):
    return band_on_ring(lax.rem(place_on_ring(lax.axis_index("band"), count) + count // 2, count), count)


def ring_offsets(count):
    offsets = [(0, 0, 2)]
    for step in range(1, count // 2 + 1):
        last = 2 * step == count
        offsets += [(-step, 0, 1 if last else 2), (step, 1 if last else 0, 2)]
    return offsets


def partners(devices):
    return sorted(range(1, devices), key=lambda k: (k == 1, k % 2, k))


def send_groups(devices):
    soon, *others, near = partners(devices)
    return [[soon, soon ^ 1], *(k for k in others if k != soon ^ 1), near]


def stages(devices):
    far = partners(devices)[:-1]
    return [("lay1", [0, 1]), ("lay2", far[:-1]), ("lay3", far[-1:])]


def per_device(bands, coeffs, potential, stick_map):
    devices = stick_map.shape[1] // coeffs.shape[3]
    s = Sizes(coeffs.shape[2], coeffs.shape[3], potential.shape[2], potential.shape[0], devices)
    tab = {name: jnp.asarray(value) for name, value in tables(s, bands).items()}
    rows = 2 * s.batch
    block = jax.ShapeDtypeStruct((rows, s.sticks), f32)

    order = list(range(0, bands, 2)) + list(range(bands - 1, 0, -2))
    along = [(order[i], order[(i + 1) % bands]) for i in range(bands)]
    against = [(b, a) for a, b in along]

    def exchange(blocks):
        out = [blocks[0]] + [None] * (devices - 1)
        for k in partners(devices):
            out[k] = lax.ppermute(blocks[k], "plane", [(i, i ^ k) for i in range(devices)])
        return out

    def ring():
        slabs = [potential]
        up = down = potential
        for step in range(1, bands // 2 + 1):
            last = 2 * step == bands
            if last:
                up, down = up[: s.planes // 2], down[s.planes // 2 :]
            up = lax.ppermute(up, "band", along)
            down = lax.ppermute(down, "band", against)
            slabs += [up, down]
        return slabs

    def kernel(body, inputs, out_shape, limit, flops, scratch_shapes=(), place=VMEM, fetched=()):
        single = not isinstance(out_shape, list)
        outs = [out_shape] if single else out_shape
        extra = [jax.ShapeDtypeStruct(a.shape, a.dtype) for a in fetched]
        if fetched:
            body = functools.partial(fetching_kernel, body, len(inputs), len(outs), len(fetched))
        results = pl.pallas_call(
            body,
            in_specs=[place] * len(inputs) + [HBM] * len(fetched),
            out_specs=[VMEM] * (len(outs) + len(fetched)),
            out_shape=outs + extra,
            scratch_shapes=[*scratch_shapes] + [pltpu.SemaphoreType.DMA((len(fetched),))] * bool(fetched),
            compiler_params=pltpu.CompilerParams(vmem_limit_bytes=limit << 10),
            cost_estimate=pl.CostEstimate(flops=flops, bytes_accessed=1 << 20, transcendentals=0),
        )(*inputs, *(pltpu.with_memory_space_constraint(a, pltpu.HBM) for a in fetched))
        if fetched:
            return results[: len(outs)], results[len(outs) :]
        return results[0] if single else results

    slabs = ring()
    positions = 2 * s.tiles * s.rows_y
    results = []
    for pair in range(coeffs.shape[0]):
        given = jnp.transpose(coeffs[pair : pair + 1], (0, 2, 1, 3))
        sent = kernel(
            functools.partial(ahead_kernel, s),
            [pltpu.with_memory_space_constraint(a, pltpu.HBM) for a in (given, stick_map, tab["z_ahead"])],
            [block] * devices,
            16 << 10,
            1 << 31,
            [
                pltpu.VMEM(given.shape, f32),
                pltpu.VMEM(stick_map.shape, jnp.int32),
                pltpu.VMEM(tab["z_ahead"].shape, bf16),
                pltpu.SemaphoreType.DMA((3,)),
            ],
            HBM,
        )
        held = exchange(sent)
        half = None
        ready = results
        later = ["y_ahead", "x_ahead", "x_back", "x_last", "y_back", "z_back"]
        grid_shape = (s.tiles * s.batch, 4 * s.rows_y)
        for name, which in stages(devices):
            started, ended = half is not None, name == "lay3"
            shape = (4, s.even * s.step, s.length) if ended else grid_shape
            own = [pltpu.VMEM((s.rows_y, len(which) * s.sticks), bf16)] * 2
            own.append(pltpu.VMEM((2 * rows, len(which) * s.sticks), bf16))
            fetch = [] if started or ready else [tab[key] for key in later] + [potential]
            half = kernel(
                functools.partial(lay_kernel, s, which, started, ended),
                [held[k] for k in which] + [half] * started + [stick_map] + [tab["y_ahead"]] * ended,
                jax.ShapeDtypeStruct(shape, f32),
                24 << 10,
                1 << 31,
                [pltpu.VMEM(grid_shape, f32)] * ended + own,
                fetched=fetch,
            )
            if fetch:
                (half,), (*ready, slabs[0]) = half
                tab.update(zip(later, ready, strict=True))
        turned_shape = (4, s.even * s.step, s.length)
        real = kernel(
            functools.partial(turn_kernel, s, bands),
            [half, tab["x_ahead"]],
            jax.ShapeDtypeStruct((s.planes, s.length + s.length // bands, 2 * s.length), f32),
            16 << 10,
            1 << 31,
        )
        turned = kernel(
            functools.partial(space_kernel, s, bands),
            [real, *slabs[:-2], tab["x_back"]],
            jax.ShapeDtypeStruct(turned_shape, f32),
            16 << 10,
            1 << 31,
            [pltpu.VMEM((s.planes, s.length, s.length), f32)],
        )
        flats = [
            kernel(
                functools.partial(finish_kernel, s, bands, half),
                [turned, real, slabs[half - 2], tab["x_last"], tab["y_back"]],
                jax.ShapeDtypeStruct((4 * s.planes, positions), bf16),
                20 << 10,
                1 << 31,
                [pltpu.VMEM(turned_shape, f32)],
            )
            for half in range(2)
        ]

        def pick(which, flats, joined=False):
            size = len(flats) * 2 * s.planes
            shape = jax.ShapeDtypeStruct((size * len(which) if joined else size, s.sticks), f32)
            return kernel(
                functools.partial(pick_kernel, s, which, len(flats), joined),
                [*flats, stick_map],
                [shape] if joined else [shape] * len(which),
                16 << 10,
                1 << 31,
                [
                    pltpu.VMEM((s.rows_y, len(which) * s.sticks), bf16),
                    pltpu.VMEM((s.rows_y, len(which) * s.sticks), bf16),
                    pltpu.VMEM((positions, s.sticks), bf16),
                ],
            )

        def send(k, block):
            return lax.ppermute(block, "plane", [(i, i ^ k) for i in range(devices)])

        (soon, across), *others, near = send_groups(devices)
        both = send(soon, *pick([across, soon], [flats[0]], True))
        hop, last = pick([across, soon], [flats[1]])
        hop = send(across, hop)
        last = send(soon, last)
        returned = [(k, None, 0, send(k, *pick([k], flats))) for k in others]
        beside, own = pick([near, 0], flats)
        returned += [(near, None, 0, send(near, beside)), (0, None, 0, own), (soon, 0, s.batch, both)]
        late = [(across, 0, 0, send(near, both[: s.batch]))]
        late += [(across, 1, 0, hop), (soon, 1, 0, last)]
        begun = kernel(
            functools.partial(back_kernel, s, [block[:3] for block in returned], False, False),
            [*(block[3] for block in returned), tab["z_back"]],
            jax.ShapeDtypeStruct((s.depth_rows, s.sticks), f32),
            16 << 10,
            1 << 31,
        )
        result = kernel(
            functools.partial(back_kernel, s, [block[:3] for block in late], True, True),
            [*(block[3] for block in late), begun, stick_map, tab["z_back"]],
            jax.ShapeDtypeStruct((1,) + given.shape[1:], f32),
            16 << 10,
            1 << 31,
        )
        results.append(jnp.transpose(result, (0, 2, 1, 3)))
    return results[0] if len(results) == 1 else jnp.concatenate(results, 0)


def solution(mesh):
    placed = (P("band", None, None, "plane"), P("plane", "band", None), P())
    return jax.shard_map(
        functools.partial(per_device, mesh.shape["band"]),
        mesh=mesh,
        in_specs=placed,
        out_specs=P("band", None, None, "plane"),
        check_vma=False,
    )
```

```python
import functools
import math

import jax
import jax.numpy as jnp
import ml_dtypes
import numpy as np
from jax import lax
from jax.experimental import pallas as pl
from jax.experimental.pallas import tpu as pltpu
from jax.sharding import PartitionSpec as P


bf16 = jnp.bfloat16
f32 = jnp.float32
VMEM = pl.BlockSpec(memory_space=pltpu.VMEM)
HBM = pl.BlockSpec(memory_space=pltpu.HBM)


def up8(n):
    return -(-n // 8) * 8


def halves(table):
    high = table.astype(ml_dtypes.bfloat16)
    return high, (table - high.astype(np.float64)).astype(ml_dtypes.bfloat16)


def split(value):
    high = value.astype(bf16)
    return high, (value - high.astype(f32)).astype(bf16)


class Sizes:
    def __init__(self, span, sticks, length, planes, devices):
        self.span, self.length, self.planes, self.devices = span, length, planes, devices
        self.sticks = sticks
        self.radius = (span - 1) // 2
        self.rows_y = 2 * self.radius
        self.tiles = self.radius // 2 + 1
        self.even = up8(self.tiles)
        self.odd = up8(self.radius // 2)
        self.kept = 2 * (self.even + self.odd)
        self.batch = 2 * planes
        self.step = self.batch + 1
        self.depths = span - 2
        self.depth_rows = -(-4 * self.depths // 16) * 16


def tables(s, bands):
    turn = 2.0 * math.pi / s.length
    grid = np.arange(s.length)
    depth = np.arange(s.depths) + 1 - s.radius
    y = np.arange(s.rows_y) + 1 - s.radius

    def trig(left, right):
        angle = turn * np.mod(np.outer(left, right), s.length)
        return np.cos(angle), np.sin(angle)

    cos, sin = trig(depth, grid)
    ahead = np.zeros((s.devices, 2, 2, s.planes, s.depths, 2, 2))
    back = np.zeros((s.devices, s.depths, 2, 2, 2, 2, s.planes))
    scale = 1.0 / float(s.length) ** 3
    for d in range(s.devices):
        own = slice(d * s.planes, (d + 1) * s.planes)
        c, n = cos[:, own], sin[:, own]
        for o in range(2):
            ahead[d, 0, o, :, :, o, 0] = c.T
            ahead[d, 0, o, :, :, o, 1] = -n.T
            ahead[d, 1, o, :, :, o, 0] = n.T
            ahead[d, 1, o, :, :, o, 1] = c.T
            back[d, :, o, 0, 0, o] = c * scale
            back[d, :, o, 0, 1, o] = n * scale
            back[d, :, o, 1, 0, o] = -n * scale
            back[d, :, o, 1, 1, o] = c * scale
    gap = s.depth_rows - 4 * s.depths
    ahead = np.pad(ahead.reshape(s.devices, 2 * s.batch, 4 * s.depths), ((0, 0), (0, 0), (0, gap)))
    back = back.reshape(s.devices, 4 * s.depths, 4, 2, s.planes // 2).transpose(0, 1, 3, 2, 4)
    back = np.pad(back.reshape(s.devices, 4 * s.depths, 2 * s.batch), ((0, 0), (0, gap), (0, 0)))

    cos, sin = trig(y, grid)
    y_ahead = np.stack([np.stack([cos, sin], 1), np.stack([-sin, cos], 1)]).reshape(2 * s.rows_y, 2 * s.length)
    y_back = np.stack([np.stack([cos.T, -sin.T], 1), np.stack([sin.T, cos.T], 1)]).reshape(2 * s.length, 2 * s.rows_y)

    x_ahead = np.zeros((s.length, s.kept))
    x_back = np.zeros((s.kept, s.length))
    at = 0
    for component in range(2):
        for parity in range(2):
            count = s.tiles if parity == 0 else s.radius // 2
            cos, sin = trig(2 * np.arange(count) + parity, grid)
            x_ahead[:, at : at + count] = 2.0 * cos.T if component == 0 else -2.0 * sin.T
            x_back[at : at + count] = cos if component == 0 else -sin
            at += s.even if parity == 0 else s.odd

    def beside(table, axis, order):
        parts = halves(table)
        return np.concatenate([parts[i] for i in order], axis)

    def folded(table, axis):
        high, low = halves(table)
        zero = np.zeros(table.shape, ml_dtypes.bfloat16)
        first, second = (high, high), (low, zero)
        return np.concatenate([np.concatenate(first, 1 - axis), np.concatenate(second, 1 - axis)], axis)

    by_slab = x_back.reshape(s.kept, bands, s.length // bands).transpose(1, 0, 2)
    return dict(
        z_ahead=beside(ahead, 2, (0, 1)),
        z_back=beside(back, 2, (0, 1)),
        y_ahead=np.stack(halves(y_ahead)),
        y_back=folded(y_back, 1),
        x_ahead=beside(x_ahead, 1, (0, 1, 0)),
        x_last=beside(by_slab, 2, (0, 0, 1)),
        x_back=folded(x_back, 0),
    )


def braid(left, right):
    half = left.shape[1] // 2
    first = lax.broadcasted_iota(jnp.int32, left.shape, 1) < half
    return jnp.where(first, left, pltpu.roll(right, half, 1)), jnp.where(first, pltpu.roll(left, half, 1), right)


def dot(left, right):
    return jnp.dot(left, right, preferred_element_type=f32)


def partner(me, k):
    return jnp.bitwise_xor(me, k)


def live_of(s, sticks_ref, source):
    columns = pl.ds(pl.multiple_of(source * s.sticks, s.sticks), s.sticks)
    depth = lax.broadcasted_iota(jnp.int32, (4 * s.depths, s.sticks), 0) // 4 + 1 - s.radius
    return jnp.abs(depth) <= sticks_ref[2:3, columns]


def ahead_kernel(s, coeffs_hbm, sticks_hbm, table_hbm, *refs):
    out_refs, (coeffs_ref, sticks_ref, table_ref, sems) = refs[: s.devices], refs[s.devices :]
    pairs = [(sticks_hbm, sticks_ref), (coeffs_hbm, coeffs_ref), (table_hbm, table_ref)]
    copies = [pltpu.make_async_copy(source, target, sems.at[i]) for i, (source, target) in enumerate(pairs)]
    for copy in copies:
        copy.start()
    me = lax.axis_index("plane")
    copies[0].wait()
    live = live_of(s, sticks_ref, me)
    copies[1].wait()
    data = jnp.where(live, coeffs_ref[0, 1 : s.span - 1].reshape(4 * s.depths, s.sticks), 0.0)
    gap = jnp.zeros((s.depth_rows - 4 * s.depths, s.sticks), f32)
    high, low = split(jnp.concatenate([data, gap], 0))
    data = jnp.concatenate([high, high, low], 0)
    copies[2].wait()
    for k in [*partners(s.devices), 0]:
        table = table_ref[partner(me, k)]
        out_refs[k][...] = dot(jnp.concatenate([table, table[:, : s.depth_rows]], 1), data)


def back_kernel(s, which, started, ended, *refs):
    in_refs, refs = refs[: len(which)], refs[len(which) :]
    table_ref, out_ref = refs[-2:]
    part = jnp.zeros((s.batch, s.sticks), f32)
    me = lax.axis_index("plane")
    total = refs[0][...] if started else None
    blocks = {}
    for (k, half, row), ref in zip(which, in_refs, strict=True):
        if half is None:
            blocks[k] = ref[...]
        else:
            blocks.setdefault(k, [part, part])[half] = ref[row : row + s.batch, :]
    for k, block in blocks.items():
        high, low = split(jnp.concatenate(block, 0) if isinstance(block, list) else block)
        table = table_ref[partner(me, k)]
        table = jnp.concatenate([table, table[:, : 2 * s.batch]], 1)
        term = dot(table, jnp.concatenate([high, high, low], 0))
        total = term if total is None else total + term
    if ended:
        total = jnp.where(live_of(s, refs[-3], me), total[: 4 * s.depths], 0.0)
        out_ref[0, 1 : s.span - 1] = total.reshape(s.depths, 4, s.sticks)
        for depth in (0, s.span - 1):
            out_ref[0, depth] = jnp.zeros((4, s.sticks), f32)
    else:
        out_ref[...] = total


def fetching_kernel(body, inputs, outs, count, *refs):
    sources, targets = refs[inputs : inputs + count], refs[inputs + count + outs : inputs + 2 * count + outs]
    copies = [pltpu.make_async_copy(sources[i], targets[i], refs[-1].at[i]) for i in range(count)]
    for copy in copies:
        copy.start()
    body(*refs[:inputs], *refs[inputs + count : inputs + count + outs], *refs[inputs + 2 * count + outs : -1])
    for copy in copies:
        copy.wait()


def places(s, sticks_ref, sources, x_ref, y_ref):
    at = 0
    for source in sources:
        columns = pl.ds(pl.multiple_of(source * s.sticks, s.sticks), s.sticks)
        shape = (s.rows_y, s.sticks)
        x_ref[:, at : at + s.sticks] = jnp.broadcast_to(sticks_ref[0:1, columns].astype(f32), shape).astype(bf16)
        row = lax.broadcasted_iota(jnp.int32, shape, 0) + 1 - s.radius
        hit = sticks_ref[1:2, columns] == row
        y_ref[:, at : at + s.sticks] = jnp.where(hit, 1.0, 0.0).astype(bf16)
        at += s.sticks


def one_hot(x, x_all, y_all):
    return jnp.where(x_all == jnp.asarray(x, bf16), y_all, jnp.zeros_like(y_all))


def lay_kernel(s, which, started, ended, *refs):
    in_refs, refs = refs[: len(which)], refs[len(which) :]
    before_ref, refs = (refs[0], refs[1:]) if started else (None, refs)
    sticks_ref, refs = refs[0], refs[1:]
    table_ref, out_ref, grid_ref = refs[:3] if ended else (None, None, refs[0])
    x_ref, y_ref, both_ref = refs[-3:]
    me = lax.axis_index("plane")
    places(s, sticks_ref, [partner(me, k) for k in which], x_ref, y_ref)
    rows = 2 * s.batch
    for i in range(len(which)):
        high, low = split(in_refs[i][...])
        both_ref[:rows, i * s.sticks : (i + 1) * s.sticks] = high
        both_ref[rows:, i * s.sticks : (i + 1) * s.sticks] = low
    lanes = 2 * s.rows_y
    for first in range(0, s.tiles, 2):
        count = min(2, s.tiles - first)
        hot = jnp.concatenate([one_hot(x, x_ref[...], y_ref[...]) for x in range(2 * first, 2 * (first + count))], 0)
        laid = lax.dot_general(both_ref[...], hot, (((1,), (1,)), ((), ())), preferred_element_type=f32)
        laid = laid[:rows] + laid[rows:]
        for t in range(count):
            for component in range(2):
                own = pl.ds((first + t) * s.batch, s.batch), slice(component * lanes, (component + 1) * lanes)
                part = laid[component * s.batch : (component + 1) * s.batch, t * lanes : (t + 1) * lanes]
                grid_ref[own] = part + before_ref[own] if started else part
    if not ended:
        return
    total = s.tiles * s.batch
    table = jnp.concatenate([table_ref[0], table_ref[0], table_ref[1]], 0)
    for start in range(0, total, 4 * s.batch):
        end = min(total, start + 4 * s.batch)
        sides = braid(grid_ref[start:end, :lanes], grid_ref[start:end, lanes:])
        high, low = split(jnp.concatenate(sides, 0))
        moved = dot(jnp.concatenate([high, low, high], 1), table)
        for t in range(4):
            for row in range(0, end - start, s.batch):
                at = (start + row) // s.batch * s.step
                own = t // 2 * (end - start) + row
                part = moved[own : own + s.batch, t % 2 * s.length : (t % 2 + 1) * s.length]
                out_ref[t, at : at + s.batch, :] = part
    for t in range(4):
        out_ref[t, s.tiles * s.step :, :] = jnp.zeros(((s.even - s.tiles) * s.step, s.length), f32)


def turn_kernel(s, bands, half_ref, x_ahead_ref, real_ref):
    width = s.length // bands
    last = pl.ds(pl.multiple_of(last_owner(bands) * width, width), width)
    table = jnp.concatenate([x_ahead_ref[...], x_ahead_ref[last, :]], 0)

    def plane(z, carry):
        parts = []
        for component in range(2):
            for parity in range(2):
                count = s.odd if parity else s.even
                parts.append(
                    jnp.concatenate(
                        [
                            half_ref[2 * parity + component, pl.ds(o * s.planes + z, count, stride=s.step), :]
                            for o in range(2)
                        ],
                        1,
                    )
                )
        high, low = split(jnp.concatenate(parts, 0))
        real_ref[z] = dot(table, jnp.concatenate([high, high, low], 0))
        return carry

    lax.fori_loop(0, s.planes, plane, 0, unroll=s.planes)


def space_kernel(s, bands, real_ref, *refs):
    offsets = ring_offsets(bands)[:-2]
    slab_refs, (x_back_ref, turned_ref, field_ref) = refs[: len(offsets)], refs[len(offsets) :]
    width = s.length // bands
    band = lax.axis_index("band")
    at = place_on_ring(band, bands)
    for (offset, _, _), slab_ref in zip(offsets, slab_refs, strict=True):
        owner = band_on_ring(lax.rem(at + offset + bands, bands), bands)
        field_ref[:, pl.ds(pl.multiple_of(owner * width, width), width), :] = slab_ref[...]
    last = pl.ds(pl.multiple_of(last_owner(bands) * width, width), width)
    field_ref[:, last, :] = jnp.zeros((s.planes, width, s.length), f32)
    for t in range(2, 4):
        turned_ref[t, s.odd * s.step :, :] = jnp.zeros(((s.even - s.odd) * s.step, s.length), f32)

    def plane(z, carry):
        field = field_ref[z]
        high, low = split(real_ref[z, : s.length, :] * jnp.concatenate([field, field], 1))
        turned = dot(x_back_ref[...], jnp.concatenate([high, low], 0))
        keep_turned(s, turned_ref, z, turned[: s.kept] + turned[s.kept :])
        return carry

    lax.fori_loop(0, s.planes, plane, 0, unroll=s.planes)


def keep_turned(s, turned_ref, z, turned):
    at = 0
    for component in range(2):
        for parity in range(2):
            count = s.odd if parity else s.even
            for o in range(2):
                turned_ref[2 * parity + component, pl.ds(o * s.planes + z, count, stride=s.step), :] = turned[
                    at : at + count, o * s.length : (o + 1) * s.length
                ]
            at += count


def finish_kernel(s, bands, half, first_ref, real_ref, slab_ref, x_last_ref, y_back_ref, flat_ref, turned_ref):
    for t in range(2, 4):
        turned_ref[t, s.odd * s.step :, :] = jnp.zeros(((s.even - s.odd) * s.step, s.length), f32)
    x_last = x_last_ref[last_owner(bands)]
    part = s.planes // 2

    def plane(z, carry):
        field = slab_ref[z]
        high, low = split(real_ref[half * part + z, s.length :, :] * jnp.concatenate([field, field], 1))
        keep_turned(s, turned_ref, half * part + z, dot(x_last, jnp.concatenate([high, low, high], 0)))
        return carry

    lax.fori_loop(0, part, plane, 0, unroll=part)

    lanes = 2 * s.rows_y
    for start in range(0, s.tiles, 8):
        end = min(s.tiles, start + 8)
        parts = []
        for parity in range(2):
            for tile in range(start, end):
                for o in range(2):
                    row = tile * s.step + o * s.planes + half * part
                    own = slice(row, row + part)
                    both = [first_ref[t, own, :] + turned_ref[t, own, :] for t in (2 * parity, 2 * parity + 1)]
                    parts.append(jnp.concatenate(both, 1))
        high, low = split(jnp.concatenate(parts, 0))
        moved = dot(jnp.concatenate([high, low], 1), y_back_ref[...])
        moved = moved[:, :lanes] + moved[:, lanes:]
        count = (end - start) * s.planes
        for component, value in enumerate(braid(moved[:count], moved[count:])):
            for row, piece in zip((component, 2 + component), split(value), strict=True):
                for tile in range(start, end):
                    at = (tile - start) * s.planes
                    flat_ref[row * s.planes : (row + 1) * s.planes, tile * lanes : (tile + 1) * lanes] = piece[
                        at : at + s.planes
                    ]


def pick_kernel(s, which, count, joined, *refs):
    flat_refs, sticks_ref, refs = refs[:count], refs[count], refs[count + 1 :]
    out_refs, (x_ref, y_ref, hot_ref) = refs[:-3], refs[-3:]
    me = lax.axis_index("plane")
    places(s, sticks_ref, [partner(me, k) for k in which], x_ref, y_ref)
    rows = 2 * s.planes
    flat = jnp.concatenate([flat_ref[...] for flat_ref in flat_refs], 0)
    for i in range(len(which)):
        columns = slice(i * s.sticks, (i + 1) * s.sticks)
        for x in range(2 * s.tiles):
            hot_ref[x * s.rows_y : (x + 1) * s.rows_y, :] = one_hot(x, x_ref[:, columns], y_ref[:, columns])
        found = dot(flat, hot_ref[...])
        for h in range(count):
            row = 2 * h * rows
            out_ref, at = (out_refs[0], (i * count + h) * rows) if joined else (out_refs[i], h * rows)
            out_ref[at : at + rows, :] = found[row : row + rows] + found[row + rows : row + 2 * rows]


def band_on_ring(place, count):
    return jnp.where(2 * place < count, 2 * place, 2 * (count - 1 - place) + 1)


def place_on_ring(band, count):
    return jnp.where(lax.rem(band, 2) == 0, band // 2, count - 1 - band // 2)


def last_owner(count):
    return band_on_ring(lax.rem(place_on_ring(lax.axis_index("band"), count) + count // 2, count), count)


def ring_offsets(count):
    offsets = [(0, 0, 2)]
    for step in range(1, count // 2 + 1):
        last = 2 * step == count
        offsets += [(-step, 0, 1 if last else 2), (step, 1 if last else 0, 2)]
    return offsets


def partners(devices):
    return sorted(range(1, devices), key=lambda k: (k == 1, k % 2, k))


def send_groups(devices):
    soon, *others, near = partners(devices)
    return [[soon, soon ^ 1], *(k for k in others if k != soon ^ 1), near]


def stages(devices):
    far = partners(devices)[:-1]
    return [("lay1", [0, 1]), ("lay2", far[:-1]), ("lay3", far[-1:])]


def per_device(bands, coeffs, potential, stick_map):
    devices = stick_map.shape[1] // coeffs.shape[3]
    s = Sizes(coeffs.shape[2], coeffs.shape[3], potential.shape[2], potential.shape[0], devices)
    tab = {name: jnp.asarray(value) for name, value in tables(s, bands).items()}
    rows = 2 * s.batch
    block = jax.ShapeDtypeStruct((rows, s.sticks), f32)

    order = list(range(0, bands, 2)) + list(range(bands - 1, 0, -2))
    along = [(order[i], order[(i + 1) % bands]) for i in range(bands)]
    against = [(b, a) for a, b in along]

    def exchange(blocks):
        out = [blocks[0]] + [None] * (devices - 1)
        for k in partners(devices):
            out[k] = lax.ppermute(blocks[k], "plane", [(i, i ^ k) for i in range(devices)])
        return out

    def ring():
        slabs = [potential]
        up = down = potential
        for step in range(1, bands // 2 + 1):
            last = 2 * step == bands
            if last:
                up, down = up[: s.planes // 2], down[s.planes // 2 :]
            up = lax.ppermute(up, "band", along)
            down = lax.ppermute(down, "band", against)
            slabs += [up, down]
        return slabs

    def kernel(body, inputs, out_shape, limit, flops, scratch_shapes=(), place=VMEM, fetched=()):
        single = not isinstance(out_shape, list)
        outs = [out_shape] if single else out_shape
        extra = [jax.ShapeDtypeStruct(a.shape, a.dtype) for a in fetched]
        if fetched:
            body = functools.partial(fetching_kernel, body, len(inputs), len(outs), len(fetched))
        results = pl.pallas_call(
            body,
            in_specs=[place] * len(inputs) + [HBM] * len(fetched),
            out_specs=[VMEM] * (len(outs) + len(fetched)),
            out_shape=outs + extra,
            scratch_shapes=[*scratch_shapes] + [pltpu.SemaphoreType.DMA((len(fetched),))] * bool(fetched),
            compiler_params=pltpu.CompilerParams(vmem_limit_bytes=limit << 10),
            cost_estimate=pl.CostEstimate(flops=flops, bytes_accessed=1 << 20, transcendentals=0),
        )(*inputs, *(pltpu.with_memory_space_constraint(a, pltpu.HBM) for a in fetched))
        if fetched:
            return results[: len(outs)], results[len(outs) :]
        return results[0] if single else results

    slabs = ring()
    positions = 2 * s.tiles * s.rows_y
    results = []
    for pair in range(coeffs.shape[0]):
        given = jnp.transpose(coeffs[pair : pair + 1], (0, 2, 1, 3))
        sent = kernel(
            functools.partial(ahead_kernel, s),
            [pltpu.with_memory_space_constraint(a, pltpu.HBM) for a in (given, stick_map, tab["z_ahead"])],
            [block] * devices,
            16 << 10,
            1 << 31,
            [
                pltpu.VMEM(given.shape, f32),
                pltpu.VMEM(stick_map.shape, jnp.int32),
                pltpu.VMEM(tab["z_ahead"].shape, bf16),
                pltpu.SemaphoreType.DMA((3,)),
            ],
            HBM,
        )
        held = exchange(sent)
        half = None
        ready = results
        later = ["y_ahead", "x_ahead", "x_back", "x_last", "y_back", "z_back"]
        grid_shape = (s.tiles * s.batch, 4 * s.rows_y)
        for name, which in stages(devices):
            started, ended = half is not None, name == "lay3"
            shape = (4, s.even * s.step, s.length) if ended else grid_shape
            own = [pltpu.VMEM((s.rows_y, len(which) * s.sticks), bf16)] * 2
            own.append(pltpu.VMEM((2 * rows, len(which) * s.sticks), bf16))
            fetch = [] if started or ready else [tab[key] for key in later] + [potential]
            half = kernel(
                functools.partial(lay_kernel, s, which, started, ended),
                [held[k] for k in which] + [half] * started + [stick_map] + [tab["y_ahead"]] * ended,
                jax.ShapeDtypeStruct(shape, f32),
                24 << 10,
                1 << 31,
                [pltpu.VMEM(grid_shape, f32)] * ended + own,
                fetched=fetch,
            )
            if fetch:
                (half,), (*ready, slabs[0]) = half
                tab.update(zip(later, ready, strict=True))
        turned_shape = (4, s.even * s.step, s.length)
        real = kernel(
            functools.partial(turn_kernel, s, bands),
            [half, tab["x_ahead"]],
            jax.ShapeDtypeStruct((s.planes, s.length + s.length // bands, 2 * s.length), f32),
            16 << 10,
            1 << 31,
        )
        turned = kernel(
            functools.partial(space_kernel, s, bands),
            [real, *slabs[:-2], tab["x_back"]],
            jax.ShapeDtypeStruct(turned_shape, f32),
            16 << 10,
            1 << 31,
            [pltpu.VMEM((s.planes, s.length, s.length), f32)],
        )
        flats = [
            kernel(
                functools.partial(finish_kernel, s, bands, half),
                [turned, real, slabs[half - 2], tab["x_last"], tab["y_back"]],
                jax.ShapeDtypeStruct((4 * s.planes, positions), bf16),
                20 << 10,
                1 << 31,
                [pltpu.VMEM(turned_shape, f32)],
            )
            for half in range(2)
        ]

        def pick(which, flats, joined=False):
            size = len(flats) * 2 * s.planes
            shape = jax.ShapeDtypeStruct((size * len(which) if joined else size, s.sticks), f32)
            return kernel(
                functools.partial(pick_kernel, s, which, len(flats), joined),
                [*flats, stick_map],
                [shape] if joined else [shape] * len(which),
                16 << 10,
                1 << 31,
                [
                    pltpu.VMEM((s.rows_y, len(which) * s.sticks), bf16),
                    pltpu.VMEM((s.rows_y, len(which) * s.sticks), bf16),
                    pltpu.VMEM((positions, s.sticks), bf16),
                ],
            )

        def send(k, block):
            return lax.ppermute(block, "plane", [(i, i ^ k) for i in range(devices)])

        (soon, across), *others, near = send_groups(devices)
        both = send(soon, *pick([across, soon], [flats[0]], True))
        hop, last = pick([across, soon], [flats[1]])
        hop = send(across, hop)
        last = send(soon, last)
        returned = [(k, None, 0, send(k, *pick([k], flats))) for k in others]
        beside, own = pick([near, 0], flats)
        returned += [(near, None, 0, send(near, beside)), (0, None, 0, own), (soon, 0, s.batch, both)]
        late = [(across, 0, 0, send(near, both[: s.batch]))]
        late += [(across, 1, 0, hop), (soon, 1, 0, last)]
        begun = kernel(
            functools.partial(back_kernel, s, [block[:3] for block in returned], False, False),
            [*(block[3] for block in returned), tab["z_back"]],
            jax.ShapeDtypeStruct((s.depth_rows, s.sticks), f32),
            16 << 10,
            1 << 31,
        )
        result = kernel(
            functools.partial(back_kernel, s, [block[:3] for block in late], True, True),
            [*(block[3] for block in late), begun, stick_map, tab["z_back"]],
            jax.ShapeDtypeStruct((1,) + given.shape[1:], f32),
            16 << 10,
            1 << 31,
        )
        results.append(jnp.transpose(result, (0, 2, 1, 3)))
    return results[0] if len(results) == 1 else jnp.concatenate(results, 0)


def solution(mesh):
    placed = (P("band", None, None, "plane"), P("plane", "band", None), P())
    return jax.shard_map(
        functools.partial(per_device, mesh.shape["band"]),
        mesh=mesh,
        in_specs=placed,
        out_specs=P("band", None, None, "plane"),
        check_vma=False,
    )
```

```python
import functools
import math

import jax
import jax.numpy as jnp
import ml_dtypes
import numpy as np
from jax import lax
from jax.experimental import pallas as pl
from jax.experimental.pallas import tpu as pltpu
from jax.sharding import PartitionSpec as P


bf16 = jnp.bfloat16
f32 = jnp.float32
VMEM = pl.BlockSpec(memory_space=pltpu.VMEM)
HBM = pl.BlockSpec(memory_space=pltpu.HBM)


def up8(n):
    return -(-n // 8) * 8


def halves(table):
    high = table.astype(ml_dtypes.bfloat16)
    return high, (table - high.astype(np.float64)).astype(ml_dtypes.bfloat16)


def split(value):
    high = value.astype(bf16)
    return high, (value - high.astype(f32)).astype(bf16)


class Sizes:
    def __init__(self, span, sticks, length, planes, devices):
        self.span, self.length, self.planes, self.devices = span, length, planes, devices
        self.sticks = sticks
        self.radius = (span - 1) // 2
        self.rows_y = 2 * self.radius
        self.tiles = self.radius // 2 + 1
        self.even = up8(self.tiles)
        self.odd = up8(self.radius // 2)
        self.kept = 2 * (self.even + self.odd)
        self.batch = 2 * planes
        self.step = self.batch + 1
        self.depths = span - 2
        self.depth_rows = -(-4 * self.depths // 16) * 16


def tables(s, bands):
    turn = 2.0 * math.pi / s.length
    grid = np.arange(s.length)
    depth = np.arange(s.depths) + 1 - s.radius
    y = np.arange(s.rows_y) + 1 - s.radius

    def trig(left, right):
        angle = turn * np.mod(np.outer(left, right), s.length)
        return np.cos(angle), np.sin(angle)

    cos, sin = trig(depth, grid)
    ahead = np.zeros((s.devices, 2, 2, s.planes, s.depths, 2, 2))
    back = np.zeros((s.devices, s.depths, 2, 2, 2, 2, s.planes))
    scale = 1.0 / float(s.length) ** 3
    for d in range(s.devices):
        own = slice(d * s.planes, (d + 1) * s.planes)
        c, n = cos[:, own], sin[:, own]
        for o in range(2):
            ahead[d, 0, o, :, :, o, 0] = c.T
            ahead[d, 0, o, :, :, o, 1] = -n.T
            ahead[d, 1, o, :, :, o, 0] = n.T
            ahead[d, 1, o, :, :, o, 1] = c.T
            back[d, :, o, 0, 0, o] = c * scale
            back[d, :, o, 0, 1, o] = n * scale
            back[d, :, o, 1, 0, o] = -n * scale
            back[d, :, o, 1, 1, o] = c * scale
    gap = s.depth_rows - 4 * s.depths
    ahead = np.pad(ahead.reshape(s.devices, 2 * s.batch, 4 * s.depths), ((0, 0), (0, 0), (0, gap)))
    back = back.reshape(s.devices, 4 * s.depths, 4, 2, s.planes // 2).transpose(0, 1, 3, 2, 4)
    back = np.pad(back.reshape(s.devices, 4 * s.depths, 2 * s.batch), ((0, 0), (0, gap), (0, 0)))

    cos, sin = trig(y, grid)
    y_ahead = np.stack([np.stack([cos, sin], 1), np.stack([-sin, cos], 1)]).reshape(2 * s.rows_y, 2 * s.length)
    y_back = np.stack([np.stack([cos.T, -sin.T], 1), np.stack([sin.T, cos.T], 1)]).reshape(2 * s.length, 2 * s.rows_y)

    x_ahead = np.zeros((s.length, s.kept))
    x_back = np.zeros((s.kept, s.length))
    at = 0
    for component in range(2):
        for parity in range(2):
            count = s.tiles if parity == 0 else s.radius // 2
            cos, sin = trig(2 * np.arange(count) + parity, grid)
            x_ahead[:, at : at + count] = 2.0 * cos.T if component == 0 else -2.0 * sin.T
            x_back[at : at + count] = cos if component == 0 else -sin
            at += s.even if parity == 0 else s.odd

    def beside(table, axis, order):
        parts = halves(table)
        return np.concatenate([parts[i] for i in order], axis)

    def folded(table, axis):
        high, low = halves(table)
        zero = np.zeros(table.shape, ml_dtypes.bfloat16)
        first, second = (high, high), (low, zero)
        return np.concatenate([np.concatenate(first, 1 - axis), np.concatenate(second, 1 - axis)], axis)

    by_slab = x_back.reshape(s.kept, bands, s.length // bands).transpose(1, 0, 2)
    return dict(
        z_ahead=beside(ahead, 2, (0, 1)),
        z_back=beside(back, 2, (0, 1)),
        y_ahead=np.stack(halves(y_ahead)),
        y_back=folded(y_back, 1),
        x_ahead=beside(x_ahead, 1, (0, 1, 0)),
        x_last=beside(by_slab, 2, (0, 0, 1)),
        x_back=folded(x_back, 0),
    )


def braid(left, right):
    half = left.shape[1] // 2
    first = lax.broadcasted_iota(jnp.int32, left.shape, 1) < half
    return jnp.where(first, left, pltpu.roll(right, half, 1)), jnp.where(first, pltpu.roll(left, half, 1), right)


def dot(left, right):
    return jnp.dot(left, right, preferred_element_type=f32)


def partner(me, k):
    return jnp.bitwise_xor(me, k)


def live_of(s, sticks_ref, source):
    columns = pl.ds(pl.multiple_of(source * s.sticks, s.sticks), s.sticks)
    depth = lax.broadcasted_iota(jnp.int32, (4 * s.depths, s.sticks), 0) // 4 + 1 - s.radius
    return jnp.abs(depth) <= sticks_ref[2:3, columns]


def ahead_kernel(s, coeffs_hbm, sticks_hbm, table_hbm, *refs):
    out_refs, (coeffs_ref, sticks_ref, table_ref, sems) = refs[: s.devices], refs[s.devices :]
    pairs = [(sticks_hbm, sticks_ref), (coeffs_hbm, coeffs_ref), (table_hbm, table_ref)]
    copies = [pltpu.make_async_copy(source, target, sems.at[i]) for i, (source, target) in enumerate(pairs)]
    for copy in copies:
        copy.start()
    me = lax.axis_index("plane")
    copies[0].wait()
    live = live_of(s, sticks_ref, me)
    copies[1].wait()
    data = jnp.where(live, coeffs_ref[0, 1 : s.span - 1].reshape(4 * s.depths, s.sticks), 0.0)
    gap = jnp.zeros((s.depth_rows - 4 * s.depths, s.sticks), f32)
    high, low = split(jnp.concatenate([data, gap], 0))
    data = jnp.concatenate([high, high, low], 0)
    copies[2].wait()
    for k in [*partners(s.devices), 0]:
        table = table_ref[partner(me, k)]
        out_refs[k][...] = dot(jnp.concatenate([table, table[:, : s.depth_rows]], 1), data)


def back_kernel(s, which, started, ended, *refs):
    in_refs, refs = refs[: len(which)], refs[len(which) :]
    table_ref, out_ref = refs[len(refs) - 4 : len(refs) - 2] if ended else refs[-2:]
    part = jnp.zeros((s.batch, s.sticks), f32)
    me = lax.axis_index("plane")
    blocks = {}
    for (k, half, row), ref in zip(which, in_refs, strict=True):
        if half is None:
            blocks[k] = ref[...]
        else:
            blocks.setdefault(k, [part, part])[half] = ref[row : row + s.batch, :]
    tables, data = [], []
    for k, block in blocks.items():
        high, low = split(jnp.concatenate(block, 0) if isinstance(block, list) else block)
        table = table_ref[partner(me, k)]
        tables.append(jnp.concatenate([table, table[:, : 2 * s.batch]], 1))
        data.append(jnp.concatenate([high, high, low], 0))
    if not ended:
        out_ref[...] = sum(dot(table, block) for table, block in zip(tables[1:], data[1:])) + dot(tables[0], data[0])
        return
    staged_ref, sems = refs[-2:]
    live = live_of(s, refs[1], me)
    for depth in (0, s.span - 1):
        staged_ref[0, depth] = jnp.zeros((4, s.sticks), f32)
    middle = s.depths // 2 + 1
    copies = []
    for i, (first, end) in enumerate(((1, middle), (middle, s.span - 1))):
        rows = slice(4 * (first - 1), 4 * (end - 1))
        total = refs[0][rows, :] if started else 0.0
        for table, block in zip(tables, data, strict=True):
            total = total + dot(table[rows], block)
        staged_ref[0, first:end] = jnp.where(live[rows], total, 0.0).reshape(end - first, 4, s.sticks)
        own = slice(0, middle) if i == 0 else slice(middle, s.span)
        copies.append(pltpu.make_async_copy(staged_ref.at[0, own], out_ref.at[0, own], sems.at[i]))
        copies[-1].start()
    for copy in copies:
        copy.wait()


def fetching_kernel(body, inputs, outs, count, *refs):
    sources, targets = refs[inputs : inputs + count], refs[inputs + count + outs : inputs + 2 * count + outs]
    copies = [pltpu.make_async_copy(sources[i], targets[i], refs[-1].at[i]) for i in range(count)]
    for copy in copies:
        copy.start()
    body(*refs[:inputs], *refs[inputs + count : inputs + count + outs], *refs[inputs + 2 * count + outs : -1])
    for copy in copies:
        copy.wait()


def places(s, sticks_ref, sources, x_ref, y_ref):
    at = 0
    for source in sources:
        columns = pl.ds(pl.multiple_of(source * s.sticks, s.sticks), s.sticks)
        shape = (s.rows_y, s.sticks)
        x_ref[:, at : at + s.sticks] = jnp.broadcast_to(sticks_ref[0:1, columns].astype(f32), shape).astype(bf16)
        row = lax.broadcasted_iota(jnp.int32, shape, 0) + 1 - s.radius
        hit = sticks_ref[1:2, columns] == row
        y_ref[:, at : at + s.sticks] = jnp.where(hit, 1.0, 0.0).astype(bf16)
        at += s.sticks


def one_hot(x, x_all, y_all):
    return jnp.where(x_all == jnp.asarray(x, bf16), y_all, jnp.zeros_like(y_all))


def lay_kernel(s, which, started, ended, *refs):
    in_refs, refs = refs[: len(which)], refs[len(which) :]
    before_ref, refs = (refs[0], refs[1:]) if started else (None, refs)
    sticks_ref, refs = refs[0], refs[1:]
    table_ref, out_ref, grid_ref = refs[:3] if ended else (None, None, refs[0])
    x_ref, y_ref, both_ref = refs[-3:]
    me = lax.axis_index("plane")
    places(s, sticks_ref, [partner(me, k) for k in which], x_ref, y_ref)
    rows = 2 * s.batch
    for i in range(len(which)):
        high, low = split(in_refs[i][...])
        both_ref[:rows, i * s.sticks : (i + 1) * s.sticks] = high
        both_ref[rows:, i * s.sticks : (i + 1) * s.sticks] = low
    lanes = 2 * s.rows_y
    for first in range(0, s.tiles, 2):
        count = min(2, s.tiles - first)
        hot = jnp.concatenate([one_hot(x, x_ref[...], y_ref[...]) for x in range(2 * first, 2 * (first + count))], 0)
        laid = lax.dot_general(both_ref[...], hot, (((1,), (1,)), ((), ())), preferred_element_type=f32)
        laid = laid[:rows] + laid[rows:]
        for t in range(count):
            for component in range(2):
                own = pl.ds((first + t) * s.batch, s.batch), slice(component * lanes, (component + 1) * lanes)
                part = laid[component * s.batch : (component + 1) * s.batch, t * lanes : (t + 1) * lanes]
                grid_ref[own] = part + before_ref[own] if started else part
    if not ended:
        return
    total = s.tiles * s.batch
    table = jnp.concatenate([table_ref[0], table_ref[0], table_ref[1]], 0)
    for start in range(0, total, 4 * s.batch):
        end = min(total, start + 4 * s.batch)
        sides = braid(grid_ref[start:end, :lanes], grid_ref[start:end, lanes:])
        high, low = split(jnp.concatenate(sides, 0))
        moved = dot(jnp.concatenate([high, low, high], 1), table)
        for t in range(4):
            for row in range(0, end - start, s.batch):
                at = (start + row) // s.batch * s.step
                own = t // 2 * (end - start) + row
                part = moved[own : own + s.batch, t % 2 * s.length : (t % 2 + 1) * s.length]
                out_ref[t, at : at + s.batch, :] = part
    for t in range(4):
        out_ref[t, s.tiles * s.step :, :] = jnp.zeros(((s.even - s.tiles) * s.step, s.length), f32)


def turn_kernel(s, bands, half_ref, x_ahead_ref, real_ref):
    width = s.length // bands
    last = pl.ds(pl.multiple_of(last_owner(bands) * width, width), width)
    table = jnp.concatenate([x_ahead_ref[...], x_ahead_ref[last, :]], 0)

    def plane(z, carry):
        parts = []
        for component in range(2):
            for parity in range(2):
                count = s.odd if parity else s.even
                parts.append(
                    jnp.concatenate(
                        [
                            half_ref[2 * parity + component, pl.ds(o * s.planes + z, count, stride=s.step), :]
                            for o in range(2)
                        ],
                        1,
                    )
                )
        high, low = split(jnp.concatenate(parts, 0))
        real_ref[z] = dot(table, jnp.concatenate([high, high, low], 0))
        return carry

    lax.fori_loop(0, s.planes, plane, 0, unroll=s.planes)


def space_kernel(s, bands, real_ref, *refs):
    offsets = ring_offsets(bands)[:-2]
    slab_refs, (x_back_ref, turned_ref, field_ref) = refs[: len(offsets)], refs[len(offsets) :]
    width = s.length // bands
    band = lax.axis_index("band")
    at = place_on_ring(band, bands)
    for (offset, _, _), slab_ref in zip(offsets, slab_refs, strict=True):
        owner = band_on_ring(lax.rem(at + offset + bands, bands), bands)
        field_ref[:, pl.ds(pl.multiple_of(owner * width, width), width), :] = slab_ref[...]
    last = pl.ds(pl.multiple_of(last_owner(bands) * width, width), width)
    field_ref[:, last, :] = jnp.zeros((s.planes, width, s.length), f32)
    for t in range(2, 4):
        turned_ref[t, s.odd * s.step :, :] = jnp.zeros(((s.even - s.odd) * s.step, s.length), f32)

    def plane(z, carry):
        field = field_ref[z]
        high, low = split(real_ref[z, : s.length, :] * jnp.concatenate([field, field], 1))
        turned = dot(x_back_ref[...], jnp.concatenate([high, low], 0))
        keep_turned(s, turned_ref, z, turned[: s.kept] + turned[s.kept :])
        return carry

    lax.fori_loop(0, s.planes, plane, 0, unroll=s.planes)


def keep_turned(s, turned_ref, z, turned):
    at = 0
    for component in range(2):
        for parity in range(2):
            count = s.odd if parity else s.even
            for o in range(2):
                turned_ref[2 * parity + component, pl.ds(o * s.planes + z, count, stride=s.step), :] = turned[
                    at : at + count, o * s.length : (o + 1) * s.length
                ]
            at += count


def finish_kernel(s, bands, half, first_ref, real_ref, slab_ref, x_last_ref, y_back_ref, flat_ref, turned_ref):
    for t in range(2, 4):
        turned_ref[t, s.odd * s.step :, :] = jnp.zeros(((s.even - s.odd) * s.step, s.length), f32)
    x_last = x_last_ref[last_owner(bands)]
    part = s.planes // 2

    def plane(z, carry):
        field = slab_ref[z]
        high, low = split(real_ref[half * part + z, s.length :, :] * jnp.concatenate([field, field], 1))
        keep_turned(s, turned_ref, half * part + z, dot(x_last, jnp.concatenate([high, low, high], 0)))
        return carry

    lax.fori_loop(0, part, plane, 0, unroll=part)

    lanes = 2 * s.rows_y
    for start in range(0, s.tiles, 8):
        end = min(s.tiles, start + 8)
        parts = []
        for parity in range(2):
            for tile in range(start, end):
                for o in range(2):
                    row = tile * s.step + o * s.planes + half * part
                    own = slice(row, row + part)
                    both = [first_ref[t, own, :] + turned_ref[t, own, :] for t in (2 * parity, 2 * parity + 1)]
                    parts.append(jnp.concatenate(both, 1))
        high, low = split(jnp.concatenate(parts, 0))
        moved = dot(jnp.concatenate([high, low], 1), y_back_ref[...])
        moved = moved[:, :lanes] + moved[:, lanes:]
        count = (end - start) * s.planes
        for component, value in enumerate(braid(moved[:count], moved[count:])):
            for row, piece in zip((component, 2 + component), split(value), strict=True):
                for tile in range(start, end):
                    at = (tile - start) * s.planes
                    flat_ref[row * s.planes : (row + 1) * s.planes, tile * lanes : (tile + 1) * lanes] = piece[
                        at : at + s.planes
                    ]


def pick_kernel(s, which, count, joined, *refs):
    flat_refs, sticks_ref, refs = refs[:count], refs[count], refs[count + 1 :]
    out_refs, (x_ref, y_ref) = refs[:-2], refs[-2:]
    me = lax.axis_index("plane")
    places(s, sticks_ref, [partner(me, k) for k in which], x_ref, y_ref)
    rows = 2 * s.planes
    flat = jnp.concatenate([flat_ref[...] for flat_ref in flat_refs], 0)
    for i in range(len(which)):
        columns = slice(i * s.sticks, (i + 1) * s.sticks)
        hot = [one_hot(x, x_ref[:, columns], y_ref[:, columns]) for x in range(2 * s.tiles)]
        found = dot(flat, jnp.concatenate(hot, 0))
        for h in range(count):
            row = 2 * h * rows
            out_ref, at = (out_refs[0], (i * count + h) * rows) if joined else (out_refs[i], h * rows)
            out_ref[at : at + rows, :] = found[row : row + rows] + found[row + rows : row + 2 * rows]


def band_on_ring(place, count):
    return jnp.where(2 * place < count, 2 * place, 2 * (count - 1 - place) + 1)


def place_on_ring(band, count):
    return jnp.where(lax.rem(band, 2) == 0, band // 2, count - 1 - band // 2)


def last_owner(count):
    return band_on_ring(lax.rem(place_on_ring(lax.axis_index("band"), count) + count // 2, count), count)


def ring_offsets(count):
    offsets = [(0, 0, 2)]
    for step in range(1, count // 2 + 1):
        last = 2 * step == count
        offsets += [(-step, 0, 1 if last else 2), (step, 1 if last else 0, 2)]
    return offsets


def partners(devices):
    return sorted(range(1, devices), key=lambda k: (k == 1, k % 2, k))


def send_groups(devices):
    soon, *others, near = partners(devices)
    return [[soon, soon ^ 1], *(k for k in others if k != soon ^ 1), near]


def stages(devices):
    far = partners(devices)[:-1]
    return [("lay1", [0, 1]), ("lay2", far[:-1]), ("lay3", far[-1:])]


def per_device(bands, coeffs, potential, stick_map):
    devices = stick_map.shape[1] // coeffs.shape[3]
    s = Sizes(coeffs.shape[2], coeffs.shape[3], potential.shape[2], potential.shape[0], devices)
    tab = {name: jnp.asarray(value) for name, value in tables(s, bands).items()}
    rows = 2 * s.batch
    block = jax.ShapeDtypeStruct((rows, s.sticks), f32)

    order = list(range(0, bands, 2)) + list(range(bands - 1, 0, -2))
    along = [(order[i], order[(i + 1) % bands]) for i in range(bands)]
    against = [(b, a) for a, b in along]

    def exchange(blocks):
        out = [blocks[0]] + [None] * (devices - 1)
        for k in partners(devices):
            out[k] = lax.ppermute(blocks[k], "plane", [(i, i ^ k) for i in range(devices)])
        return out

    def ring():
        slabs = [potential]
        up = down = potential
        for step in range(1, bands // 2 + 1):
            last = 2 * step == bands
            if last:
                up, down = up[: s.planes // 2], down[s.planes // 2 :]
            up = lax.ppermute(up, "band", along)
            down = lax.ppermute(down, "band", against)
            slabs += [up, down]
        return slabs

    def kernel(body, inputs, out_shape, limit, flops, scratch_shapes=(), place=VMEM, fetched=(), into=VMEM):
        single = not isinstance(out_shape, list)
        outs = [out_shape] if single else out_shape
        extra = [jax.ShapeDtypeStruct(a.shape, a.dtype) for a in fetched]
        if fetched:
            body = functools.partial(fetching_kernel, body, len(inputs), len(outs), len(fetched))
        results = pl.pallas_call(
            body,
            in_specs=[place] * len(inputs) + [HBM] * len(fetched),
            out_specs=[into] * (len(outs) + len(fetched)),
            out_shape=outs + extra,
            scratch_shapes=[*scratch_shapes] + [pltpu.SemaphoreType.DMA((len(fetched),))] * bool(fetched),
            compiler_params=pltpu.CompilerParams(vmem_limit_bytes=limit << 10),
            cost_estimate=pl.CostEstimate(flops=flops, bytes_accessed=1 << 20, transcendentals=0),
        )(*inputs, *(pltpu.with_memory_space_constraint(a, pltpu.HBM) for a in fetched))
        if fetched:
            return results[: len(outs)], results[len(outs) :]
        return results[0] if single else results

    slabs = ring()
    positions = 2 * s.tiles * s.rows_y
    results = []
    for pair in range(coeffs.shape[0]):
        given = jnp.transpose(coeffs[pair : pair + 1], (0, 2, 1, 3))
        sent = kernel(
            functools.partial(ahead_kernel, s),
            [pltpu.with_memory_space_constraint(a, pltpu.HBM) for a in (given, stick_map, tab["z_ahead"])],
            [block] * devices,
            16 << 10,
            1 << 31,
            [
                pltpu.VMEM(given.shape, f32),
                pltpu.VMEM(stick_map.shape, jnp.int32),
                pltpu.VMEM(tab["z_ahead"].shape, bf16),
                pltpu.SemaphoreType.DMA((3,)),
            ],
            HBM,
        )
        held = exchange(sent)
        half = None
        ready = results
        later = ["y_ahead", "x_ahead", "x_back", "x_last", "y_back", "z_back"]
        grid_shape = (s.tiles * s.batch, 4 * s.rows_y)
        for name, which in stages(devices):
            started, ended = half is not None, name == "lay3"
            shape = (4, s.even * s.step, s.length) if ended else grid_shape
            own = [pltpu.VMEM((s.rows_y, len(which) * s.sticks), bf16)] * 2
            own.append(pltpu.VMEM((2 * rows, len(which) * s.sticks), bf16))
            fetch = [] if started or ready else [tab[key] for key in later] + [potential]
            half = kernel(
                functools.partial(lay_kernel, s, which, started, ended),
                [held[k] for k in which] + [half] * started + [stick_map] + [tab["y_ahead"]] * ended,
                jax.ShapeDtypeStruct(shape, f32),
                24 << 10,
                1 << 31,
                [pltpu.VMEM(grid_shape, f32)] * ended + own,
                fetched=fetch,
            )
            if fetch:
                (half,), (*ready, slabs[0]) = half
                tab.update(zip(later, ready, strict=True))
        turned_shape = (4, s.even * s.step, s.length)
        real = kernel(
            functools.partial(turn_kernel, s, bands),
            [half, tab["x_ahead"]],
            jax.ShapeDtypeStruct((s.planes, s.length + s.length // bands, 2 * s.length), f32),
            16 << 10,
            1 << 31,
        )
        turned = kernel(
            functools.partial(space_kernel, s, bands),
            [real, *slabs[:-2], tab["x_back"]],
            jax.ShapeDtypeStruct(turned_shape, f32),
            16 << 10,
            1 << 31,
            [pltpu.VMEM((s.planes, s.length, s.length), f32)],
        )
        flats = [
            kernel(
                functools.partial(finish_kernel, s, bands, half),
                [turned, real, slabs[half - 2], tab["x_last"], tab["y_back"]],
                jax.ShapeDtypeStruct((4 * s.planes, positions), bf16),
                20 << 10,
                1 << 31,
                [pltpu.VMEM(turned_shape, f32)],
            )
            for half in range(2)
        ]

        def pick(which, flats, joined=False):
            size = len(flats) * 2 * s.planes
            shape = jax.ShapeDtypeStruct((size * len(which) if joined else size, s.sticks), f32)
            return kernel(
                functools.partial(pick_kernel, s, which, len(flats), joined),
                [*flats, stick_map],
                [shape] if joined else [shape] * len(which),
                16 << 10,
                1 << 31,
                [
                    pltpu.VMEM((s.rows_y, len(which) * s.sticks), bf16),
                    pltpu.VMEM((s.rows_y, len(which) * s.sticks), bf16),
                ],
            )

        def send(k, block):
            return lax.ppermute(block, "plane", [(i, i ^ k) for i in range(devices)])

        (soon, across), *others, near = send_groups(devices)
        both = send(soon, *pick([across, soon], [flats[0]], True))
        hop, last = pick([across, soon], [flats[1]])
        hop = send(across, hop)
        last = send(soon, last)
        returned = [(k, None, 0, send(k, *pick([k], flats))) for k in others]
        beside, own = pick([near, 0], flats)
        returned += [(near, None, 0, send(near, beside)), (0, None, 0, own), (soon, 0, s.batch, both)]
        late = [(across, 0, 0, send(near, both[: s.batch]))]
        late += [(across, 1, 0, hop), (soon, 1, 0, last)]
        begun = kernel(
            functools.partial(back_kernel, s, [block[:3] for block in returned], False, False),
            [*(block[3] for block in returned), tab["z_back"]],
            jax.ShapeDtypeStruct((s.depth_rows, s.sticks), f32),
            16 << 10,
            1 << 31,
        )
        result = kernel(
            functools.partial(back_kernel, s, [block[:3] for block in late], True, True),
            [*(block[3] for block in late), begun, stick_map, tab["z_back"]],
            jax.ShapeDtypeStruct((1,) + given.shape[1:], f32),
            16 << 10,
            1 << 31,
            [pltpu.VMEM((1,) + given.shape[1:], f32), pltpu.SemaphoreType.DMA((2,))],
            into=HBM,
        )
        results.append(jnp.transpose(result, (0, 2, 1, 3)))
    return results[0] if len(results) == 1 else jnp.concatenate(results, 0)


def solution(mesh):
    placed = (P("band", None, None, "plane"), P("plane", "band", None), P())
    return jax.shard_map(
        functools.partial(per_device, mesh.shape["band"]),
        mesh=mesh,
        in_specs=placed,
        out_specs=P("band", None, None, "plane"),
        check_vma=False,
    )
```
